256 devices in a mesh: slab: 64 (over z_hi, x, y, core), rep: 4 (over z_lo).
Axes of the slice: x: 4, y: 4, z: 8 (z_hi: 2, z_lo: 4; z = z_hi * 4 + z_lo), core: 2. Of those that a mesh axis runs over, the one named last changes fastest.
Arguments:
- embeddings: bfloat16 [262144, 512], P(('slab', 'rep')), may hold values from -6 to 6
- indicators: bfloat16 [262144, 256], P(('slab', 'rep')), may hold values from -6 to 6
- neighbours: int32 [256, 4], P(('slab', 'rep')), may hold values from 0 to 257, as said below
- hub_ids: int32 [2], replicated, may hold values from 0 to 255, as said below
- columns: int32 [262144, 4, 16], P(('slab', 'rep')), may hold values from 0 to 1023
Outputs:
- propagated: bfloat16 [262144, 256], P(('slab', 'rep'))
The draws below stay inside these ranges and needn't reach their ends.
Inputs may be any that keep to these rules, and one draw needn't show every extreme that they name: `neighbours`: slot 0 of block b is b; slot 1 names a block c with c // 4 == b // 4; slots 2 to 3 hold 256 + h for each hub number h once, in some order. `hub_ids`: distinct block ids; the last block, 255, is always one of the hubs.
All inputs are finite; a program needn't handle non-finite values.
Results may differ from the reference program's by a relative error of at most 0.0048.
Values may be sent and summed in bfloat16 or wider, within the bound.
No kernel may reach another device: no remote copies, remote signals or barrier semaphores. Data moves between devices by JAX's collectives and lax.ppermute only.
A program may use at most 64 MiB of HBM per device.

```python
import jax
import jax.numpy as jnp
from jax import lax

R = 1024
D_EMB = 512
CLUST = 256
K = 4
TOPK = 16
HUBS = 2
ITERS = 2
GROUP = 4
BLOCKS = 256
ROWS = 262144


def draw_neighbours(key, part):
    block_ids = jnp.arange(BLOCKS, dtype=jnp.int32)[:, None]
    member = block_ids // GROUP * GROUP + jax.random.randint(jax.random.fold_in(key, 12), (BLOCKS, 1), 0, GROUP)
    row_keys = jax.random.split(jax.random.fold_in(key, 13), BLOCKS)
    orders = jax.vmap(lambda k: jax.random.permutation(k, HUBS))(row_keys).astype(jnp.int32)
    return jnp.concatenate([block_ids, member.astype(jnp.int32), BLOCKS + orders], axis=1).astype(jnp.int32)


def draw_hub_ids(key, part):
    others = jax.random.permutation(jax.random.fold_in(key, 11), BLOCKS - 1)[:HUBS - 1].astype(jnp.int32)
    chosen = jnp.concatenate([jnp.full((1,), BLOCKS - 1, jnp.int32), others], axis=0)
    order = jax.random.permutation(jax.random.fold_in(key, 14), HUBS)
    return chosen[order].astype(jnp.int32)


def plant(result, stream_key, low, largest):
    place = [jax.random.randint(jax.random.fold_in(stream_key, axis), (), 0, length) for axis, length in enumerate(result.shape)]
    widest = result.shape.index(max(result.shape))
    neighbour = place[:widest] + [(place[widest] + 1) % result.shape[widest]] + place[widest + 1:]
    return result.at[tuple(place)].set(low).at[tuple(neighbour)].set(largest)


def shard_levels(stream_key, dims, pieces, smallest, top_value):
    level, own = 1.0, jax.random.fold_in(stream_key, 6)
    for axis_at, parts in pieces:
        draws = jnp.exp(jax.random.uniform(jax.random.fold_in(own, axis_at), (parts,), jnp.float32, smallest / len(pieces), top_value / len(pieces)))
        level = level * jnp.repeat(draws, dims[axis_at] // parts).reshape([-1 if axis == axis_at else 1 for axis in range(len(dims))])
    return level


def scatter_about(own_key, extent, scale, most, shards=(), held_as=jnp.bfloat16):
    result = scale * jax.random.normal(own_key, extent, jnp.float32)
    if shards:
        result = result * shard_levels(own_key, extent, shards, -0.22, 0.18)
    return jnp.clip(result, -most, most).astype(held_as)


def setup_inputs(seed: int = 0) -> dict:
    keys = jax.random.split(jax.random.key(seed), 6)
    embeddings = scatter_about(keys[0], (ROWS, D_EMB), 1.0, 6.0, ((0, 256),))
    indicators = scatter_about(keys[1], (ROWS, CLUST), 1.0, 6.0, ((0, 256),))
    neighbours = draw_neighbours(jax.random.fold_in(keys[5], 71), 0)
    hub_ids = draw_hub_ids(jax.random.fold_in(keys[5], 71), 0)
    columns = plant(jax.random.randint(keys[4], (ROWS, K, TOPK), 0, R), jax.random.fold_in(keys[4], 1), 0, R - 1).astype(jnp.int32)
    return dict(embeddings=embeddings, indicators=indicators, neighbours=neighbours, hub_ids=hub_ids, columns=columns)


EPS = 1e-06
TAU = 0.04
ALPHA = 0.8

def normalize(rows):
    values = rows.astype(jnp.float32)
    return (values * lax.rsqrt(lax.optimization_barrier(jnp.sum(values * values, axis=1, keepdims=True)) + EPS)).astype(jnp.bfloat16)

def edge_weight(cosine, kept):
    row_ids = jnp.arange(cosine.shape[0], dtype=jnp.int32)[:, None]
    mask = jnp.zeros(cosine.shape, jnp.float32).at[row_ids, kept].set(1.0)
    return mask * jnp.exp((cosine - 1.0) / TAU)

def reference(embeddings, indicators, neighbours, hub_ids, columns):
    normed = normalize(embeddings).reshape(BLOCKS, R, D_EMB)
    kept_cols = columns.reshape(BLOCKS, R, K, TOPK)
    anchor = indicators.reshape(BLOCKS, R, CLUST)
    hub_index = jnp.clip(neighbours - BLOCKS, 0, HUBS - 1).astype(jnp.int32)
    resolved = jnp.where(neighbours >= BLOCKS, hub_ids.astype(jnp.int32)[hub_index], neighbours).astype(jnp.int32)

    def propagate(current):
        blocks_y = current.reshape(BLOCKS, R, CLUST)

        def one_block(block):
            own = normed[block]
            degree = jnp.zeros((R,), jnp.float32)
            gathered = jnp.zeros((R, CLUST), jnp.float32)
            tiles = []
            for slot in range(K):
                other = normed[resolved[block, slot]]
                cosine = jnp.dot(own, other.T, preferred_element_type=jnp.float32)
                raw = edge_weight(cosine, kept_cols[block, :, slot, :])
                degree = degree + lax.optimization_barrier(jnp.sum(raw, axis=1))
                tiles.append(raw.astype(jnp.bfloat16))
            for slot in range(K):
                gathered = gathered + jnp.dot(tiles[slot], blocks_y[resolved[block, slot]], preferred_element_type=jnp.float32)
            mixed = ALPHA * gathered / degree[:, None] + (1.0 - ALPHA) * anchor[block].astype(jnp.float32)
            return mixed.astype(jnp.bfloat16)
        return lax.map(one_block, jnp.arange(BLOCKS, dtype=jnp.int32)).reshape(ROWS, CLUST)
    current = indicators
    for step in range(ITERS):
        current = propagate(current)
    return current
```

```python
import functools

import jax
import jax.numpy as jnp
from jax import lax
from jax.experimental import pallas as pl
from jax.experimental.pallas import tpu as pltpu
from jax.sharding import PartitionSpec as P

K = 4
HUBS = 2
TOPK = 16
LANES = 128
EPS = 1e-06
TAU = 0.04
ALPHA = 0.8
AXES = ("slab", "rep")
ROW_TILE = 256


def normalize(rows):
    values = rows.astype(jnp.float32)
    return (values * lax.rsqrt(jnp.sum(values * values, axis=1, keepdims=True) + EPS)).astype(
        jnp.bfloat16
    )


def words_kernel(cols_ref, out_ref):
    cols = cols_ref[...]
    low = cols & (LANES - 1)
    bit = jnp.left_shift(jnp.ones_like(cols), cols >> 7)
    lane = lax.broadcasted_iota(jnp.int32, (cols.shape[0], LANES), 1)
    for slot in range(K):
        word = jnp.zeros(lane.shape, jnp.int32)
        for t in range(slot * TOPK, (slot + 1) * TOPK):
            word = word | jnp.where(lane == low[:, t : t + 1], bit[:, t : t + 1], 0)
        out_ref[slot] = word


def keep_words(columns):
    rows = columns.shape[0]
    flat = columns.reshape(rows, K * TOPK)
    tile = 128
    return pl.pallas_call(
        words_kernel,
        out_shape=jax.ShapeDtypeStruct((K, rows, LANES), jnp.int32),
        grid=(rows // tile,),
        in_specs=[pl.BlockSpec((tile, K * TOPK), lambda r: (r, 0))],
        out_specs=pl.BlockSpec((K, tile, LANES), lambda r: (0, r, 0)),
        cost_estimate=pl.CostEstimate(
            flops=rows * LANES * K * TOPK * 3, bytes_accessed=rows * K * (TOPK + LANES) * 4, transcendentals=0
        ),
        name="keep_words",
    )(flat)


def mix(acc, degree, anchor):
    return (ALPHA * acc / degree + (1.0 - ALPHA) * anchor.astype(jnp.float32)).astype(jnp.bfloat16)


def tile_kernel(width, has_in, sel_ref, x_ref, pool_ref, w_ref, *refs):
    if has_in:
        acc_in, deg_in, tile_ref, acc_ref, deg_ref = refs
    else:
        tile_ref, acc_ref, deg_ref = refs
    slot, row = pl.program_id(0), pl.program_id(1)
    here = pl.ds(pl.multiple_of(row * ROW_TILE, ROW_TILE), ROW_TILE)
    rows = pool_ref.shape[0] * pool_ref.shape[2]
    other = pool_ref[:, 0].reshape(rows, pool_ref.shape[3])
    cosine = lax.dot_general(
        x_ref[...], other[:, :width], (((1,), (1,)), ((), ())), preferred_element_type=jnp.float32
    )
    word = w_ref[0]
    total = jnp.zeros(word.shape, jnp.float32)
    for j in range(rows // LANES):
        part = cosine[:, j * LANES : (j + 1) * LANES]
        raw = jnp.where((word & (1 << j)) != 0, jnp.exp((part - 1.0) * (1.0 / TAU)), 0.0)
        total = total + raw
        tile_ref[0, :, j * LANES : (j + 1) * LANES] = raw.astype(jnp.bfloat16)
    gathered = jnp.dot(tile_ref[0], other[:, width:], preferred_element_type=jnp.float32)

    @pl.when(slot == 0)
    def _():
        acc_ref[here, :] = acc_in[here, :] + gathered if has_in else gathered
        deg_ref[here, :] = deg_in[here, :] + total if has_in else total

    @pl.when(slot > 0)
    def _():
        acc_ref[here, :] += gathered
        deg_ref[here, :] += total


def tiles_of(slots, pick, joined, pool, words, carry, width):
    rows, full = joined.shape
    clust = full - width
    first = slots[0]
    n = len(slots)
    whole = lambda shape: pl.BlockSpec(shape, lambda s, r, pick_ref: (0,) * len(shape))
    has_in = carry is not None
    outs = [
        jax.ShapeDtypeStruct((n, rows, rows), jnp.bfloat16),
        jax.ShapeDtypeStruct((rows, clust), jnp.float32),
        jax.ShapeDtypeStruct((rows, LANES), jnp.float32),
    ]
    return pl.pallas_call(
        functools.partial(tile_kernel, width, has_in),
        out_shape=outs,
        grid_spec=pltpu.PrefetchScalarGridSpec(
            num_scalar_prefetch=1,
            grid=(n, rows // ROW_TILE),
            in_specs=[
                pl.BlockSpec((ROW_TILE, width), lambda s, r, pick_ref: (r, 0)),
                pl.BlockSpec(
                    (pool.shape[0], 1, pool.shape[2], full), lambda s, r, pick_ref: (0, pick_ref[s], 0, 0)
                ),
                pl.BlockSpec((1, ROW_TILE, LANES), lambda s, r, pick_ref: (first + s, r, 0)),
            ]
            + ([whole((rows, clust)), whole((rows, LANES))] if has_in else []),
            out_specs=[
                pl.BlockSpec((1, ROW_TILE, rows), lambda s, r, pick_ref: (s, r, 0)),
                whole((rows, clust)),
                whole((rows, LANES)),
            ],
        ),
        compiler_params=pltpu.CompilerParams(vmem_limit_bytes=40 << 20),
        cost_estimate=pl.CostEstimate(
            flops=2 * n * rows * rows * full,
            bytes_accessed=n * rows * (2 * rows + 2 * full + 4 * LANES),
            transcendentals=n * rows * rows,
        ),
        name="tiles",
    )(pick, joined, pool, words, *(carry or ()))


def gather_kernel(last, has_in, sel_ref, tile_ref, pool_ref, *refs):
    refs = list(refs)
    acc_in = refs.pop(0) if has_in else None
    deg_ref, anchor_ref = (refs.pop(0), refs.pop(0)) if last else (None, None)
    out_ref, acc_ref = refs if last else (None, refs[0])
    slot = pl.program_id(0)
    row = pl.program_id(1)
    here = pl.ds(pl.multiple_of(row * ROW_TILE, ROW_TILE), ROW_TILE)
    rows = pool_ref.shape[0] * pool_ref.shape[2]
    other = pool_ref[:, 0].reshape(rows, pool_ref.shape[3])
    gathered = jnp.dot(tile_ref[0], other, preferred_element_type=jnp.float32)

    @pl.when(slot == 0)
    def _():
        acc_ref[here, :] = acc_in[here, :] + gathered if has_in else gathered

    @pl.when(slot > 0)
    def _():
        acc_ref[here, :] += gathered

    if last:

        @pl.when(slot == pl.num_programs(0) - 1)
        def _():
            degree = jnp.sum(deg_ref[here, :], axis=1, keepdims=True)
            out_ref[here, :] = mix(acc_ref[here, :], degree, anchor_ref[here, :])


def gather_of(pick, tiles, pool, acc, finish=None):
    n, rows, _ = tiles.shape
    clust = pool.shape[3]
    whole = lambda shape: pl.BlockSpec(shape, lambda s, r, pick_ref: (0,) * len(shape))
    has_in, last = acc is not None, finish is not None
    args = ([acc] if has_in else []) + (list(finish) if last else [])
    specs = ([whole((rows, clust))] if has_in else []) + (
        [whole((rows, LANES)), whole((rows, clust))] if last else []
    )
    return pl.pallas_call(
        functools.partial(gather_kernel, last, has_in),
        out_shape=jax.ShapeDtypeStruct((rows, clust), jnp.bfloat16 if last else jnp.float32),
        grid_spec=pltpu.PrefetchScalarGridSpec(
            num_scalar_prefetch=1,
            grid=(n, rows // ROW_TILE),
            in_specs=[
                pl.BlockSpec((1, ROW_TILE, rows), lambda s, r, pick_ref: (s, r, 0)),
                pl.BlockSpec(
                    (pool.shape[0], 1, pool.shape[2], clust), lambda s, r, pick_ref: (0, pick_ref[s], 0, 0)
                ),
            ]
            + specs,
            out_specs=whole((rows, clust)),
            scratch_shapes=[pltpu.VMEM((rows, clust), jnp.float32)] if last else [],
        ),
        compiler_params=pltpu.CompilerParams(vmem_limit_bytes=40 << 20),
        cost_estimate=pl.CostEstimate(
            flops=2 * n * rows * rows * clust,
            bytes_accessed=n * rows * (2 * rows + 2 * clust) + 8 * rows * clust,
            transcendentals=0,
        ),
        name="gather",
    )(pick, tiles, pool, *args)


def spread_hubs(block, hub_ids):
    slabs, reps = lax.axis_size("slab"), lax.axis_size("rep")
    halves = 2
    members = slabs // halves
    planes = [[h * members + m for m in range(members)] for h in range(halves)]
    rows, width = block.shape
    piece = rows // members
    mine = lax.all_to_all(
        block.reshape(members, piece, width), "slab", 0, 0, axis_index_groups=planes, tiled=True
    )
    own_z = lax.axis_index("slab") // members * reps + lax.axis_index("rep")
    hub_slab, hub_rep = hub_ids // reps, hub_ids % reps
    hub_z = hub_slab // members * reps + hub_rep
    member = hub_slab % members
    held = jnp.stack(
        [lax.dynamic_index_in_dim(mine, member[h], 0, keepdims=False) for h in range(HUBS)], axis=0
    )
    away = own_z ^ hub_z
    total = slabs * reps
    for bit in range((halves * reps - 1).bit_length()):
        pairs = []
        for device in range(total):
            slab, rep = divmod(device, reps)
            z = (slab // members * reps + rep) ^ (1 << bit)
            pairs.append((device, (z // reps * members + slab % members) * reps + z % reps))
        received = lax.ppermute(held, AXES, pairs)
        held = jnp.where(((away >> bit) & 1 == 1)[:, None, None], received, held)
    repeated = jnp.broadcast_to(held[None], (members,) + held.shape)
    return lax.all_to_all(repeated, "slab", 0, 0, axis_index_groups=planes, tiled=True)


def body(embeddings, indicators, neighbours, hub_ids, columns):
    rows, width = embeddings.shape
    clust = indicators.shape[1]
    reps = lax.axis_size("rep")
    total = lax.axis_size("slab") * reps
    slots = neighbours[0].astype(jnp.int32)
    zero = jnp.zeros((1,), jnp.int32)
    group_pick = (slots[1] % reps)[None]
    hub_pick = slots[2:] - total
    joined = jnp.concatenate([normalize(embeddings), indicators], axis=1)
    group = lax.all_gather(joined[None], "rep", axis=0, tiled=True)
    hubs = spread_hubs(joined, hub_ids)
    words = keep_words(columns)
    own_tiles, *carry = tiles_of((0,), zero, joined, joined[None, None], words, None, width)
    hub_tiles, *carry = tiles_of((2, 3), hub_pick, joined, hubs, words, carry, width)
    group_tiles, acc, degree = tiles_of((1,), group_pick, joined, group[None], words, carry, width)
    current = mix(acc, jnp.sum(degree, axis=1, keepdims=True), indicators)
    group = lax.all_gather(current[None], "rep", axis=0, tiled=True)
    hubs = spread_hubs(current, hub_ids)
    acc = gather_of(zero, own_tiles, current[None, None], None)
    acc = gather_of(group_pick, group_tiles, group[None], acc)
    return gather_of(hub_pick, hub_tiles, hubs, acc, (degree, indicators))


def solution(mesh):
    return jax.shard_map(
        body,
        mesh=mesh,
        in_specs=(
            P(("slab", "rep"), None),
            P(("slab", "rep"), None),
            P(("slab", "rep"), None),
            P(),
            P(("slab", "rep"), None, None),
        ),
        out_specs=P(("slab", "rep"), None),
        check_vma=False,
    )
```

```python
import functools

import jax
import jax.numpy as jnp
from jax import lax
from jax.experimental import pallas as pl
from jax.experimental.pallas import tpu as pltpu
from jax.sharding import PartitionSpec as P

K = 4
HUBS = 2
TOPK = 16
LANES = 128
EPS = 1e-06
TAU = 0.04
ALPHA = 0.8
AXES = ("slab", "rep")
ROW_TILE = 256
VMEM_LIMIT = 16 << 20
HALF = 32


def join_kernel(flag_ref, x_ref, y_ref, cols_ref, all_ref, rows_ref):
    width, clust = x_ref.shape[1], y_ref.shape[1]
    values = x_ref[...].astype(jnp.float32)
    scale = lax.rsqrt(jnp.sum(values * values, axis=1, keepdims=True) + EPS)
    normed = (values * scale).astype(jnp.bfloat16)
    cols = cols_ref[...].reshape(K * TOPK, cols_ref.shape[2])
    coded = jnp.concatenate([cols // HALF + HALF * flag_ref[0], cols % HALF], axis=0)
    coded = coded.astype(jnp.float32).T.astype(jnp.bfloat16)
    all_ref[:, :width] = normed
    all_ref[:, width : width + clust] = y_ref[...]
    all_ref[:, width + clust :] = coded
    rows_ref[:, :width] = normed
    rows_ref[:, width:] = coded


def join(flag, embeddings, indicators, columns):
    rows, width = embeddings.shape
    clust = indicators.shape[1]
    by_row = lambda cols: pl.BlockSpec((ROW_TILE, cols), lambda r, flag: (r, 0))
    wide = (width + clust + 2 * K * TOPK, width + 2 * K * TOPK)
    return pl.pallas_call(
        join_kernel,
        out_shape=[jax.ShapeDtypeStruct((rows, w), jnp.bfloat16) for w in wide],
        grid_spec=pltpu.PrefetchScalarGridSpec(
            num_scalar_prefetch=1,
            grid=(rows // ROW_TILE,),
            in_specs=[
                by_row(width),
                by_row(clust),
                pl.BlockSpec((K, TOPK, ROW_TILE), lambda r, flag: (0, 0, r)),
            ],
            out_specs=[by_row(w) for w in wide],
        ),
        compiler_params=pltpu.CompilerParams(vmem_limit_bytes=VMEM_LIMIT),
        name="join",
    )(flag, embeddings, indicators, jnp.transpose(columns, (1, 2, 0)))


def words_kernel(pick_ref, coded_ref, out_ref):
    half = K * TOPK
    lane = lax.broadcasted_iota(jnp.int32, (LANES, LANES), 0)

    @pl.loop(0, coded_ref.shape[0] // LANES)
    def _(block):
        here = pl.ds(pl.multiple_of(block * LANES, LANES), LANES)
        coded = coded_ref[here, :].astype(jnp.float32).T.astype(jnp.int32)
        high = coded[:half] & (HALF - 1)
        low = (high & 3) * HALF + coded[half:]
        bit = jnp.left_shift(jnp.ones_like(high), high >> 2)
        for slot in range(K):
            word = jnp.zeros((LANES, LANES), jnp.int32)
            for t in range(slot * TOPK, (slot + 1) * TOPK):
                word = word | jnp.where(lane == low[t : t + 1], bit[t : t + 1], 0)
            out_ref[slot, here, :] = word.T


def keep_words(pick, coded, place, rows):
    return pl.pallas_call(
        words_kernel,
        out_shape=jax.ShapeDtypeStruct((K, rows, LANES), jnp.int32),
        grid_spec=pltpu.PrefetchScalarGridSpec(
            num_scalar_prefetch=1,
            grid=(1,),
            in_specs=[pl.BlockSpec((rows, LANES), lambda i, pick: place(pick))],
            out_specs=pl.BlockSpec((K, rows, LANES), lambda i, pick: (0, 0, 0)),
        ),
        compiler_params=pltpu.CompilerParams(vmem_limit_bytes=VMEM_LIMIT),
        cost_estimate=pl.CostEstimate(flops=rows * LANES * K * TOPK, bytes_accessed=rows * 512, transcendentals=0),
        name="keep_words",
    )(pick, coded)


def mix(acc, degree, anchor):
    return (ALPHA * acc / degree + (1.0 - ALPHA) * anchor.astype(jnp.float32)).astype(jnp.bfloat16)


def weights(cosine, word, total, put):
    for j in range(cosine.shape[1] // LANES):
        part = cosine[:, j * LANES : (j + 1) * LANES]
        raw = jnp.where((word & (1 << j)) != 0, jnp.exp((part - 1.0) * (1.0 / TAU)), 0.0)
        total = total + raw
        put(slice(j * LANES, (j + 1) * LANES), raw.astype(jnp.bfloat16))
    return total


def cosines(rows, others):
    return lax.dot_general(rows, others, (((1,), (1,)), ((), ())), preferred_element_type=jnp.float32)


def flat(ref):
    value = ref[...]
    return value.reshape(-1, value.shape[-1])


def tile_kernel(has_deg, has_y, has_acc, keep, pick_ref, x_ref, other_ref, w_ref, *refs):
    refs = list(refs)
    y_ref = refs.pop(0) if has_y else None
    deg_in = refs.pop(0) if has_deg else None
    acc_in = refs.pop(0) if has_acc else None
    deg_ref = refs.pop(0)
    acc_ref = refs.pop(0) if has_y else None
    tile_ref = refs.pop(0)
    word = w_ref[0]
    total = deg_in[...] if has_deg else jnp.zeros(word.shape, jnp.float32)

    def put(lanes, value):
        tile_ref[:, lanes] = value

    deg_ref[...] = weights(cosines(x_ref[...], flat(other_ref)), word, total, put)
    if has_y:
        gathered = jnp.dot(tile_ref[...], flat(y_ref), preferred_element_type=jnp.float32)
        acc_ref[...] = acc_in[...] + gathered if has_acc else gathered


def tile_of(pick, x, other, words, slot, degree, y=None, acc=None, keep=True):
    rows = words.shape[1]
    by_row = lambda cols: pl.BlockSpec((ROW_TILE, cols), lambda r, pick: (r, 0))
    spec = lambda operand: pl.BlockSpec(operand[1], operand[2])
    clust = y[1][-1] if y else 0
    args = [x[0], other[0], words] + ([y[0]] if y else [])
    specs = [spec(x), spec(other), pl.BlockSpec((1, ROW_TILE, LANES), lambda r, pick: (slot(pick), r, 0))]
    specs += [spec(y)] if y else []
    for extra, cols in ((degree, LANES), (acc, clust)):
        if extra is not None:
            args.append(extra)
            specs.append(by_row(cols))
    outs = [(LANES, jnp.float32)] + ([(clust, jnp.float32)] if y else []) + ([(rows, jnp.bfloat16)] if keep else [])
    return pl.pallas_call(
        functools.partial(tile_kernel, degree is not None, y is not None, acc is not None, keep),
        out_shape=[jax.ShapeDtypeStruct((rows, cols), kind) for cols, kind in outs],
        grid_spec=pltpu.PrefetchScalarGridSpec(
            num_scalar_prefetch=1,
            grid=(rows // ROW_TILE,),
            in_specs=specs,
            out_specs=[by_row(cols) for cols, _ in outs],
            scratch_shapes=[] if keep else [pltpu.VMEM((ROW_TILE, rows), jnp.bfloat16)],
        ),
        compiler_params=pltpu.CompilerParams(vmem_limit_bytes=VMEM_LIMIT),
        cost_estimate=pl.CostEstimate(flops=2 * rows * rows * 768, bytes_accessed=4 * rows * rows, transcendentals=rows * rows),
        name="tile",
    )(pick, *args)


def gather_kernel(has_acc, last, pick_ref, tile_ref, y_ref, *refs):
    refs = list(refs)
    acc_in = refs.pop(0) if has_acc else None
    deg_ref, anchor_ref = (refs.pop(0), refs.pop(0)) if last else (None, None)
    gathered = jnp.dot(tile_ref[...], flat(y_ref), preferred_element_type=jnp.float32)
    if has_acc:
        gathered = acc_in[...] + gathered
    if last:
        gathered = mix(gathered, jnp.sum(deg_ref[...], axis=1, keepdims=True), anchor_ref[...])
    refs[0][...] = gathered


def gather_of(pick, tile, y, acc, degree=None, anchor=None):
    rows, clust = tile.shape[0], y[1][-1]
    by_row = lambda cols: pl.BlockSpec((ROW_TILE, cols), lambda r, pick: (r, 0))
    spec = lambda operand: pl.BlockSpec(operand[1], operand[2])
    last = degree is not None
    args = [tile, y[0]] + ([acc] if acc is not None else []) + ([degree, anchor[0]] if last else [])
    specs = [by_row(rows), spec(y)] + ([by_row(clust)] if acc is not None else [])
    specs += [by_row(LANES), spec(anchor)] if last else []
    return pl.pallas_call(
        functools.partial(gather_kernel, acc is not None, last),
        out_shape=jax.ShapeDtypeStruct((rows, clust), jnp.bfloat16 if last else jnp.float32),
        grid_spec=pltpu.PrefetchScalarGridSpec(
            num_scalar_prefetch=1, grid=(rows // ROW_TILE,), in_specs=specs, out_specs=by_row(clust)
        ),
        compiler_params=pltpu.CompilerParams(vmem_limit_bytes=VMEM_LIMIT),
        cost_estimate=pl.CostEstimate(flops=2 * rows * rows * clust, bytes_accessed=3 * rows * rows, transcendentals=0),
        name="gather",
    )(pick, *args)


def hub_rows_kernel(width, pick_ref, rows_ref, near_ref, far_ref, out_ref, word_ref, tile_ref):
    clust = out_ref.shape[1]
    half = K * TOPK
    coded = rows_ref[:, width + clust :].astype(jnp.float32).astype(jnp.int32)
    high = coded[:, :half] & (HALF - 1)
    low = (high & 3) * HALF + coded[:, half:]
    bit = jnp.left_shift(jnp.ones_like(high), high >> 2)
    lane = lax.broadcasted_iota(jnp.int32, (rows_ref.shape[0], LANES), 1)
    for slot in range(K):
        word = jnp.zeros(lane.shape, jnp.int32)
        for t in range(slot * TOPK, (slot + 1) * TOPK):
            word = word | jnp.where(lane == low[:, t : t + 1], bit[:, t : t + 1], 0)
        word_ref[slot] = word
    total = jnp.zeros(lane.shape, jnp.float32)
    acc = jnp.zeros(out_ref.shape, jnp.float32)

    def put(lanes, value):
        tile_ref[:, lanes] = value

    self_block = near_ref[:, 0].reshape(-1, width + clust)
    member_block = near_ref[:, 1].reshape(-1, width + clust)
    far_block = flat(far_ref)
    slots = (0, 1, pick_ref[0], 5 - pick_ref[0])
    for slot, block in zip(slots, (self_block, member_block, self_block, far_block)):
        total = weights(cosines(rows_ref[:, :width], block[:, :width]), word_ref[slot], total, put)
        acc = acc + jnp.dot(tile_ref[...], block[:, width:], preferred_element_type=jnp.float32)
    out_ref[...] = mix(acc, jnp.sum(total, axis=1, keepdims=True), rows_ref[:, width : width + clust])


def hub_rows(self_slot, mine, near, far, width):
    share = mine.shape[0]
    clust = near.shape[3] - width
    rows = near.shape[0] * near.shape[2]
    return pl.pallas_call(
        functools.partial(hub_rows_kernel, width),
        out_shape=jax.ShapeDtypeStruct((share, clust), jnp.bfloat16),
        grid_spec=pltpu.PrefetchScalarGridSpec(
            num_scalar_prefetch=1,
            grid=(1,),
            in_specs=[
                pl.BlockSpec(mine.shape, lambda i, pick: (0, 0)),
                pl.BlockSpec(near.shape, lambda i, pick: (0, 0, 0, 0)),
                pl.BlockSpec(far.shape, lambda i, pick: (0, 0, 0)),
            ],
            out_specs=pl.BlockSpec((share, clust), lambda i, pick: (0, 0)),
            scratch_shapes=[pltpu.VMEM((K, share, LANES), jnp.int32), pltpu.VMEM((share, rows), jnp.bfloat16)],
        ),
        compiler_params=pltpu.CompilerParams(vmem_limit_bytes=20 << 20),
        cost_estimate=pl.CostEstimate(flops=share * rows * 6144, bytes_accessed=6 << 20, transcendentals=share * rows * K),
        name="hub_rows",
    )(self_slot, mine, near, far)


def send(block, target):
    slabs, reps = lax.axis_size("slab"), lax.axis_size("rep")
    chips = slabs // 4
    pairs = []
    for device in range(slabs * reps):
        slab, rep = divmod(device, reps)
        to = target(slab // (2 * chips), slab // 2 % chips, slab % 2, rep)
        pairs.append((device, ((to[0] * chips + to[1]) * 2 + to[2]) * reps + to[3]))
    return lax.ppermute(block, AXES, pairs)


def swap_cores(block):
    return send(block, lambda half, chip, core, rep: (half, chip, 1 - core, rep))


def flags_of(code):
    flag = code.astype(jnp.float32).astype(jnp.int32) // HALF
    return flag & 3, (flag >> 2) & 1


def join_pieces(piece):
    slabs = lax.axis_size("slab")
    members, chips = slabs // 2, slabs // 4
    layers = [[h * members + c * 2 + core for c in range(chips)] for h in range(2) for core in range(2)]
    repeated = jnp.broadcast_to(piece[None], (chips,) + piece.shape)
    return lax.all_to_all(repeated, "slab", 0, 0, axis_index_groups=layers, tiled=True)


def hub_pieces(block, hub_ids, code_at):
    slabs, reps = lax.axis_size("slab"), lax.axis_size("rep")
    members = slabs // 2
    rows, width = block.shape
    piece = rows // members
    planes = [[h * members + m for m in range(members)] for h in range(2)]
    mine = lax.all_to_all(
        block.reshape(members, piece, width), "slab", 0, 0, axis_index_groups=planes, tiled=True
    )
    slab, rep = lax.axis_index("slab"), lax.axis_index("rep")
    hub_slab, hub_rep = lax.div(hub_ids, reps), lax.rem(hub_ids, reps)
    member = lax.rem(hub_slab, members)
    held = jnp.stack(
        [lax.dynamic_index_in_dim(mine, member[h], 0, keepdims=False) for h in range(HUBS)], axis=0
    )[None]
    for bit in range(2):
        got = send(held, lambda half, chip, core, rep: (half, chip, core, rep ^ (1 << bit)))
        upper = (rep >> bit) & 1 == 1
        held = jnp.concatenate([jnp.where(upper, got, held), jnp.where(upper, held, got)], axis=0)
    chosen = []
    for h in range(HUBS):
        hub = lax.dynamic_index_in_dim(held[:, h], hub_rep[h], 0, keepdims=False)
        want, _ = flags_of(hub[0, code_at])
        chosen.append(jnp.stack([hub, lax.dynamic_index_in_dim(held[:, h], want, 0, keepdims=False)], axis=0))
    held = jnp.stack(chosen, axis=0)
    got = send(held, lambda half, chip, core, rep: (1 - half, chip, core, rep))
    away = lax.div(hub_slab, members) != lax.div(slab, members)
    held = jnp.where(away[:, None, None, None], got, held)
    first_core = lax.rem(slab, 2) == 0
    keep = jnp.where(first_core, held[0], held[1])
    got = swap_cores(jnp.where(first_core, held[1], held[0]))
    return jnp.concatenate([jnp.where(first_core, keep, got), jnp.where(first_core, got, keep)], axis=1)


def body(embeddings, indicators, neighbours, hub_ids, columns):
    rows, width = embeddings.shape
    clust = indicators.shape[1]
    full = width + clust
    reps = lax.axis_size("rep")
    total = lax.axis_size("slab") * reps
    steps = rows // ROW_TILE
    slots = neighbours[0].astype(jnp.int32)
    want = slots[1] & 3
    order = slots[2] - total
    core = lax.rem(lax.axis_index("slab"), 2)

    joined, coded = join((want + 4 * order)[None], embeddings, indicators, columns)
    group_x = lax.all_gather(coded, "rep", axis=0, tiled=True)
    anchor_in, group_x = lax.optimization_barrier((indicators, group_x))
    group_y = lax.all_gather(anchor_in, "rep", axis=0, tiled=True)

    both = hub_pieces(joined, hub_ids, full)
    near = join_pieces(both[:, :, :full])
    far = swap_cores(near[:, 0])
    _, hub_order = flags_of(both[0, 0, full])
    share = hub_rows(jnp.where(hub_order == core, 2, 3)[None], both[0], near, far, width)
    near_y = join_pieces(share).reshape(rows, clust)
    far_y = swap_cores(near_y)

    member_want, member_order = flags_of(lax.dynamic_index_in_dim(group_x[:, width], want * rows, 0, keepdims=False))
    near_slot = jnp.where(order == core, 2, 3)
    member_near = jnp.where(member_order == core, 2, 3)
    pick = jnp.stack([want, member_want, near_slot, member_near]).astype(jnp.int32)
    words = keep_words(pick, joined, lambda pick: (0, full // LANES), rows)
    member_words = keep_words(pick, group_x, lambda pick: (pick[0], width // LANES), rows)
    own_rows = (joined, (ROW_TILE, width), lambda r, pick: (r, 0))
    member_rows = (group_x, (ROW_TILE, width), lambda r, pick: (pick[0] * steps + r, 0))
    own_x = (joined, (rows, width), lambda r, pick: (0, 0))
    own_y = (indicators, (rows, clust), lambda r, pick: (0, 0))
    at_member = lambda array, cols: (array, (rows, cols), lambda r, pick: (pick[0], 0))
    at_second = lambda array, cols: (array, (rows, cols), lambda r, pick: (pick[1], 0))
    chips, piece = near.shape[0], near.shape[2]
    near_x0 = (near, (chips, 1, piece, width), lambda r, pick: (0, 0, 0, 0))
    near_y0 = (near, (chips, 1, piece, clust), lambda r, pick: (0, 0, 0, width // clust))
    far_x0 = (far, (chips, piece, width), lambda r, pick: (0, 0, 0))
    far_y0 = (far, (chips, piece, clust), lambda r, pick: (0, 0, width // clust))
    whole = lambda array: (array, array.shape, lambda r, pick: (0, 0))

    degree, acc, own_tile = tile_of(pick, own_rows, own_x, words, lambda pick: 0, None, own_y)
    degree, member_tile = tile_of(pick, own_rows, at_member(group_x, width), words, lambda pick: 1, degree)
    degree_c, tile_c0 = tile_of(pick, member_rows, at_member(group_x, width), member_words, lambda pick: 0, None)
    degree_c, tile_c1 = tile_of(pick, member_rows, at_second(group_x, width), member_words, lambda pick: 1, degree_c)
    degree, acc, near_tile = tile_of(pick, own_rows, near_x0, words, lambda pick: pick[2], degree, near_y0, acc)
    degree_c, acc_c = tile_of(
        pick, member_rows, near_x0, member_words, lambda pick: pick[3], degree_c, near_y0, None, False
    )
    degree, acc, far_tile = tile_of(pick, own_rows, far_x0, words, lambda pick: 5 - pick[2], degree, far_y0, acc)
    degree_c, acc_c = tile_of(
        pick, member_rows, far_x0, member_words, lambda pick: 5 - pick[3], degree_c, far_y0, acc_c, False
    )
    by_row = (indicators, (ROW_TILE, clust), lambda r, pick: (r, 0))
    member_anchor = (group_y, (ROW_TILE, clust), lambda r, pick: (pick[0] * steps + r, 0))
    acc_c = gather_of(pick, tile_c0, at_member(group_y, clust), acc_c)
    member_new = gather_of(pick, tile_c1, at_second(group_y, clust), acc_c, degree_c, member_anchor)
    new = gather_of(pick, member_tile, at_member(group_y, clust), acc, degree, by_row)

    acc = gather_of(pick, near_tile, whole(near_y), None)
    acc = gather_of(pick, far_tile, whole(far_y), acc)
    acc = gather_of(pick, own_tile, whole(new), acc)
    return gather_of(pick, member_tile, whole(member_new), acc, degree, by_row)


def solution(mesh):
    return jax.shard_map(
        body,
        mesh=mesh,
        in_specs=(
            P(("slab", "rep"), None),
            P(("slab", "rep"), None),
            P(("slab", "rep"), None),
            P(),
            P(("slab", "rep"), None, None),
        ),
        out_specs=P(("slab", "rep"), None),
        check_vma=False,
    )
```

```python
import functools

import jax
import jax.numpy as jnp
from jax import lax
from jax.experimental import pallas as pl
from jax.experimental.pallas import tpu as pltpu
from jax.sharding import PartitionSpec as P

K = 4
HUBS = 2
TOPK = 16
LANES = 128
EPS = 1e-06
TAU = 0.04
ALPHA = 0.8
AXES = ("slab", "rep")
ROW_TILE = 256
VMEM_LIMIT = 16 << 20
HALF = 32


def join_kernel(flag_ref, x_ref, y_ref, cols_ref, all_ref, normed_ref, rest_ref):
    width, clust = x_ref.shape[1], y_ref.shape[1]
    values = x_ref[...].astype(jnp.float32)
    scale = lax.rsqrt(jnp.sum(values * values, axis=1, keepdims=True) + EPS)
    normed = (values * scale).astype(jnp.bfloat16)
    cols = cols_ref[...].reshape(K * TOPK, cols_ref.shape[2])
    coded = jnp.concatenate([cols // HALF + HALF * flag_ref[0], cols % HALF], axis=0)
    coded = coded.astype(jnp.float32).T.astype(jnp.bfloat16)
    all_ref[:, :width] = normed
    all_ref[:, width : width + clust] = y_ref[...]
    all_ref[:, width + clust :] = coded
    normed_ref[...] = normed
    rest_ref[:, :clust] = y_ref[...]
    rest_ref[:, clust:] = coded


def join(flag, embeddings, indicators, columns):
    rows, width = embeddings.shape
    clust = indicators.shape[1]
    by_row = lambda cols: pl.BlockSpec((ROW_TILE, cols), lambda r, flag: (r, 0))
    wide = (width + clust + 2 * K * TOPK, width, clust + 2 * K * TOPK)
    return pl.pallas_call(
        join_kernel,
        out_shape=[jax.ShapeDtypeStruct((rows, w), jnp.bfloat16) for w in wide],
        grid_spec=pltpu.PrefetchScalarGridSpec(
            num_scalar_prefetch=1,
            grid=(rows // ROW_TILE,),
            in_specs=[
                by_row(width),
                by_row(clust),
                pl.BlockSpec((K, TOPK, ROW_TILE), lambda r, flag: (0, 0, r)),
            ],
            out_specs=[by_row(w) for w in wide],
        ),
        compiler_params=pltpu.CompilerParams(vmem_limit_bytes=VMEM_LIMIT),
        name="join",
    )(flag, embeddings, indicators, jnp.transpose(columns, (1, 2, 0)))


def words_kernel(pick_ref, coded_ref, out_ref):
    half = K * TOPK
    lane = lax.broadcasted_iota(jnp.int32, (LANES, LANES), 0)

    @pl.loop(0, coded_ref.shape[0] // LANES)
    def _(block):
        here = pl.ds(pl.multiple_of(block * LANES, LANES), LANES)
        coded = coded_ref[here, :].astype(jnp.float32).T.astype(jnp.int32)
        high = coded[:half] & (HALF - 1)
        low = (high & 3) * HALF + coded[half:]
        bit = jnp.left_shift(jnp.ones_like(high), high >> 2)
        for slot in range(K):
            word = jnp.zeros((LANES, LANES), jnp.int32)
            for t in range(slot * TOPK, (slot + 1) * TOPK):
                word = word | jnp.where(lane == low[t : t + 1], bit[t : t + 1], 0)
            out_ref[slot, here, :] = word.T


def keep_words(pick, coded, place, rows):
    return pl.pallas_call(
        words_kernel,
        out_shape=jax.ShapeDtypeStruct((K, rows, LANES), jnp.int32),
        grid_spec=pltpu.PrefetchScalarGridSpec(
            num_scalar_prefetch=1,
            grid=(1,),
            in_specs=[pl.BlockSpec((rows, LANES), lambda i, pick: place(pick))],
            out_specs=pl.BlockSpec((K, rows, LANES), lambda i, pick: (0, 0, 0)),
        ),
        compiler_params=pltpu.CompilerParams(vmem_limit_bytes=VMEM_LIMIT),
        cost_estimate=pl.CostEstimate(flops=rows * LANES * K * TOPK, bytes_accessed=rows * 512, transcendentals=0),
        name="keep_words",
    )(pick, coded)


def mix(acc, degree, anchor):
    return (ALPHA * acc / degree + (1.0 - ALPHA) * anchor.astype(jnp.float32)).astype(jnp.bfloat16)


def weights(cosine, word, total, put):
    for j in range(cosine.shape[1] // LANES):
        part = cosine[:, j * LANES : (j + 1) * LANES]
        raw = jnp.where((word & (1 << j)) != 0, jnp.exp((part - 1.0) * (1.0 / TAU)), 0.0)
        total = total + raw
        put(slice(j * LANES, (j + 1) * LANES), raw.astype(jnp.bfloat16))
    return total


def cosines(rows, others):
    return lax.dot_general(rows, others, (((1,), (1,)), ((), ())), preferred_element_type=jnp.float32)


def flat(ref):
    value = ref[...]
    return value.reshape(-1, value.shape[-1])


def tile_kernel(has_carry, last, pick_ref, x_ref, other_ref, w_ref, y_ref, *refs):
    refs = list(refs)
    deg_in, acc_in = (refs.pop(0), refs.pop(0)) if has_carry else (None, None)
    anchor_ref = refs.pop(0) if last else None
    deg_ref, acc_ref, tile_ref = refs
    word = w_ref[0]
    total = deg_in[...] if has_carry else jnp.zeros(word.shape, jnp.float32)

    def put(lanes, value):
        tile_ref[:, lanes] = value

    total = weights(cosines(x_ref[...], flat(other_ref)), word, total, put)
    deg_ref[...] = total
    gathered = jnp.dot(tile_ref[...], flat(y_ref), preferred_element_type=jnp.float32)
    if has_carry:
        gathered = acc_in[...] + gathered
    if last:
        gathered = mix(gathered, jnp.sum(total, axis=1, keepdims=True), anchor_ref[...])
    acc_ref[...] = gathered


def tile_of(pick, x, other, y, words, slot, carry=None, anchor=None, keep=True):
    rows, clust = words.shape[1], y[1][-1]
    by_row = lambda cols: pl.BlockSpec((ROW_TILE, cols), lambda r, pick: (r, 0))
    spec = lambda operand: pl.BlockSpec(operand[1], operand[2])
    last = anchor is not None
    args = [x[0], other[0], words, y[0], *(carry or ())] + ([anchor[0]] if last else [])
    specs = [spec(x), spec(other), pl.BlockSpec((1, ROW_TILE, LANES), lambda r, pick: (slot(pick), r, 0)), spec(y)]
    specs += ([by_row(LANES), by_row(clust)] if carry else []) + ([spec(anchor)] if last else [])
    outs = [(LANES, jnp.float32), (clust, jnp.bfloat16 if last else jnp.float32)] + [(rows, jnp.bfloat16)] * keep
    return pl.pallas_call(
        functools.partial(tile_kernel, carry is not None, last),
        out_shape=[jax.ShapeDtypeStruct((rows, cols), kind) for cols, kind in outs],
        grid_spec=pltpu.PrefetchScalarGridSpec(
            num_scalar_prefetch=1,
            grid=(rows // ROW_TILE,),
            in_specs=specs,
            out_specs=[by_row(cols) for cols, _ in outs],
            scratch_shapes=[] if keep else [pltpu.VMEM((ROW_TILE, rows), jnp.bfloat16)],
        ),
        compiler_params=pltpu.CompilerParams(vmem_limit_bytes=VMEM_LIMIT),
        cost_estimate=pl.CostEstimate(flops=2 * rows * rows * 768, bytes_accessed=4 * rows * rows, transcendentals=rows * rows),
        name="tile",
    )(pick, *args)


def gather_kernel(has_acc, last, pick_ref, tile_ref, y_ref, *refs):
    refs = list(refs)
    acc_in = refs.pop(0) if has_acc else None
    deg_ref, anchor_ref = (refs.pop(0), refs.pop(0)) if last else (None, None)
    gathered = jnp.dot(tile_ref[...], flat(y_ref), preferred_element_type=jnp.float32)
    if has_acc:
        gathered = acc_in[...] + gathered
    if last:
        gathered = mix(gathered, jnp.sum(deg_ref[...], axis=1, keepdims=True), anchor_ref[...])
    refs[0][...] = gathered


def gather_of(pick, tile, y, acc, degree=None, anchor=None):
    rows, clust = tile.shape[0], y[1][-1]
    by_row = lambda cols: pl.BlockSpec((ROW_TILE, cols), lambda r, pick: (r, 0))
    spec = lambda operand: pl.BlockSpec(operand[1], operand[2])
    last = degree is not None
    args = [tile, y[0]] + ([acc] if acc is not None else []) + ([degree, anchor[0]] if last else [])
    specs = [by_row(rows), spec(y)] + ([by_row(clust)] if acc is not None else [])
    specs += [by_row(LANES), spec(anchor)] if last else []
    return pl.pallas_call(
        functools.partial(gather_kernel, acc is not None, last),
        out_shape=jax.ShapeDtypeStruct((rows, clust), jnp.bfloat16 if last else jnp.float32),
        grid_spec=pltpu.PrefetchScalarGridSpec(
            num_scalar_prefetch=1, grid=(rows // ROW_TILE,), in_specs=specs, out_specs=by_row(clust)
        ),
        compiler_params=pltpu.CompilerParams(vmem_limit_bytes=VMEM_LIMIT),
        cost_estimate=pl.CostEstimate(flops=2 * rows * rows * clust, bytes_accessed=3 * rows * rows, transcendentals=0),
        name="gather",
    )(pick, *args)


def hub_rows_kernel(width, pick_ref, rows_ref, near_ref, far_ref, out_ref, word_ref, tile_ref):
    clust = out_ref.shape[1]
    half = K * TOPK
    coded = rows_ref[:, width + clust :].astype(jnp.float32).astype(jnp.int32)
    high = coded[:, :half] & (HALF - 1)
    low = (high & 3) * HALF + coded[:, half:]
    bit = jnp.left_shift(jnp.ones_like(high), high >> 2)
    lane = lax.broadcasted_iota(jnp.int32, (rows_ref.shape[0], LANES), 1)
    for slot in range(K):
        word = jnp.zeros(lane.shape, jnp.int32)
        for t in range(slot * TOPK, (slot + 1) * TOPK):
            word = word | jnp.where(lane == low[:, t : t + 1], bit[:, t : t + 1], 0)
        word_ref[slot] = word
    total = jnp.zeros(lane.shape, jnp.float32)
    acc = jnp.zeros(out_ref.shape, jnp.float32)

    def put(lanes, value):
        tile_ref[:, lanes] = value

    self_block = near_ref[:, 0].reshape(-1, width + clust)
    member_block = near_ref[:, 1].reshape(-1, width + clust)
    far_block = flat(far_ref)
    slots = (0, 1, pick_ref[0], 5 - pick_ref[0])
    for slot, block in zip(slots, (self_block, member_block, self_block, far_block)):
        total = weights(cosines(rows_ref[:, :width], block[:, :width]), word_ref[slot], total, put)
        acc = acc + jnp.dot(tile_ref[...], block[:, width:], preferred_element_type=jnp.float32)
    out_ref[...] = mix(acc, jnp.sum(total, axis=1, keepdims=True), rows_ref[:, width : width + clust])


def hub_rows(self_slot, mine, near, far, width):
    share = mine.shape[0]
    clust = near.shape[3] - width
    rows = near.shape[0] * near.shape[2]
    return pl.pallas_call(
        functools.partial(hub_rows_kernel, width),
        out_shape=jax.ShapeDtypeStruct((share, clust), jnp.bfloat16),
        grid_spec=pltpu.PrefetchScalarGridSpec(
            num_scalar_prefetch=1,
            grid=(1,),
            in_specs=[
                pl.BlockSpec(mine.shape, lambda i, pick: (0, 0)),
                pl.BlockSpec(near.shape, lambda i, pick: (0, 0, 0, 0)),
                pl.BlockSpec(far.shape, lambda i, pick: (0, 0, 0)),
            ],
            out_specs=pl.BlockSpec((share, clust), lambda i, pick: (0, 0)),
            scratch_shapes=[pltpu.VMEM((K, share, LANES), jnp.int32), pltpu.VMEM((share, rows), jnp.bfloat16)],
        ),
        compiler_params=pltpu.CompilerParams(vmem_limit_bytes=20 << 20),
        cost_estimate=pl.CostEstimate(flops=share * rows * 6144, bytes_accessed=6 << 20, transcendentals=share * rows * K),
        name="hub_rows",
    )(self_slot, mine, near, far)


def send(block, target):
    slabs, reps = lax.axis_size("slab"), lax.axis_size("rep")
    chips = slabs // 4
    pairs = []
    for device in range(slabs * reps):
        slab, rep = divmod(device, reps)
        to = target(slab // (2 * chips), slab // 2 % chips, slab % 2, rep)
        if to is not None:
            pairs.append((device, ((to[0] * chips + to[1]) * 2 + to[2]) * reps + to[3]))
    return lax.ppermute(block, AXES, pairs)


def along_line(block, table):
    return send(
        block, lambda half, chip, core, rep: (half, chip, core, table[rep]) if rep in table else None
    )


def swap_cores(block):
    return send(block, lambda half, chip, core, rep: (half, chip, 1 - core, rep))


def flags_of(code):
    flag = code.astype(jnp.float32).astype(jnp.int32) // HALF
    return flag & 3, (flag >> 2) & 1


def join_pieces(piece):
    slabs = lax.axis_size("slab")
    members, chips = slabs // 2, slabs // 4
    layers = [[h * members + c * 2 + core for c in range(chips)] for h in range(2) for core in range(2)]
    repeated = jnp.broadcast_to(piece[None], (chips,) + piece.shape)
    return lax.all_to_all(repeated, "slab", 0, 0, axis_index_groups=layers, tiled=True)


def scatter(block):
    members = lax.axis_size("slab") // 2
    rows, width = block.shape
    planes = [[h * members + m for m in range(members)] for h in range(2)]
    return lax.all_to_all(
        block.reshape(members, rows // members, width), "slab", 0, 0, axis_index_groups=planes, tiled=True
    )


def hub_pieces(mine, hub_ids, code_at):
    members, reps = lax.axis_size("slab") // 2, lax.axis_size("rep")
    slab = lax.axis_index("slab")
    hub_slab, hub_rep = lax.div(hub_ids, reps), lax.rem(hub_ids, reps)
    member = lax.rem(hub_slab, members)
    held = jnp.stack(
        [lax.dynamic_index_in_dim(mine, member[h], 0, keepdims=False) for h in range(HUBS)], axis=0
    )
    held = lax.all_gather(held, "rep", axis=0, tiled=False)
    chosen = []
    for h in range(HUBS):
        hub = lax.dynamic_index_in_dim(held[:, h], hub_rep[h], 0, keepdims=False)
        want, _ = flags_of(hub[0, code_at])
        chosen.append(jnp.stack([hub, lax.dynamic_index_in_dim(held[:, h], want, 0, keepdims=False)], axis=0))
    held = jnp.stack(chosen, axis=0)
    got = send(held, lambda half, chip, core, rep: (1 - half, chip, core, rep))
    away = lax.div(hub_slab, members) != lax.div(slab, members)
    held = jnp.where(away[:, None, None, None], got, held)
    first_core = lax.rem(slab, 2) == 0
    keep = jnp.where(first_core, held[0], held[1])
    got = swap_cores(jnp.where(first_core, held[1], held[0]))
    return jnp.concatenate([jnp.where(first_core, keep, got), jnp.where(first_core, got, keep)], axis=1)


def body(embeddings, indicators, neighbours, hub_ids, columns):
    rows, width = embeddings.shape
    clust = indicators.shape[1]
    full = width + clust
    reps = lax.axis_size("rep")
    total = lax.axis_size("slab") * reps
    rep = lax.axis_index("rep")
    steps = rows // ROW_TILE
    slots = neighbours[0].astype(jnp.int32)
    want = slots[1] & 3
    order = slots[2] - total
    core = lax.rem(lax.axis_index("slab"), 2)
    near_slot = jnp.where(order == core, 2, 3)
    barrier = lax.optimization_barrier

    joined, normed, rest = join((want + 4 * order)[None], embeddings, indicators, columns)
    group_x = lax.all_gather(normed, "rep", axis=0, tiled=True)
    across = along_line(rest, {0: 2, 2: 0, 1: 3, 3: 1})
    beside = along_line(rest, {0: 1, 1: 0, 2: 3, 3: 2})
    middle = along_line(rest, {1: 2, 2: 1})

    pick = jnp.stack([near_slot]).astype(jnp.int32)
    own_rows = (joined, (ROW_TILE, width), lambda r, pick: (r, 0))
    own_x = (joined, (rows, width), lambda r, pick: (0, 0))
    own_y = (joined, (rows, clust), lambda r, pick: (0, width // clust))
    words = keep_words(pick, joined, lambda pick: (0, full // LANES), rows)
    *carry, own_tile = tile_of(pick, own_rows, own_x, own_y, words, lambda pick: 0)
    mine, words, carry, own_tile = barrier((scatter(joined), words, carry, own_tile))

    both = hub_pieces(mine, hub_ids, full)
    outer = along_line(across, {1: 0, 2: 3})
    third = jnp.where((rep == 0) | (rep == 3), outer, middle)
    group_rest = jnp.concatenate([rest, beside, across, third], axis=0)
    at = want ^ rep
    member_want, member_order = flags_of(
        lax.dynamic_index_in_dim(group_rest[:, clust], at * rows, 0, keepdims=False)
    )
    pick = jnp.stack(
        [near_slot, want, member_want, jnp.where(member_order == core, 2, 3), at, member_want ^ rep]
    ).astype(jnp.int32)
    member_words = keep_words(pick, group_rest, lambda pick: (pick[4], clust // LANES), rows)
    both, group_rest, member_words = barrier((both, group_rest, member_words))

    member_rows = (group_x, (ROW_TILE, width), lambda r, pick: (pick[1] * steps + r, 0))
    member_x = (group_x, (rows, width), lambda r, pick: (pick[1], 0))
    second_x = (group_x, (rows, width), lambda r, pick: (pick[2], 0))
    member_y = (group_rest, (rows, clust), lambda r, pick: (pick[4], 0))
    second_y = (group_rest, (rows, clust), lambda r, pick: (pick[5], 0))
    near = join_pieces(both[:, :, :full])
    *carry, member_tile = tile_of(pick, own_rows, member_x, member_y, words, lambda pick: 1, carry)
    carry_c = tile_of(pick, member_rows, member_x, member_y, member_words, lambda pick: 0, None, None, False)
    carry_c = tile_of(pick, member_rows, second_x, second_y, member_words, lambda pick: 1, carry_c, None, False)
    near, carry, carry_c = barrier((near, carry, carry_c))

    chips, _, piece, _ = near.shape
    near_x = (near, (chips, 1, piece, width), lambda r, pick: (0, 0, 0, 0))
    near_y = (near, (chips, 1, piece, clust), lambda r, pick: (0, 0, 0, width // clust))
    far = swap_cores(near[:, 0])
    far_x = (far, (chips, piece, width), lambda r, pick: (0, 0, 0))
    far_y = (far, (chips, piece, clust), lambda r, pick: (0, 0, width // clust))
    *carry, near_tile = tile_of(pick, own_rows, near_x, near_y, words, lambda pick: pick[0], carry)
    far, carry = barrier((far, carry))
    far_x, far_y = (far, *far_x[1:]), (far, *far_y[1:])
    _, hub_order = flags_of(both[0, 0, full])
    share = hub_rows(jnp.where(hub_order == core, 2, 3)[None], both[0], near, far, width)

    near_new = join_pieces(share).reshape(rows, clust)
    by_row = (indicators, (ROW_TILE, clust), lambda r, pick: (r, 0))
    member_anchor = (group_rest, (ROW_TILE, clust), lambda r, pick: (pick[4] * steps + r, 0))
    carry_c = tile_of(
        pick, member_rows, near_x, near_y, member_words, lambda pick: pick[3], carry_c, None, False
    )
    degree, new, far_tile = tile_of(pick, own_rows, far_x, far_y, words, lambda pick: 5 - pick[0], carry, by_row)
    _, member_new = tile_of(
        pick, member_rows, far_x, far_y, member_words, lambda pick: 5 - pick[3], carry_c, member_anchor, False
    )
    near_new, new, member_new = barrier((near_new, new, member_new))
    far_new = swap_cores(near_new)

    whole = lambda array: (array, array.shape, lambda r, pick: (0, 0))
    acc = gather_of(pick, own_tile, whole(new), None)
    acc = gather_of(pick, member_tile, whole(member_new), acc)
    acc = gather_of(pick, near_tile, whole(near_new), acc)
    return gather_of(pick, far_tile, whole(far_new), acc, degree, by_row)


def solution(mesh):
    return jax.shard_map(
        body,
        mesh=mesh,
        in_specs=(
            P(("slab", "rep"), None),
            P(("slab", "rep"), None),
            P(("slab", "rep"), None),
            P(),
            P(("slab", "rep"), None, None),
        ),
        out_specs=P(("slab", "rep"), None),
        check_vma=False,
    )
```

```python
import functools

import jax
import jax.numpy as jnp
from jax import lax
from jax.experimental import pallas as pl
from jax.experimental.pallas import tpu as pltpu
from jax.sharding import PartitionSpec as P

K = 4
HUBS = 2
TOPK = 16
LANES = 128
EPS = 1e-06
TAU = 0.04
ALPHA = 0.8
AXES = ("slab", "rep")
ROW_TILE = 256
VMEM_LIMIT = 58 << 20
SCALE = 1.4426950408889634 / TAU
HALF = 32


def join_kernel(flag_ref, x_ref, y_ref, cols_ref, all_ref):
    width, clust = x_ref.shape[1], y_ref.shape[1]
    values = x_ref[...].astype(jnp.float32)
    scale = lax.rsqrt(jnp.sum(values * values, axis=1, keepdims=True) + EPS)
    normed = (values * scale).astype(jnp.bfloat16)
    cols = cols_ref[...].reshape(K * TOPK, cols_ref.shape[2])
    coded = jnp.concatenate([(cols >> 5) + HALF * flag_ref[0], cols & (HALF - 1)], axis=0)
    coded = coded.astype(jnp.float32).T.astype(jnp.bfloat16)
    all_ref[:, :width] = normed
    all_ref[:, width : width + clust] = y_ref[...]
    all_ref[:, width + clust :] = coded


def join(flag, embeddings, indicators, columns):
    rows, width = embeddings.shape
    clust = indicators.shape[1]
    by_row = lambda cols: pl.BlockSpec((ROW_TILE, cols), lambda r, flag: (r, 0))
    wide = width + clust + 2 * K * TOPK
    return pl.pallas_call(
        join_kernel,
        out_shape=jax.ShapeDtypeStruct((rows, wide), jnp.bfloat16),
        grid_spec=pltpu.PrefetchScalarGridSpec(
            num_scalar_prefetch=1,
            grid=(rows // ROW_TILE,),
            in_specs=[
                by_row(width),
                by_row(clust),
                pl.BlockSpec((K, TOPK, ROW_TILE), lambda r, flag: (0, 0, r)),
            ],
            out_specs=by_row(wide),
        ),
        compiler_params=pltpu.CompilerParams(vmem_limit_bytes=VMEM_LIMIT),
        name="join",
    )(flag, embeddings, indicators, jnp.transpose(columns, (1, 2, 0)))


def words_kernel(pick_ref, coded_ref, out_ref):
    half = K * TOPK
    lane = lax.broadcasted_iota(jnp.int32, (LANES, LANES), 0)

    @pl.loop(0, coded_ref.shape[0] // LANES)
    def _(block):
        here = pl.ds(pl.multiple_of(block * LANES, LANES), LANES)
        coded = coded_ref[here, :].astype(jnp.float32).T.astype(jnp.int32)
        high = coded[:half] & (HALF - 1)
        low = (high & 3) * HALF + coded[half:]
        bit = jnp.left_shift(jnp.ones_like(high), high >> 2)
        for slot in range(K):
            word = jnp.zeros((LANES, LANES), jnp.int32)
            for t in range(slot * TOPK, (slot + 1) * TOPK):
                word = word | jnp.where(lane == low[t : t + 1], bit[t : t + 1], 0)
            out_ref[slot, here, :] = word.T


def keep_words(pick, coded, place, rows):
    return pl.pallas_call(
        words_kernel,
        out_shape=jax.ShapeDtypeStruct((K, rows, LANES), jnp.int32),
        grid_spec=pltpu.PrefetchScalarGridSpec(
            num_scalar_prefetch=1,
            grid=(1,),
            in_specs=[pl.BlockSpec((rows, LANES), lambda i, pick: place(pick))],
            out_specs=pl.BlockSpec((K, rows, LANES), lambda i, pick: (0, 0, 0)),
        ),
        compiler_params=pltpu.CompilerParams(vmem_limit_bytes=VMEM_LIMIT),
        cost_estimate=pl.CostEstimate(flops=rows * LANES * K * TOPK, bytes_accessed=rows * 512, transcendentals=0),
        name="keep_words",
    )(pick, coded)


def mix(acc, degree, anchor):
    return (ALPHA * acc / degree + (1.0 - ALPHA) * anchor.astype(jnp.float32)).astype(jnp.bfloat16)


def weights(cosine, word, total, put):
    for j in range(cosine.shape[1] // LANES):
        part = cosine[:, j * LANES : (j + 1) * LANES]
        raw = jnp.where((word & (1 << j)) != 0, jnp.exp2(part * SCALE - SCALE), 0.0)
        total = total + raw
        put(slice(j * LANES, (j + 1) * LANES), raw.astype(jnp.bfloat16))
    return total


def cosines(rows, others):
    return lax.dot_general(rows, others, (((1,), (1,)), ((), ())), preferred_element_type=jnp.float32)


def flat(ref):
    value = ref[...]
    return value.reshape(-1, value.shape[-1])


def tile_kernel(has_carry, last, pick_ref, x_ref, other_ref, w_ref, y_ref, *refs):
    refs = list(refs)
    deg_in, acc_in = (refs.pop(0), refs.pop(0)) if has_carry else (None, None)
    anchor_ref = refs.pop(0) if last else None
    deg_ref, acc_ref, tile_ref = refs
    word = w_ref[0]
    total = deg_in[...] if has_carry else jnp.zeros(word.shape, jnp.float32)

    def put(lanes, value):
        tile_ref[:, lanes] = value

    total = weights(cosines(x_ref[...], flat(other_ref)), word, total, put)
    deg_ref[...] = total
    gathered = jnp.dot(tile_ref[...], flat(y_ref), preferred_element_type=jnp.float32)
    if has_carry:
        gathered = acc_in[...] + gathered
    if last:
        gathered = mix(gathered, jnp.sum(total, axis=1, keepdims=True), anchor_ref[...])
    acc_ref[...] = gathered


def tile_of(pick, x, other, y, words, slot, carry=None, anchor=None, keep=True):
    rows, clust = words.shape[1], y[1][-1]
    by_row = lambda cols: pl.BlockSpec((ROW_TILE, cols), lambda r, pick: (r, 0))
    spec = lambda operand: pl.BlockSpec(operand[1], operand[2])
    last = anchor is not None
    args = [x[0], other[0], words, y[0], *(carry or ())] + ([anchor[0]] if last else [])
    specs = [spec(x), spec(other), pl.BlockSpec((1, ROW_TILE, LANES), lambda r, pick: (slot(pick), r, 0)), spec(y)]
    specs += ([by_row(LANES), by_row(clust)] if carry else []) + ([spec(anchor)] if last else [])
    outs = [(LANES, jnp.float32), (clust, jnp.bfloat16 if last else jnp.float32)] + [(rows, jnp.bfloat16)] * keep
    return pl.pallas_call(
        functools.partial(tile_kernel, carry is not None, last),
        out_shape=[jax.ShapeDtypeStruct((rows, cols), kind) for cols, kind in outs],
        grid_spec=pltpu.PrefetchScalarGridSpec(
            num_scalar_prefetch=1,
            grid=(rows // ROW_TILE,),
            in_specs=specs,
            out_specs=[by_row(cols) for cols, _ in outs],
            scratch_shapes=[] if keep else [pltpu.VMEM((ROW_TILE, rows), jnp.bfloat16)],
        ),
        compiler_params=pltpu.CompilerParams(vmem_limit_bytes=VMEM_LIMIT),
        cost_estimate=pl.CostEstimate(flops=2 * rows * rows * 768, bytes_accessed=4 * rows * rows, transcendentals=rows * rows),
        name="tile",
    )(pick, *args)


def seven_kernel(
    width, pick_ref, rows_ref, first_ref, second_ref, near_ref, far_ref, words_ref, member_ref, deg_in, acc_in, anchor_ref,
    near_tile, far_tile, member_tile, deg_ref, new_ref, other_ref, held_ref,
):
    def put_to(ref):
        def put(lanes, value):
            ref[:, lanes] = value

        return put

    def run(rows, plan, total, acc):
        for word, (other, y), tile in plan:
            total = weights(cosines(rows, other), word, total, put_to(tile))
            acc = acc + jnp.dot(tile[...], y, preferred_element_type=jnp.float32)
        return total, acc

    step = pl.program_id(0)
    split = lambda block: (block[:, :width], block[:, width:])
    first, second = split(first_ref[...]), split(second_ref[...])
    near, far = split(near_ref[:, 0].reshape(-1, near_ref.shape[3])), split(flat(far_ref))
    plan = (
        (words_ref[1], first, member_tile),
        (words_ref[pick_ref[0]], near, near_tile),
        (words_ref[5 - pick_ref[0]], far, far_tile),
    )
    total, acc = run(rows_ref[...], plan, deg_in[...], acc_in[...])
    deg_ref[...] = total
    new_ref[...] = mix(acc, jnp.sum(total, axis=1, keepdims=True), anchor_ref[...])
    here = pl.ds(pl.multiple_of(step * ROW_TILE, ROW_TILE), ROW_TILE)
    mine = first_ref[here, :]
    plan = (
        (member_ref[0], first, held_ref),
        (member_ref[1], second, held_ref),
        (member_ref[pick_ref[3]], near, held_ref),
        (member_ref[5 - pick_ref[3]], far, held_ref),
    )
    total, acc = run(mine[:, :width], plan, jnp.zeros(deg_in.shape, jnp.float32), jnp.zeros(acc_in.shape, jnp.float32))
    other_ref[...] = mix(acc, jnp.sum(total, axis=1, keepdims=True), mine[:, width:])


def seven_of(pick, joined, group, near, far, words, member_words, carry, anchor, width):
    rows, clust = anchor.shape
    chips, _, piece, full = near.shape
    once = pl.Buffered(1)
    by_row = lambda cols: pl.BlockSpec((ROW_TILE, cols), lambda r, pick: (r, 0))
    group_at = lambda k: pl.BlockSpec((rows, full), lambda r, pick: (pick[k], 0), pipeline_mode=once)
    by_word = pl.BlockSpec((K, ROW_TILE, LANES), lambda r, pick: (0, r, 0))
    outs = [(rows, jnp.bfloat16)] * 3 + [(LANES, jnp.float32)] + [(clust, jnp.bfloat16)] * 2
    return pl.pallas_call(
        functools.partial(seven_kernel, width),
        out_shape=[jax.ShapeDtypeStruct((rows, cols), kind) for cols, kind in outs],
        grid_spec=pltpu.PrefetchScalarGridSpec(
            num_scalar_prefetch=1,
            grid=(rows // ROW_TILE,),
            in_specs=[
                by_row(width),
                group_at(1),
                group_at(2),
                pl.BlockSpec((chips, 1, piece, full), lambda r, pick: (0, 0, 0, 0), pipeline_mode=once),
                pl.BlockSpec((chips, piece, full), lambda r, pick: (0, 0, 0), pipeline_mode=once),
                by_word,
                by_word,
                by_row(LANES),
                by_row(clust),
                by_row(clust),
            ],
            out_specs=[by_row(cols) for cols, _ in outs],
            scratch_shapes=[pltpu.VMEM((ROW_TILE, rows), jnp.bfloat16)],
        ),
        compiler_params=pltpu.CompilerParams(vmem_limit_bytes=VMEM_LIMIT),
        cost_estimate=pl.CostEstimate(
            flops=14 * rows * rows * full, bytes_accessed=16 * rows * rows, transcendentals=7 * rows * rows
        ),
        name="seven",
    )(pick, joined, group, group, near, far, words, member_words, *carry, anchor)


def last_kernel(*refs):
    tiles, news, (deg_ref, anchor_ref, out_ref) = refs[:K], refs[K : 2 * K], refs[2 * K :]
    acc = sum(jnp.dot(t[...], y[...], preferred_element_type=jnp.float32) for t, y in zip(tiles, news))
    out_ref[...] = mix(acc, jnp.sum(deg_ref[...], axis=1, keepdims=True), anchor_ref[...])


def last_of(tiles, news, degree, anchor):
    rows, clust = anchor.shape
    by_row = lambda cols: pl.BlockSpec((ROW_TILE, cols), lambda r: (r, 0))
    return pl.pallas_call(
        last_kernel,
        out_shape=jax.ShapeDtypeStruct((rows, clust), jnp.bfloat16),
        grid=(rows // ROW_TILE,),
        in_specs=[by_row(rows)] * K
        + [pl.BlockSpec((rows, clust), lambda r: (0, 0))] * K
        + [by_row(LANES), by_row(clust)],
        out_specs=by_row(clust),
        compiler_params=pltpu.CompilerParams(vmem_limit_bytes=VMEM_LIMIT),
        cost_estimate=pl.CostEstimate(flops=8 * rows * rows * clust, bytes_accessed=8 * rows * rows, transcendentals=0),
        name="last",
    )(*tiles, *news, degree, anchor)


def hub_rows_kernel(width, pick_ref, rows_ref, near_ref, far_ref, out_ref, word_ref, tile_ref):
    clust = out_ref.shape[1]
    half = K * TOPK
    coded = rows_ref[:, width + clust :].astype(jnp.float32).astype(jnp.int32)
    high = coded[:, :half] & (HALF - 1)
    low = (high & 3) * HALF + coded[:, half:]
    bit = jnp.left_shift(jnp.ones_like(high), high >> 2)
    lane = lax.broadcasted_iota(jnp.int32, (rows_ref.shape[0], LANES), 1)
    for slot in range(K):
        word = jnp.zeros(lane.shape, jnp.int32)
        for t in range(slot * TOPK, (slot + 1) * TOPK):
            word = word | jnp.where(lane == low[:, t : t + 1], bit[:, t : t + 1], 0)
        word_ref[slot] = word
    total = jnp.zeros(lane.shape, jnp.float32)
    acc = jnp.zeros(out_ref.shape, jnp.float32)

    def put(lanes, value):
        tile_ref[:, lanes] = value

    self_block = near_ref[:, 0].reshape(-1, width + clust)
    member_block = near_ref[:, 1].reshape(-1, width + clust)
    far_block = flat(far_ref)
    slots = (0, 1, pick_ref[0], 5 - pick_ref[0])
    for slot, block in zip(slots, (self_block, member_block, self_block, far_block)):
        total = weights(cosines(rows_ref[:, :width], block[:, :width]), word_ref[slot], total, put)
        acc = acc + jnp.dot(tile_ref[...], block[:, width:], preferred_element_type=jnp.float32)
    out_ref[...] = mix(acc, jnp.sum(total, axis=1, keepdims=True), rows_ref[:, width : width + clust])


def hub_rows(self_slot, mine, near, far, width):
    share = mine.shape[0]
    clust = near.shape[3] - width
    rows = near.shape[0] * near.shape[2]
    return pl.pallas_call(
        functools.partial(hub_rows_kernel, width),
        out_shape=jax.ShapeDtypeStruct((share, clust), jnp.bfloat16),
        grid_spec=pltpu.PrefetchScalarGridSpec(
            num_scalar_prefetch=1,
            grid=(1,),
            in_specs=[
                pl.BlockSpec(mine.shape, lambda i, pick: (0, 0)),
                pl.BlockSpec(near.shape, lambda i, pick: (0, 0, 0, 0)),
                pl.BlockSpec(far.shape, lambda i, pick: (0, 0, 0)),
            ],
            out_specs=pl.BlockSpec((share, clust), lambda i, pick: (0, 0)),
            scratch_shapes=[pltpu.VMEM((K, share, LANES), jnp.int32), pltpu.VMEM((share, rows), jnp.bfloat16)],
        ),
        compiler_params=pltpu.CompilerParams(vmem_limit_bytes=VMEM_LIMIT),
        cost_estimate=pl.CostEstimate(flops=share * rows * 6144, bytes_accessed=6 << 20, transcendentals=share * rows * K),
        name="hub_rows",
    )(self_slot, mine, near, far)


def send(block, target):
    slabs, reps = lax.axis_size("slab"), lax.axis_size("rep")
    chips = slabs // 4
    pairs = []
    for device in range(slabs * reps):
        slab, rep = divmod(device, reps)
        to = target(slab // (2 * chips), slab // 2 % chips, slab % 2, rep)
        if to is not None:
            pairs.append((device, ((to[0] * chips + to[1]) * 2 + to[2]) * reps + to[3]))
    return lax.ppermute(block, AXES, pairs)


def along_line(block, table):
    return send(
        block, lambda half, chip, core, rep: (half, chip, core, table[rep]) if rep in table else None
    )


def swap_cores(block):
    return send(block, lambda half, chip, core, rep: (half, chip, 1 - core, rep))


def flags_of(code):
    flag = code.astype(jnp.float32).astype(jnp.int32) // HALF
    return flag & 3, (flag >> 2) & 1


def join_pieces(piece):
    slabs = lax.axis_size("slab")
    members, chips = slabs // 2, slabs // 4
    layers = [[h * members + c * 2 + core for c in range(chips)] for h in range(2) for core in range(2)]
    repeated = jnp.broadcast_to(piece[None], (chips,) + piece.shape)
    return lax.all_to_all(repeated, "slab", 0, 0, axis_index_groups=layers, tiled=True)


def scatter(block):
    members = lax.axis_size("slab") // 2
    rows, width = block.shape
    planes = [[h * members + m for m in range(members)] for h in range(2)]
    return lax.all_to_all(
        block.reshape(members, rows // members, width), "slab", 0, 0, axis_index_groups=planes, tiled=True
    )


def hub_pieces(mine, hub_ids, code_at):
    members, reps = lax.axis_size("slab") // 2, lax.axis_size("rep")
    slab = lax.axis_index("slab")
    hub_slab, hub_rep = lax.div(hub_ids, reps), lax.rem(hub_ids, reps)
    member = lax.rem(hub_slab, members)
    held = jnp.stack(
        [lax.dynamic_index_in_dim(mine, member[h], 0, keepdims=False) for h in range(HUBS)], axis=0
    )
    held = held[None]
    rep = lax.axis_index("rep")
    for bit in range(2):
        got = along_line(held, {r: r ^ (1 << bit) for r in range(4)})
        upper = (rep >> bit) & 1 == 1
        held = jnp.concatenate([jnp.where(upper, got, held), jnp.where(upper, held, got)], axis=0)
    chosen = []
    for h in range(HUBS):
        pieces = held[:, h]
        hub = lax.dynamic_index_in_dim(pieces, hub_rep[h], 0, keepdims=False)
        want, _ = flags_of(hub[:1, code_at : code_at + 1])
        wanted = jnp.where(want < 2, jnp.where(want == 0, pieces[0], pieces[1]), jnp.where(want == 2, pieces[2], pieces[3]))
        chosen.append(jnp.stack([hub, wanted], axis=0))
    held = jnp.stack(chosen, axis=0)
    got = send(held, lambda half, chip, core, rep: (1 - half, chip, core, rep))
    away = lax.div(hub_slab, members) != lax.div(slab, members)
    held = jnp.where(away[:, None, None, None], got, held)
    first_core = lax.rem(slab, 2) == 0
    keep = jnp.where(first_core, held[0], held[1])
    got = swap_cores(jnp.where(first_core, held[1], held[0]))
    return jnp.concatenate([jnp.where(first_core, keep, got), jnp.where(first_core, got, keep)], axis=1)


def body(embeddings, indicators, neighbours, hub_ids, columns):
    rows, width = embeddings.shape
    clust = indicators.shape[1]
    full = width + clust
    reps = lax.axis_size("rep")
    total = lax.axis_size("slab") * reps
    slots = neighbours[0].astype(jnp.int32)
    want = slots[1] & 3
    order = slots[2] - total
    core = lax.rem(lax.axis_index("slab"), 2)
    near_slot = jnp.where(order == core, 2, 3)
    barrier = lax.optimization_barrier

    joined = join((want + 4 * order)[None], embeddings, indicators, columns)
    group = lax.all_gather(joined, "rep", axis=0, tiled=True)

    pick = jnp.stack([near_slot]).astype(jnp.int32)
    own_rows = (joined, (ROW_TILE, width), lambda r, pick: (r, 0))
    own_x = (joined, (rows, width), lambda r, pick: (0, 0))
    own_y = (joined, (rows, clust), lambda r, pick: (0, width // clust))
    words = keep_words(pick, joined, lambda pick: (0, full // LANES), rows)
    *carry, own_tile = tile_of(pick, own_rows, own_x, own_y, words, lambda pick: 0)
    mine, words, carry, own_tile = barrier((scatter(joined), words, carry, own_tile))

    both = hub_pieces(mine, hub_ids, full)
    near = join_pieces(both[:, :, :full])
    far = swap_cores(near[:, 0])
    _, hub_order = flags_of(both[0, 0, full])
    share = hub_rows(jnp.where(hub_order == core, 2, 3).astype(jnp.int32)[None], both[0], near, far, width)
    share, group = barrier((share, group))

    near_new = join_pieces(share).reshape(rows, clust)
    member_want, member_order = flags_of(
        lax.dynamic_index_in_dim(group[:, full], want * rows, 0, keepdims=False)
    )
    pick = jnp.stack([near_slot, want, member_want, jnp.where(member_order == core, 2, 3)]).astype(jnp.int32)
    member_words = keep_words(pick, group, lambda pick: (pick[1], full // LANES), rows)
    near_tile, far_tile, member_tile, degree, new, member_new = seven_of(
        pick, joined, group, near, far, words, member_words, carry, indicators, width
    )
    near_new, new = barrier((near_new, new))
    far_new = swap_cores(near_new)
    return last_of(
        (own_tile, member_tile, near_tile, far_tile), (new, member_new, near_new, far_new), degree, indicators
    )


def solution(mesh):
    return jax.shard_map(
        body,
        mesh=mesh,
        in_specs=(
            P(("slab", "rep"), None),
            P(("slab", "rep"), None),
            P(("slab", "rep"), None),
            P(),
            P(("slab", "rep"), None, None),
        ),
        out_specs=P(("slab", "rep"), None),
        check_vma=False,
    )
```

```python
import functools

import jax
import jax.numpy as jnp
from jax import lax
from jax.experimental import pallas as pl
from jax.experimental.pallas import tpu as pltpu
from jax.sharding import PartitionSpec as P

K = 4
HUBS = 2
TOPK = 16
LANES = 128
EPS = 1e-06
TAU = 0.04
ALPHA = 0.8
AXES = ("slab", "rep")
ROW_TILE = 256
VMEM_LIMIT = 58 << 20
SCALE = 1.4426950408889634 / TAU
HALF = 32
FLAG_ROWS = 16
BLOCKS_NEAR = 5


def join_kernel(flag_ref, x_ref, y_ref, cols_ref, all_ref, normed_ref, rest_ref):
    width, clust = x_ref.shape[1], y_ref.shape[1]
    step = pl.program_id(0)
    rows = pl.num_programs(0) * ROW_TILE
    values = x_ref[...].astype(jnp.float32)
    scale = lax.rsqrt(jnp.sum(values * values, axis=1, keepdims=True) + EPS)
    normed = (values * scale).astype(jnp.bfloat16)
    cols = cols_ref[...].reshape(K * TOPK, cols_ref.shape[2])
    coded = jnp.concatenate([(cols >> 5) + HALF * flag_ref[0], cols & (HALF - 1)], axis=0)
    all_ref[:, :width] = normed
    all_ref[:, width : width + clust] = y_ref[...]
    all_ref[:, width + clust :] = coded.astype(jnp.float32).T.astype(jnp.bfloat16)
    normed_ref[...] = normed
    rest_ref[pl.ds(pl.multiple_of(step * ROW_TILE, ROW_TILE), ROW_TILE), :] = y_ref[...]
    single = jnp.left_shift((cols & (LANES - 1)) + LANES, cols >> 7)
    place = pl.multiple_of(rows + step * K * TOPK, K * TOPK)
    rest_ref[pl.ds(place, K * TOPK), :] = single.astype(jnp.float32).astype(jnp.bfloat16)
    flags = jnp.full((FLAG_ROWS, clust), flag_ref[0], jnp.int32)
    rest_ref[rows + rows // ROW_TILE * K * TOPK :, :] = flags.astype(jnp.float32).astype(jnp.bfloat16)


def join(flag, embeddings, indicators, columns):
    rows, width = embeddings.shape
    clust = indicators.shape[1]
    by_row = lambda cols: pl.BlockSpec((ROW_TILE, cols), lambda r, flag: (r, 0))
    steps = rows // ROW_TILE
    rest = (rows + steps * K * TOPK + FLAG_ROWS, clust)
    return pl.pallas_call(
        join_kernel,
        out_shape=[
            jax.ShapeDtypeStruct(shape, jnp.bfloat16)
            for shape in ((rows, width + clust + 2 * K * TOPK), (rows, width), rest)
        ],
        grid_spec=pltpu.PrefetchScalarGridSpec(
            num_scalar_prefetch=1,
            grid=(steps,),
            in_specs=[
                by_row(width),
                by_row(clust),
                pl.BlockSpec((K, TOPK, ROW_TILE), lambda r, flag: (0, 0, r)),
            ],
            out_specs=[by_row(width + clust + 2 * K * TOPK), by_row(width), pl.BlockSpec(rest, lambda r, flag: (0, 0))],
        ),
        compiler_params=pltpu.CompilerParams(vmem_limit_bytes=VMEM_LIMIT),
        name="join",
    )(flag, embeddings, indicators, jnp.transpose(columns, (1, 2, 0)))


def words_kernel(pick_ref, coded_ref, out_ref):
    lane = lax.broadcasted_iota(jnp.int32, (LANES, LANES), 0)
    for step in range(coded_ref.shape[1] // (K * TOPK)):
        coded = coded_ref[0, step * K * TOPK : (step + 1) * K * TOPK].astype(jnp.float32).astype(jnp.int32)
        high = sum((coded >= LANES << m).astype(jnp.int32) for m in range(1, 8))
        low = jnp.right_shift(coded, high) & (LANES - 1)
        bit = jnp.left_shift(jnp.ones_like(high), high)
        for part in range(ROW_TILE // LANES):
            here = slice(part * LANES, (part + 1) * LANES)
            for slot in range(K):
                word = jnp.zeros((LANES, LANES), jnp.int32)
                for t in range(slot * TOPK, (slot + 1) * TOPK):
                    word = word | jnp.where(lane == low[t : t + 1, here], bit[t : t + 1, here], 0)
                start = step * ROW_TILE + part * LANES
                out_ref[slot, start : start + LANES, :] = word.T


def keep_words(pick, rest, which, rows):
    part = rows // ROW_TILE * K * TOPK
    clust = rest.shape[2]
    return pl.pallas_call(
        words_kernel,
        out_shape=jax.ShapeDtypeStruct((K, rows, LANES), jnp.int32),
        grid_spec=pltpu.PrefetchScalarGridSpec(
            num_scalar_prefetch=1,
            grid=(1,),
            in_specs=[pl.BlockSpec((1, part, clust), lambda i, pick: (which(pick), rows // part, 0))],
            out_specs=pl.BlockSpec((K, rows, LANES), lambda i, pick: (0, 0, 0)),
        ),
        compiler_params=pltpu.CompilerParams(vmem_limit_bytes=VMEM_LIMIT),
        cost_estimate=pl.CostEstimate(flops=rows * LANES * K * TOPK, bytes_accessed=rows * 512, transcendentals=0),
        name="keep_words",
    )(pick, rest)


def mix(acc, degree, anchor):
    return (ALPHA * acc / degree + (1.0 - ALPHA) * anchor.astype(jnp.float32)).astype(jnp.bfloat16)


def weights(cosine, word, total, put):
    for j in range(cosine.shape[1] // LANES):
        part = cosine[:, j * LANES : (j + 1) * LANES]
        raw = jnp.where((word & (1 << j)) != 0, jnp.exp2(part * SCALE - SCALE), 0.0)
        total = total + raw
        put(slice(j * LANES, (j + 1) * LANES), raw.astype(jnp.bfloat16))
    return total


def cosines(rows, others):
    return lax.dot_general(rows, others, (((1,), (1,)), ((), ())), preferred_element_type=jnp.float32)


def flat(ref):
    value = ref[...]
    return value.reshape(-1, value.shape[-1])


def tile_kernel(has_carry, last, pick_ref, x_ref, other_ref, w_ref, y_ref, *refs):
    refs = list(refs)
    deg_in, acc_in = (refs.pop(0), refs.pop(0)) if has_carry else (None, None)
    anchor_ref = refs.pop(0) if last else None
    deg_ref, acc_ref, tile_ref = refs
    word = w_ref[0]
    total = deg_in[...] if has_carry else jnp.zeros(word.shape, jnp.float32)

    def put(lanes, value):
        tile_ref[:, lanes] = value

    total = weights(cosines(x_ref[...], flat(other_ref)), word, total, put)
    deg_ref[...] = total
    gathered = jnp.dot(tile_ref[...], flat(y_ref), preferred_element_type=jnp.float32)
    if has_carry:
        gathered = acc_in[...] + gathered
    if last:
        gathered = mix(gathered, jnp.sum(total, axis=1, keepdims=True), anchor_ref[...])
    acc_ref[...] = gathered


def tile_of(pick, x, other, y, words, slot, carry=None, anchor=None, keep=True):
    rows, clust = words.shape[1], y[1][-1]
    by_row = lambda cols: pl.BlockSpec((ROW_TILE, cols), lambda r, pick: (r, 0))
    spec = lambda operand: pl.BlockSpec(operand[1], operand[2])
    last = anchor is not None
    args = [x[0], other[0], words, y[0], *(carry or ())] + ([anchor[0]] if last else [])
    specs = [spec(x), spec(other), pl.BlockSpec((1, ROW_TILE, LANES), lambda r, pick: (slot(pick), r, 0)), spec(y)]
    specs += ([by_row(LANES), by_row(clust)] if carry else []) + ([spec(anchor)] if last else [])
    outs = [(LANES, jnp.float32), (clust, jnp.bfloat16 if last else jnp.float32)] + [(rows, jnp.bfloat16)] * keep
    return pl.pallas_call(
        functools.partial(tile_kernel, carry is not None, last),
        out_shape=[jax.ShapeDtypeStruct((rows, cols), kind) for cols, kind in outs],
        grid_spec=pltpu.PrefetchScalarGridSpec(
            num_scalar_prefetch=1,
            grid=(rows // ROW_TILE,),
            in_specs=specs,
            out_specs=[by_row(cols) for cols, _ in outs],
            scratch_shapes=[] if keep else [pltpu.VMEM((ROW_TILE, rows), jnp.bfloat16)],
        ),
        compiler_params=pltpu.CompilerParams(vmem_limit_bytes=VMEM_LIMIT),
        cost_estimate=pl.CostEstimate(flops=rows * clust, bytes_accessed=rows * clust, transcendentals=0),
        name="tile",
    )(pick, *args)


def member_kernel(width, pick_ref, *refs):
    blocks, refs = refs[:BLOCKS_NEAR], refs[BLOCKS_NEAR:]
    (rows_ref, rest1_ref, rest2_ref, near_ref, far_ref, w_ref, words_ref, deg_in, acc_in, anchor_ref) = refs[:10]
    tile_ref, deg_ref, new_ref, other_ref, x1_ref, x2_ref, held_ref, sems = refs[10:]
    step = pl.program_id(0)

    @pl.when(step == 0)
    def _():
        for which, target in enumerate((x1_ref, x2_ref)):
            for i, block in enumerate(blocks):

                @pl.when(pick_ref[1 + which] == i)
                def _():
                    copy = pltpu.make_async_copy(block, target, sems.at[which])
                    copy.start()
                    copy.wait()

    def put_to(ref):
        def put(lanes, value):
            ref[:, lanes] = value

        return put

    total = weights(cosines(rows_ref[...], x1_ref[...]), w_ref[0], deg_in[...], put_to(tile_ref))
    deg_ref[...] = total
    gathered = acc_in[...] + jnp.dot(tile_ref[...], rest1_ref[0], preferred_element_type=jnp.float32)
    new_ref[...] = mix(gathered, jnp.sum(total, axis=1, keepdims=True), anchor_ref[...])

    here = pl.ds(pl.multiple_of(step * ROW_TILE, ROW_TILE), ROW_TILE)
    x = x1_ref[here, :]
    near, far = near_ref[:, 0].reshape(-1, near_ref.shape[3]), flat(far_ref)
    total = jnp.zeros(deg_in.shape, jnp.float32)
    acc = jnp.zeros(acc_in.shape, jnp.float32)
    slots = (0, 1, pick_ref[3], 5 - pick_ref[3])
    others = ((x1_ref[...], rest1_ref[0]), (x2_ref[...], rest2_ref[0]))
    others += tuple((block[:, :width], block[:, width:]) for block in (near, far))
    for slot, (other, y) in zip(slots, others):
        total = weights(cosines(x, other), words_ref[slot], total, put_to(held_ref))
        acc = acc + jnp.dot(held_ref[...], y, preferred_element_type=jnp.float32)
    anchor = rest1_ref[0, here, :]
    other_ref[...] = mix(acc, jnp.sum(total, axis=1, keepdims=True), anchor)


def member_of(pick, blocks, own_rows, rest, near, far, words, member_words, carry, anchor):
    rows, width = blocks[0].shape
    clust = rest.shape[2]
    chips, _, piece, full = near.shape
    once = pl.Buffered(1)
    by_row = lambda cols: pl.BlockSpec((ROW_TILE, cols), lambda r, pick: (r, 0))
    rest_at = lambda k: pl.BlockSpec((1, rows, clust), lambda r, pick: (pick[k], 0, 0), pipeline_mode=once)
    return pl.pallas_call(
        functools.partial(member_kernel, width),
        out_shape=[
            jax.ShapeDtypeStruct((rows, rows), jnp.bfloat16),
            jax.ShapeDtypeStruct((rows, LANES), jnp.float32),
            jax.ShapeDtypeStruct((rows, clust), jnp.bfloat16),
            jax.ShapeDtypeStruct((rows, clust), jnp.bfloat16),
        ],
        grid_spec=pltpu.PrefetchScalarGridSpec(
            num_scalar_prefetch=1,
            grid=(rows // ROW_TILE,),
            in_specs=[pl.BlockSpec(memory_space=pl.ANY)] * len(blocks)
            + [
                by_row(width),
                rest_at(4),
                rest_at(5),
                pl.BlockSpec((chips, 1, piece, full), lambda r, pick: (0, 0, 0, 0), pipeline_mode=once),
                pl.BlockSpec((chips, piece, full), lambda r, pick: (0, 0, 0), pipeline_mode=once),
                pl.BlockSpec((1, ROW_TILE, LANES), lambda r, pick: (1, r, 0)),
                pl.BlockSpec((K, ROW_TILE, LANES), lambda r, pick: (0, r, 0)),
                by_row(LANES),
                by_row(clust),
                by_row(clust),
            ],
            out_specs=[by_row(rows), by_row(LANES), by_row(clust), by_row(clust)],
            scratch_shapes=[
                pltpu.VMEM((rows, width), jnp.bfloat16),
                pltpu.VMEM((rows, width), jnp.bfloat16),
                pltpu.VMEM((ROW_TILE, rows), jnp.bfloat16),
                pltpu.SemaphoreType.DMA((2,)),
            ],
        ),
        compiler_params=pltpu.CompilerParams(vmem_limit_bytes=VMEM_LIMIT),
        cost_estimate=pl.CostEstimate(
            flops=10 * rows * rows * 768, bytes_accessed=8 * rows * rows, transcendentals=5 * rows * rows
        ),
        name="member",
    )(pick, *blocks, own_rows, rest, rest, near, far, words, member_words, *carry, anchor)


def pair_kernel(last, first_ref, second_ref, y1_ref, y2_ref, *refs):
    acc = jnp.dot(first_ref[...], y1_ref[...], preferred_element_type=jnp.float32)
    acc = acc + jnp.dot(second_ref[...], y2_ref[...], preferred_element_type=jnp.float32)
    if last:
        acc_in, deg_ref, anchor_ref = refs[:3]
        acc = mix(acc + acc_in[...], jnp.sum(deg_ref[...], axis=1, keepdims=True), anchor_ref[...])
    refs[-1][...] = acc


def pair_of(tiles, news, finish=None):
    rows, clust = news[0].shape
    by_row = lambda cols: pl.BlockSpec((ROW_TILE, cols), lambda r: (r, 0))
    return pl.pallas_call(
        functools.partial(pair_kernel, finish is not None),
        out_shape=jax.ShapeDtypeStruct((rows, clust), jnp.bfloat16 if finish else jnp.float32),
        grid=(rows // ROW_TILE,),
        in_specs=[by_row(rows)] * 2
        + [pl.BlockSpec((rows, clust), lambda r: (0, 0))] * 2
        + ([by_row(clust), by_row(LANES), by_row(clust)] if finish else []),
        out_specs=by_row(clust),
        compiler_params=pltpu.CompilerParams(vmem_limit_bytes=VMEM_LIMIT),
        cost_estimate=pl.CostEstimate(flops=rows * clust, bytes_accessed=rows * clust, transcendentals=0),
        name="pair",
    )(*tiles, *news, *(finish or ()))


def hub_rows_kernel(width, pick_ref, rows_ref, near_ref, far_ref, out_ref, word_ref, tile_ref):
    clust = out_ref.shape[1]
    half = K * TOPK
    coded = rows_ref[:, width + clust :].astype(jnp.float32).astype(jnp.int32)
    high = coded[:, :half] & (HALF - 1)
    low = (high & 3) * HALF + coded[:, half:]
    bit = jnp.left_shift(jnp.ones_like(high), high >> 2)
    lane = lax.broadcasted_iota(jnp.int32, (rows_ref.shape[0], LANES), 1)
    for slot in range(K):
        word = jnp.zeros(lane.shape, jnp.int32)
        for t in range(slot * TOPK, (slot + 1) * TOPK):
            word = word | jnp.where(lane == low[:, t : t + 1], bit[:, t : t + 1], 0)
        word_ref[slot] = word
    total = jnp.zeros(lane.shape, jnp.float32)
    acc = jnp.zeros(out_ref.shape, jnp.float32)

    def put(lanes, value):
        tile_ref[:, lanes] = value

    self_block = near_ref[:, 0].reshape(-1, width + clust)
    member_block = near_ref[:, 1].reshape(-1, width + clust)
    far_block = flat(far_ref)
    slots = (0, 1, pick_ref[0], 5 - pick_ref[0])
    for slot, block in zip(slots, (self_block, member_block, self_block, far_block)):
        total = weights(cosines(rows_ref[:, :width], block[:, :width]), word_ref[slot], total, put)
        acc = acc + jnp.dot(tile_ref[...], block[:, width:], preferred_element_type=jnp.float32)
    out_ref[...] = mix(acc, jnp.sum(total, axis=1, keepdims=True), rows_ref[:, width : width + clust])


def hub_rows(self_slot, mine, near, far, width):
    share = mine.shape[0]
    clust = near.shape[3] - width
    rows = near.shape[0] * near.shape[2]
    return pl.pallas_call(
        functools.partial(hub_rows_kernel, width),
        out_shape=jax.ShapeDtypeStruct((share, clust), jnp.bfloat16),
        grid_spec=pltpu.PrefetchScalarGridSpec(
            num_scalar_prefetch=1,
            grid=(1,),
            in_specs=[
                pl.BlockSpec(mine.shape, lambda i, pick: (0, 0)),
                pl.BlockSpec(near.shape, lambda i, pick: (0, 0, 0, 0)),
                pl.BlockSpec(far.shape, lambda i, pick: (0, 0, 0)),
            ],
            out_specs=pl.BlockSpec((share, clust), lambda i, pick: (0, 0)),
            scratch_shapes=[pltpu.VMEM((K, share, LANES), jnp.int32), pltpu.VMEM((share, rows), jnp.bfloat16)],
        ),
        compiler_params=pltpu.CompilerParams(vmem_limit_bytes=VMEM_LIMIT),
        cost_estimate=pl.CostEstimate(flops=rows, bytes_accessed=rows, transcendentals=0),
        name="hub_rows",
    )(self_slot, mine, near, far)


def send(block, target):
    slabs, reps = lax.axis_size("slab"), lax.axis_size("rep")
    chips = slabs // 4
    pairs = []
    for device in range(slabs * reps):
        slab, rep = divmod(device, reps)
        to = target(slab // (2 * chips), slab // 2 % chips, slab % 2, rep)
        if to is not None:
            pairs.append((device, ((to[0] * chips + to[1]) * 2 + to[2]) * reps + to[3]))
    return lax.ppermute(block, AXES, pairs)


def along_line(block, table):
    return send(
        block, lambda half, chip, core, rep: (half, chip, core, table[rep]) if rep in table else None
    )


def swap_cores(block):
    return send(block, lambda half, chip, core, rep: (half, chip, 1 - core, rep))


def flags_of(code):
    flag = code.astype(jnp.float32).astype(jnp.int32) // HALF
    return flag & 3, (flag >> 2) & 1


def join_pieces(piece):
    slabs = lax.axis_size("slab")
    members, chips = slabs // 2, slabs // 4
    layers = [[h * members + c * 2 + core for c in range(chips)] for h in range(2) for core in range(2)]
    repeated = jnp.broadcast_to(piece[None], (chips,) + piece.shape)
    return lax.all_to_all(repeated, "slab", 0, 0, axis_index_groups=layers, tiled=True)


OUTWARD = {1: 0, 2: 3}
MIDDLE = {1: 2, 2: 1}


def spread_line(block):
    across = along_line(block, {0: 2, 2: 0, 1: 3, 3: 1})
    beside = along_line(block, {0: 1, 1: 0, 2: 3, 3: 2})
    return across, beside


def scatter(block):
    members = lax.axis_size("slab") // 2
    rows, width = block.shape
    planes = [[h * members + m for m in range(members)] for h in range(2)]
    return lax.all_to_all(
        block.reshape(members, rows // members, width), "slab", 0, 0, axis_index_groups=planes, tiled=True
    )


def hub_pieces(mine, hub_ids, code_at):
    members, reps = lax.axis_size("slab") // 2, lax.axis_size("rep")
    slab = lax.axis_index("slab")
    hub_slab, hub_rep = lax.div(hub_ids, reps), lax.rem(hub_ids, reps)
    member = lax.rem(hub_slab, members)
    held = jnp.stack(
        [lax.dynamic_index_in_dim(mine, member[h], 0, keepdims=False) for h in range(HUBS)], axis=0
    )
    got = send(held, lambda half, chip, core, rep: (1 - half, chip, core, rep))
    away = lax.div(hub_slab, members) != lax.div(slab, members)
    held = jnp.where(away[:, None, None], got, held)[None]
    rep = lax.axis_index("rep")
    for bit in range(2):
        got = along_line(held, {r: r ^ (1 << bit) for r in range(4)})
        upper = (rep >> bit) & 1 == 1
        held = jnp.concatenate([jnp.where(upper, got, held), jnp.where(upper, held, got)], axis=0)
    pick = lambda pieces, at: jnp.where(
        at < 2, jnp.where(at == 0, pieces[0], pieces[1]), jnp.where(at == 2, pieces[2], pieces[3])
    )
    chosen = []
    for h in range(HUBS):
        hub = pick(held[:, h], hub_rep[h])
        want, _ = flags_of(hub[:1, code_at : code_at + 1])
        chosen.append(jnp.stack([hub, pick(held[:, h], want)], axis=0))
    held = jnp.stack(chosen, axis=0)
    first_core = lax.rem(slab, 2) == 0
    keep = jnp.where(first_core, held[0], held[1])
    got = swap_cores(jnp.where(first_core, held[1], held[0]))
    return jnp.concatenate([jnp.where(first_core, keep, got), jnp.where(first_core, got, keep)], axis=1)


def body(embeddings, indicators, neighbours, hub_ids, columns):
    rows, width = embeddings.shape
    clust = indicators.shape[1]
    full = width + clust
    reps = lax.axis_size("rep")
    total = lax.axis_size("slab") * reps
    rep = lax.axis_index("rep")
    steps = rows // ROW_TILE
    slots = neighbours[0].astype(jnp.int32)
    want = slots[1] & 3
    order = slots[2] - total
    core = lax.rem(lax.axis_index("slab"), 2)
    near_slot = jnp.where(order == core, 2, 3)
    barrier = lax.optimization_barrier

    joined, normed, rest = join((want + 4 * order)[None], embeddings, indicators, columns)
    across, beside = spread_line(rest)

    pick = jnp.stack([near_slot]).astype(jnp.int32)
    own_rows = (joined, (ROW_TILE, width), lambda r, pick: (r, 0))
    own_x = (joined, (rows, width), lambda r, pick: (0, 0))
    own_y = (joined, (rows, clust), lambda r, pick: (0, width // clust))
    words = keep_words(pick, rest[None], lambda pick: 0, rows)
    *carry, own_tile = tile_of(pick, own_rows, own_x, own_y, words, lambda pick: 0)
    mine, words, carry, own_tile, rest, across, beside = barrier(
        (scatter(joined), words, carry, own_tile, rest, across, beside)
    )

    both = hub_pieces(mine, hub_ids, full)
    both, normed, rest, across = barrier((both, normed, rest, across))

    outer, middle = along_line(across, OUTWARD), along_line(rest, MIDDLE)
    across_x, beside_x = spread_line(normed)
    near = join_pieces(both[:, :, :full])
    at_end = (rep == 0) | (rep == 3)
    group_rest = jnp.stack([rest, beside, across, jnp.where(at_end, outer, middle)], axis=0)
    at = want ^ rep
    flag = lax.dynamic_index_in_dim(group_rest[:, -1, 0], at, 0, keepdims=False).astype(jnp.int32)
    member_want, member_order = flag & 3, (flag >> 2) & 1
    second = member_want ^ rep
    place = lambda k: jnp.where((k == 3) & at_end, 4, k)
    pick = jnp.stack(
        [near_slot, place(at), place(second), jnp.where(member_order == core, 2, 3), at, second]
    ).astype(jnp.int32)
    member_words = keep_words(pick, group_rest, lambda pick: pick[4], rows)
    near, normed, across_x, beside_x, group_rest, member_words = barrier(
        (near, normed, across_x, beside_x, group_rest, member_words)
    )

    outer_x, middle_x = along_line(across_x, OUTWARD), along_line(normed, MIDDLE)
    chips, _, piece, _ = near.shape
    near_x = (near, (chips, 1, piece, width), lambda r, pick: (0, 0, 0, 0))
    near_y = (near, (chips, 1, piece, clust), lambda r, pick: (0, 0, 0, width // clust))
    far = swap_cores(near[:, 0])
    *carry, near_tile = tile_of(pick, own_rows, near_x, near_y, words, lambda pick: pick[0], carry)
    far, carry = barrier((far, carry))
    _, hub_order = flags_of(both[0, 0, full])
    share = hub_rows(jnp.where(hub_order == core, 2, 3)[None], both[0], near, far, width)
    near_new = join_pieces(share).reshape(rows, clust)
    far_x = (far, (chips, piece, width), lambda r, pick: (0, 0, 0))
    far_y = (far, (chips, piece, clust), lambda r, pick: (0, 0, width // clust))
    *carry, far_tile = tile_of(pick, own_rows, far_x, far_y, words, lambda pick: 5 - pick[0], carry)
    near_new, carry = barrier((near_new, carry))
    far_new = swap_cores(near_new)
    acc = pair_of((near_tile, far_tile), (near_new, far_new))
    acc, middle_x, outer_x = barrier((acc, middle_x, outer_x))

    member_tile, degree, new, member_new = member_of(
        pick, (normed, beside_x, across_x, middle_x, outer_x), normed, group_rest, near, far, words, member_words,
        carry, indicators,
    )
    return pair_of((own_tile, member_tile), (new, member_new), (acc, degree, indicators))


def solution(mesh):
    return jax.shard_map(
        body,
        mesh=mesh,
        in_specs=(
            P(("slab", "rep"), None),
            P(("slab", "rep"), None),
            P(("slab", "rep"), None),
            P(),
            P(("slab", "rep"), None, None),
        ),
        out_specs=P(("slab", "rep"), None),
        check_vma=False,
    )
```

```python
import functools

import jax
import jax.numpy as jnp
from jax import lax
from jax.experimental import pallas as pl
from jax.experimental.pallas import tpu as pltpu
from jax.sharding import PartitionSpec as P

K = 4
HUBS = 2
TOPK = 16
LANES = 128
EPS = 1e-06
TAU = 0.04
ALPHA = 0.8
AXES = ("slab", "rep")
ROW_TILE = 256
VMEM_LIMIT = 58 << 20
SCALE = 1.4426950408889634 / TAU
HALF = 32
FLAG_ROWS = 16
BLOCKS_NEAR = 5
WORDS_HINT = 30_000_000_000


def join_kernel(blocks, near_ref, x_ref, y_ref, cols_ref, all_ref, normed_ref, rest_ref):
    width, clust = x_ref.shape[1], y_ref.shape[1]
    step = pl.program_id(0)
    rows = pl.num_programs(0) * ROW_TILE
    values = x_ref[...].astype(jnp.float32)
    scale = lax.rsqrt(jnp.sum(values * values, axis=1, keepdims=True) + EPS)
    normed = (values * scale).astype(jnp.bfloat16)
    cols = cols_ref[...].reshape(K * TOPK, cols_ref.shape[2])
    flag = (near_ref[1] & 3) + 4 * (near_ref[2] - blocks)
    coded = jnp.concatenate([(cols >> 5) + HALF * flag, cols & (HALF - 1)], axis=0)
    all_ref[:, :width] = normed
    all_ref[:, width : width + clust] = y_ref[...]
    all_ref[:, width + clust :] = coded.astype(jnp.float32).T.astype(jnp.bfloat16)
    normed_ref[...] = normed
    rest_ref[pl.ds(pl.multiple_of(step * ROW_TILE, ROW_TILE), ROW_TILE), :] = y_ref[...]
    single = jnp.left_shift((cols & (LANES - 1)) + LANES, cols >> 7)
    place = pl.multiple_of(rows + step * K * TOPK, K * TOPK)
    rest_ref[pl.ds(place, K * TOPK), :] = single.astype(jnp.float32).astype(jnp.bfloat16)
    flags = jnp.full((FLAG_ROWS, clust), flag, jnp.int32)
    rest_ref[rows + rows // ROW_TILE * K * TOPK :, :] = flags.astype(jnp.float32).astype(jnp.bfloat16)


def join(blocks, near, embeddings, indicators, columns):
    rows, width = embeddings.shape
    clust = indicators.shape[1]
    by_row = lambda cols: pl.BlockSpec((ROW_TILE, cols), lambda r, flag: (r, 0))
    steps = rows // ROW_TILE
    rest = (rows + steps * K * TOPK + FLAG_ROWS, clust)
    return pl.pallas_call(
        functools.partial(join_kernel, blocks),
        out_shape=[
            jax.ShapeDtypeStruct(shape, jnp.bfloat16)
            for shape in ((rows, width + clust + 2 * K * TOPK), (rows, width), rest)
        ],
        grid_spec=pltpu.PrefetchScalarGridSpec(
            num_scalar_prefetch=1,
            grid=(steps,),
            in_specs=[
                by_row(width),
                by_row(clust),
                pl.BlockSpec((K, TOPK, ROW_TILE), lambda r, flag: (0, 0, r)),
            ],
            out_specs=[by_row(width + clust + 2 * K * TOPK), by_row(width), pl.BlockSpec(rest, lambda r, flag: (0, 0))],
        ),
        compiler_params=pltpu.CompilerParams(vmem_limit_bytes=VMEM_LIMIT),
        name="join",
    )(near, embeddings, indicators, jnp.transpose(columns, (1, 2, 0)))


def words_kernel(pick_ref, coded_ref, out_ref):
    lane = lax.broadcasted_iota(jnp.int32, (LANES, LANES), 0)
    for step in range(coded_ref.shape[1] // (K * TOPK)):
        coded = coded_ref[0, step * K * TOPK : (step + 1) * K * TOPK].astype(jnp.float32).astype(jnp.int32)
        high = sum((coded >= LANES << m).astype(jnp.int32) for m in range(1, 8))
        low = jnp.right_shift(coded, high) & (LANES - 1)
        bit = jnp.left_shift(jnp.ones_like(high), high)
        for part in range(ROW_TILE // LANES):
            here = slice(part * LANES, (part + 1) * LANES)
            for slot in range(K):
                word = jnp.zeros((LANES, LANES), jnp.int32)
                for t in range(slot * TOPK, (slot + 1) * TOPK):
                    word = word | jnp.where(lane == low[t : t + 1, here], bit[t : t + 1, here], 0)
                start = step * ROW_TILE + part * LANES
                out_ref[slot, start : start + LANES, :] = word.T


def keep_words(pick, rest, which, rows, hint):
    part = rows // ROW_TILE * K * TOPK
    clust = rest.shape[2]
    return pl.pallas_call(
        words_kernel,
        out_shape=jax.ShapeDtypeStruct((K, rows, LANES), jnp.int32),
        grid_spec=pltpu.PrefetchScalarGridSpec(
            num_scalar_prefetch=1,
            grid=(1,),
            in_specs=[pl.BlockSpec((1, part, clust), lambda i, pick: (which(pick), rows // part, 0))],
            out_specs=pl.BlockSpec((K, rows, LANES), lambda i, pick: (0, 0, 0)),
        ),
        compiler_params=pltpu.CompilerParams(vmem_limit_bytes=VMEM_LIMIT),
        cost_estimate=pl.CostEstimate(flops=hint, bytes_accessed=rows * 512, transcendentals=0),
        name="keep_words",
    )(pick, rest)


def mix(acc, degree, anchor):
    return (ALPHA * acc / degree + (1.0 - ALPHA) * anchor.astype(jnp.float32)).astype(jnp.bfloat16)


def weights(cosine, word, total, put):
    for j in range(cosine.shape[1] // LANES):
        part = cosine[:, j * LANES : (j + 1) * LANES]
        raw = jnp.where((word & (1 << j)) != 0, jnp.exp2(part * SCALE - SCALE), 0.0)
        total = total + raw
        put(slice(j * LANES, (j + 1) * LANES), raw.astype(jnp.bfloat16))
    return total


def cosines(rows, others):
    return lax.dot_general(rows, others, (((1,), (1,)), ((), ())), preferred_element_type=jnp.float32)


def flat(ref):
    value = ref[...]
    return value.reshape(-1, value.shape[-1])


def tile_kernel(has_carry, last, pick_ref, x_ref, other_ref, w_ref, y_ref, *refs):
    refs = list(refs)
    deg_in, acc_in = (refs.pop(0), refs.pop(0)) if has_carry else (None, None)
    anchor_ref = refs.pop(0) if last else None
    deg_ref, acc_ref, tile_ref = refs
    word = w_ref[0]
    total = deg_in[...] if has_carry else jnp.zeros(word.shape, jnp.float32)

    def put(lanes, value):
        tile_ref[:, lanes] = value

    total = weights(cosines(x_ref[...], flat(other_ref)), word, total, put)
    deg_ref[...] = total
    gathered = jnp.dot(tile_ref[...], flat(y_ref), preferred_element_type=jnp.float32)
    if has_carry:
        gathered = acc_in[...] + gathered
    if last:
        gathered = mix(gathered, jnp.sum(total, axis=1, keepdims=True), anchor_ref[...])
    acc_ref[...] = gathered


def tile_of(pick, x, other, y, words, slot, carry=None, anchor=None, keep=True):
    rows, clust = words.shape[1], y[1][-1]
    by_row = lambda cols: pl.BlockSpec((ROW_TILE, cols), lambda r, pick: (r, 0))
    spec = lambda operand: pl.BlockSpec(operand[1], operand[2])
    last = anchor is not None
    args = [x[0], other[0], words, y[0], *(carry or ())] + ([anchor[0]] if last else [])
    specs = [spec(x), spec(other), pl.BlockSpec((1, ROW_TILE, LANES), lambda r, pick: (slot(pick), r, 0)), spec(y)]
    specs += ([by_row(LANES), by_row(clust)] if carry else []) + ([spec(anchor)] if last else [])
    outs = [(LANES, jnp.float32), (clust, jnp.bfloat16 if last else jnp.float32)] + [(rows, jnp.bfloat16)] * keep
    return pl.pallas_call(
        functools.partial(tile_kernel, carry is not None, last),
        out_shape=[jax.ShapeDtypeStruct((rows, cols), kind) for cols, kind in outs],
        grid_spec=pltpu.PrefetchScalarGridSpec(
            num_scalar_prefetch=1,
            grid=(rows // ROW_TILE,),
            in_specs=specs,
            out_specs=[by_row(cols) for cols, _ in outs],
            scratch_shapes=[] if keep else [pltpu.VMEM((ROW_TILE, rows), jnp.bfloat16)],
        ),
        compiler_params=pltpu.CompilerParams(vmem_limit_bytes=VMEM_LIMIT),
        cost_estimate=pl.CostEstimate(flops=rows * clust, bytes_accessed=rows * clust, transcendentals=0),
        name="tile",
    )(pick, *args)


def seven_kernel(pick_ref, *refs):
    blocks, refs = refs[:BLOCKS_NEAR], refs[BLOCKS_NEAR:]
    rows_ref, first_y, second_y, near_ref, far_ref, words_ref, member_ref, deg_in, acc_in, anchor_ref = refs[:10]
    near_tile, far_tile, member_tile, deg_ref, new_ref, other_ref, first_x, second_x, held, spare, sems = refs[10:]
    width = rows_ref.shape[1]
    step = pl.program_id(0)

    @pl.when(step == 0)
    def _():
        for which, target in enumerate((first_x, second_x)):
            for i, block in enumerate(blocks):

                @pl.when(pick_ref[1 + which] == i)
                def _():
                    copy = pltpu.make_async_copy(block, target, sems.at[which])
                    copy.start()
                    copy.wait()

    def put_to(ref):
        def put(lanes, value):
            ref[:, lanes] = value

        return put

    def run(rows, plan, total, acc):
        for word, (other, y), tile in plan:
            total = weights(cosines(rows, other), word, total, put_to(tile))
            acc = acc + jnp.dot(tile[...], y, preferred_element_type=jnp.float32)
        return total, acc

    split = lambda block: (block[:, :width], block[:, width:])
    first, second = (first_x[...], first_y[0]), (second_x[...], second_y[0])
    near, far = split(near_ref[:, 0].reshape(-1, near_ref.shape[3])), split(flat(far_ref))
    plan = (
        (words_ref[pick_ref[0]], near, near_tile),
        (words_ref[5 - pick_ref[0]], far, far_tile),
        (words_ref[1], first, member_tile),
    )
    total, acc = run(rows_ref[...], plan, deg_in[...], acc_in[...])
    deg_ref[...] = total
    new_ref[...] = mix(acc, jnp.sum(total, axis=1, keepdims=True), anchor_ref[...])
    here = pl.ds(pl.multiple_of(step * ROW_TILE, ROW_TILE), ROW_TILE)
    plan = (
        (member_ref[pick_ref[3]], near, held),
        (member_ref[5 - pick_ref[3]], far, spare),
        (member_ref[0], first, held),
        (member_ref[1], second, spare),
    )
    total, acc = run(first_x[here, :], plan, jnp.zeros(deg_in.shape, jnp.float32), jnp.zeros(acc_in.shape, jnp.float32))
    other_ref[...] = mix(acc, jnp.sum(total, axis=1, keepdims=True), first_y[0, here, :])


def seven_of(pick, blocks, own_rows, rest, near, far, words, member_words, carry, anchor):
    rows, width = blocks[0].shape
    clust = rest.shape[2]
    chips, _, piece, full = near.shape
    once = pl.Buffered(1)
    by_row = lambda cols: pl.BlockSpec((ROW_TILE, cols), lambda r, pick: (r, 0))
    rest_at = lambda k: pl.BlockSpec((1, rows, clust), lambda r, pick: (pick[k], 0, 0), pipeline_mode=once)
    by_word = pl.BlockSpec((K, ROW_TILE, LANES), lambda r, pick: (0, r, 0))
    outs = [(rows, jnp.bfloat16)] * 3 + [(LANES, jnp.float32)] + [(clust, jnp.bfloat16)] * 2
    return pl.pallas_call(
        seven_kernel,
        out_shape=[jax.ShapeDtypeStruct((rows, cols), kind) for cols, kind in outs],
        grid_spec=pltpu.PrefetchScalarGridSpec(
            num_scalar_prefetch=1,
            grid=(rows // ROW_TILE,),
            in_specs=[pl.BlockSpec(memory_space=pl.ANY)] * len(blocks)
            + [
                by_row(width),
                rest_at(4),
                rest_at(5),
                pl.BlockSpec((chips, 1, piece, full), lambda r, pick: (0, 0, 0, 0), pipeline_mode=once),
                pl.BlockSpec((chips, piece, full), lambda r, pick: (0, 0, 0), pipeline_mode=once),
                by_word,
                by_word,
                by_row(LANES),
                by_row(clust),
                by_row(clust),
            ],
            out_specs=[by_row(cols) for cols, _ in outs],
            scratch_shapes=[pltpu.VMEM((rows, width), jnp.bfloat16)] * 2
            + [pltpu.VMEM((ROW_TILE, rows), jnp.bfloat16)] * 2
            + [pltpu.SemaphoreType.DMA((2,))],
        ),
        compiler_params=pltpu.CompilerParams(vmem_limit_bytes=VMEM_LIMIT),
        cost_estimate=pl.CostEstimate(
            flops=14 * rows * rows * full, bytes_accessed=16 * rows * rows, transcendentals=7 * rows * rows
        ),
        name="seven",
    )(pick, *blocks, own_rows, rest, rest, near, far, words, member_words, *carry, anchor)


def last_kernel(*refs):
    tiles, news, (deg_ref, anchor_ref, out_ref) = refs[:K], refs[K : 2 * K], refs[2 * K :]
    acc = sum(jnp.dot(t[...], y[...], preferred_element_type=jnp.float32) for t, y in zip(tiles, news))
    out_ref[...] = mix(acc, jnp.sum(deg_ref[...], axis=1, keepdims=True), anchor_ref[...])


def last_of(tiles, news, degree, anchor):
    rows, clust = anchor.shape
    by_row = lambda cols: pl.BlockSpec((ROW_TILE, cols), lambda r: (r, 0))
    return pl.pallas_call(
        last_kernel,
        out_shape=jax.ShapeDtypeStruct((rows, clust), jnp.bfloat16),
        grid=(rows // ROW_TILE,),
        in_specs=[by_row(rows)] * K
        + [pl.BlockSpec((rows, clust), lambda r: (0, 0))] * K
        + [by_row(LANES), by_row(clust)],
        out_specs=by_row(clust),
        compiler_params=pltpu.CompilerParams(vmem_limit_bytes=VMEM_LIMIT),
        cost_estimate=pl.CostEstimate(flops=8 * rows * rows * clust, bytes_accessed=8 * rows * rows, transcendentals=0),
        name="last",
    )(*tiles, *news, degree, anchor)


def hub_rows_kernel(width, pick_ref, rows_ref, near_ref, far_ref, out_ref, word_ref, tile_ref):
    clust = out_ref.shape[1]
    half = K * TOPK
    coded = rows_ref[:, width + clust :].astype(jnp.float32).astype(jnp.int32)
    high = coded[:, :half] & (HALF - 1)
    low = (high & 3) * HALF + coded[:, half:]
    bit = jnp.left_shift(jnp.ones_like(high), high >> 2)
    lane = lax.broadcasted_iota(jnp.int32, (rows_ref.shape[0], LANES), 1)
    for slot in range(K):
        word = jnp.zeros(lane.shape, jnp.int32)
        for t in range(slot * TOPK, (slot + 1) * TOPK):
            word = word | jnp.where(lane == low[:, t : t + 1], bit[:, t : t + 1], 0)
        word_ref[slot] = word
    total = jnp.zeros(lane.shape, jnp.float32)
    acc = jnp.zeros(out_ref.shape, jnp.float32)

    def put(lanes, value):
        tile_ref[:, lanes] = value

    self_block = near_ref[:, 0].reshape(-1, width + clust)
    member_block = near_ref[:, 1].reshape(-1, width + clust)
    far_block = flat(far_ref)
    slots = (0, 1, pick_ref[0], 5 - pick_ref[0])
    for slot, block in zip(slots, (self_block, member_block, self_block, far_block)):
        total = weights(cosines(rows_ref[:, :width], block[:, :width]), word_ref[slot], total, put)
        acc = acc + jnp.dot(tile_ref[...], block[:, width:], preferred_element_type=jnp.float32)
    out_ref[...] = mix(acc, jnp.sum(total, axis=1, keepdims=True), rows_ref[:, width : width + clust])


def hub_rows(self_slot, mine, near, far, width):
    share = mine.shape[0]
    clust = near.shape[3] - width
    rows = near.shape[0] * near.shape[2]
    return pl.pallas_call(
        functools.partial(hub_rows_kernel, width),
        out_shape=jax.ShapeDtypeStruct((share, clust), jnp.bfloat16),
        grid_spec=pltpu.PrefetchScalarGridSpec(
            num_scalar_prefetch=1,
            grid=(1,),
            in_specs=[
                pl.BlockSpec(mine.shape, lambda i, pick: (0, 0)),
                pl.BlockSpec(near.shape, lambda i, pick: (0, 0, 0, 0)),
                pl.BlockSpec(far.shape, lambda i, pick: (0, 0, 0)),
            ],
            out_specs=pl.BlockSpec((share, clust), lambda i, pick: (0, 0)),
            scratch_shapes=[pltpu.VMEM((K, share, LANES), jnp.int32), pltpu.VMEM((share, rows), jnp.bfloat16)],
        ),
        compiler_params=pltpu.CompilerParams(vmem_limit_bytes=VMEM_LIMIT),
        cost_estimate=pl.CostEstimate(flops=rows, bytes_accessed=rows, transcendentals=0),
        name="hub_rows",
    )(self_slot, mine, near, far)


def send(block, target):
    slabs, reps = lax.axis_size("slab"), lax.axis_size("rep")
    chips = slabs // 4
    pairs = []
    for device in range(slabs * reps):
        slab, rep = divmod(device, reps)
        to = target(slab // (2 * chips), slab // 2 % chips, slab % 2, rep)
        if to is not None:
            pairs.append((device, ((to[0] * chips + to[1]) * 2 + to[2]) * reps + to[3]))
    return lax.ppermute(block, AXES, pairs)


def along_line(block, table):
    return send(
        block, lambda half, chip, core, rep: (half, chip, core, table[rep]) if rep in table else None
    )


def swap_cores(block):
    return send(block, lambda half, chip, core, rep: (half, chip, 1 - core, rep))


def flags_of(code):
    flag = code.astype(jnp.float32).astype(jnp.int32) // HALF
    return flag & 3, (flag >> 2) & 1


def join_pieces(piece):
    slabs = lax.axis_size("slab")
    members, chips = slabs // 2, slabs // 4
    layers = [[h * members + c * 2 + core for c in range(chips)] for h in range(2) for core in range(2)]
    repeated = jnp.broadcast_to(piece[None], (chips,) + piece.shape)
    return lax.all_to_all(repeated, "slab", 0, 0, axis_index_groups=layers, tiled=True)


OUTWARD = {1: 0, 2: 3}
MIDDLE = {1: 2, 2: 1}


def spread_line(block):
    across = along_line(block, {0: 2, 2: 0, 1: 3, 3: 1})
    beside = along_line(block, {0: 1, 1: 0, 2: 3, 3: 2})
    return across, beside


def scatter(block):
    members = lax.axis_size("slab") // 2
    rows, width = block.shape
    planes = [[h * members + m for m in range(members)] for h in range(2)]
    return lax.all_to_all(
        block.reshape(members, rows // members, width), "slab", 0, 0, axis_index_groups=planes, tiled=True
    )


def hub_candidates(mine, hub_ids):
    members, reps = lax.axis_size("slab") // 2, lax.axis_size("rep")
    slab = lax.axis_index("slab")
    hub_slab, hub_rep = lax.div(hub_ids, reps), lax.rem(hub_ids, reps)
    member = lax.rem(hub_slab, members)
    held = jnp.stack(
        [lax.dynamic_index_in_dim(mine, member[h], 0, keepdims=False) for h in range(HUBS)], axis=0
    )
    got = send(held, lambda half, chip, core, rep: (1 - half, chip, core, rep))
    away = lax.div(hub_slab, members) != lax.div(slab, members)
    held = jnp.where(away[:, None, None], got, held)[None]
    rep = lax.axis_index("rep")
    for bit in range(2):
        got = along_line(held, {r: r ^ (1 << bit) for r in range(4)})
        upper = (rep >> bit) & 1 == 1
        held = jnp.concatenate([jnp.where(upper, got, held), jnp.where(upper, held, got)], axis=0)
    return held, hub_rep


def hub_share(held, hub_rep, code_at):
    slab = lax.axis_index("slab")
    pick = lambda pieces, at: jnp.where(
        at < 2, jnp.where(at == 0, pieces[0], pieces[1]), jnp.where(at == 2, pieces[2], pieces[3])
    )
    chosen = []
    for h in range(HUBS):
        hub = pick(held[:, h], hub_rep[h])
        want, _ = flags_of(hub[:1, code_at : code_at + 1])
        chosen.append(jnp.stack([hub, pick(held[:, h], want)], axis=0))
    held = jnp.stack(chosen, axis=0)
    first_core = lax.rem(slab, 2) == 0
    keep = jnp.where(first_core, held[0], held[1])
    got = swap_cores(jnp.where(first_core, held[1], held[0]))
    return jnp.concatenate([jnp.where(first_core, keep, got), jnp.where(first_core, got, keep)], axis=1)


def body(embeddings, indicators, neighbours, hub_ids, columns):
    rows, width = embeddings.shape
    clust = indicators.shape[1]
    full = width + clust
    reps = lax.axis_size("rep")
    total = lax.axis_size("slab") * reps
    rep = lax.axis_index("rep")
    steps = rows // ROW_TILE
    slots = neighbours[0].astype(jnp.int32)
    want = slots[1] & 3
    order = slots[2] - total
    core = lax.rem(lax.axis_index("slab"), 2)
    near_slot = jnp.where(order == core, 2, 3)
    barrier = lax.optimization_barrier

    joined, normed, rest = join(total, neighbours.reshape(-1), embeddings, indicators, columns)
    across, beside = spread_line(rest)

    pick = jnp.stack([near_slot]).astype(jnp.int32)
    own_rows = (joined, (ROW_TILE, width), lambda r, pick: (r, 0))
    own_x = (joined, (rows, width), lambda r, pick: (0, 0))
    own_y = (joined, (rows, clust), lambda r, pick: (0, width // clust))
    words = keep_words(pick, rest[None], lambda pick: 0, rows, 1)
    *carry, own_tile = tile_of(pick, own_rows, own_x, own_y, words, lambda pick: 0)
    mine, words, carry, own_tile, rest, across, beside = barrier(
        (scatter(joined), words, carry, own_tile, rest, across, beside)
    )

    held, hub_rep = hub_candidates(mine, hub_ids)
    held, normed, rest, across = barrier((held, normed, rest, across))

    outer, middle = along_line(across, OUTWARD), along_line(rest, MIDDLE)
    across_x, beside_x = spread_line(normed)
    both = hub_share(held, hub_rep, full)
    near = join_pieces(both[:, :, :full])
    at_end = (rep == 0) | (rep == 3)
    group_rest = jnp.stack([rest, beside, across, jnp.where(at_end, outer, middle)], axis=0)
    at = want ^ rep
    flag = lax.dynamic_index_in_dim(group_rest[:, -1, 0], at, 0, keepdims=False).astype(jnp.int32)
    member_want, member_order = flag & 3, (flag >> 2) & 1
    second = member_want ^ rep
    place = lambda k: jnp.where((k == 3) & at_end, 4, k)
    pick = jnp.stack(
        [near_slot, place(at), place(second), jnp.where(member_order == core, 2, 3), at, second]
    ).astype(jnp.int32)
    member_words = keep_words(pick, group_rest, lambda pick: pick[4], rows, WORDS_HINT)
    near, group_rest, member_words, pick, normed, across_x, beside_x = barrier(
        (near, group_rest, member_words, pick, normed, across_x, beside_x)
    )

    far = swap_cores(near[:, 0])
    outer_x, middle_x = along_line(across_x, OUTWARD), along_line(normed, MIDDLE)
    _, hub_order = flags_of(both[0, 0, full])
    share = hub_rows(jnp.where(hub_order == core, 2, 3)[None], both[0], near, far, width)
    near_new = join_pieces(share).reshape(rows, clust)
    far_new = swap_cores(near_new)
    near_new, far_new, outer_x, middle_x = barrier((near_new, far_new, outer_x, middle_x))

    near_tile, far_tile, member_tile, degree, new, member_new = seven_of(
        pick, (normed, beside_x, across_x, middle_x, outer_x), normed, group_rest, near, far, words, member_words,
        carry, indicators,
    )
    return last_of(
        (own_tile, member_tile, near_tile, far_tile), (new, member_new, near_new, far_new), degree, indicators
    )


def solution(mesh):
    return jax.shard_map(
        body,
        mesh=mesh,
        in_specs=(
            P(("slab", "rep"), None),
            P(("slab", "rep"), None),
            P(("slab", "rep"), None),
            P(),
            P(("slab", "rep"), None, None),
        ),
        out_specs=P(("slab", "rep"), None),
        check_vma=False,
    )
```

```python
import functools

import jax
import jax.numpy as jnp
from jax import lax
from jax.experimental import pallas as pl
from jax.experimental.pallas import tpu as pltpu
from jax.sharding import PartitionSpec as P

K = 4
HUBS = 2
TOPK = 16
LANES = 128
EPS = 1e-06
TAU = 0.04
ALPHA = 0.8
AXES = ("slab", "rep")
ROW_TILE = 256
VMEM_LIMIT = 58 << 20
SCALE = 1.4426950408889634 / TAU
HALF = 32
FLAG_ROWS = 16
BLOCKS_NEAR = 5
WORDS_HINT = 30_000_000_000


def join_kernel(blocks, near_ref, x_ref, y_ref, cols_ref, all_ref, normed_ref, rest_ref):
    width, clust = x_ref.shape[1], y_ref.shape[1]
    step = pl.program_id(0)
    rows = pl.num_programs(0) * ROW_TILE
    values = x_ref[...].astype(jnp.float32)
    scale = lax.rsqrt(jnp.sum(values * values, axis=1, keepdims=True) + EPS)
    normed = (values * scale).astype(jnp.bfloat16)
    cols = cols_ref[...].reshape(K * TOPK, cols_ref.shape[2])
    flag = (near_ref[1] & 3) + 4 * (near_ref[2] - blocks)
    coded = jnp.concatenate([(cols >> 5) + HALF * flag, cols & (HALF - 1)], axis=0)
    all_ref[:, :width] = normed
    all_ref[:, width : width + clust] = y_ref[...]
    all_ref[:, width + clust :] = coded.astype(jnp.float32).T.astype(jnp.bfloat16)
    normed_ref[...] = normed
    rest_ref[pl.ds(pl.multiple_of(step * ROW_TILE, ROW_TILE), ROW_TILE), :] = y_ref[...]
    single = jnp.left_shift((cols & (LANES - 1)) + LANES, cols >> 7)
    place = pl.multiple_of(rows + step * K * TOPK, K * TOPK)
    rest_ref[pl.ds(place, K * TOPK), :] = single.astype(jnp.float32).astype(jnp.bfloat16)
    flags = jnp.full((FLAG_ROWS, clust), flag, jnp.int32)
    rest_ref[rows + rows // ROW_TILE * K * TOPK :, :] = flags.astype(jnp.float32).astype(jnp.bfloat16)


def join(blocks, near, embeddings, indicators, columns):
    rows, width = embeddings.shape
    clust = indicators.shape[1]
    by_row = lambda cols: pl.BlockSpec((ROW_TILE, cols), lambda r, flag: (r, 0))
    steps = rows // ROW_TILE
    rest = (rows + steps * K * TOPK + FLAG_ROWS, clust)
    return pl.pallas_call(
        functools.partial(join_kernel, blocks),
        out_shape=[
            jax.ShapeDtypeStruct(shape, jnp.bfloat16)
            for shape in ((rows, width + clust + 2 * K * TOPK), (rows, width), rest)
        ],
        grid_spec=pltpu.PrefetchScalarGridSpec(
            num_scalar_prefetch=1,
            grid=(steps,),
            in_specs=[
                by_row(width),
                by_row(clust),
                pl.BlockSpec((K, TOPK, ROW_TILE), lambda r, flag: (0, 0, r)),
            ],
            out_specs=[by_row(width + clust + 2 * K * TOPK), by_row(width), pl.BlockSpec(rest, lambda r, flag: (0, 0))],
        ),
        compiler_params=pltpu.CompilerParams(vmem_limit_bytes=VMEM_LIMIT),
        name="join",
    )(near, embeddings, indicators, jnp.transpose(columns, (1, 2, 0)))


def words_kernel(pick_ref, coded_ref, out_ref):
    lane = lax.broadcasted_iota(jnp.int32, (LANES, LANES), 0)
    for step in range(coded_ref.shape[1] // (K * TOPK)):
        coded = coded_ref[0, step * K * TOPK : (step + 1) * K * TOPK].astype(jnp.float32).astype(jnp.int32)
        high = sum((coded >= LANES << m).astype(jnp.int32) for m in range(1, 8))
        low = jnp.right_shift(coded, high) & (LANES - 1)
        bit = jnp.left_shift(jnp.ones_like(high), high)
        for part in range(ROW_TILE // LANES):
            here = slice(part * LANES, (part + 1) * LANES)
            for slot in range(K):
                word = jnp.zeros((LANES, LANES), jnp.int32)
                for t in range(slot * TOPK, (slot + 1) * TOPK):
                    word = word | jnp.where(lane == low[t : t + 1, here], bit[t : t + 1, here], 0)
                start = step * ROW_TILE + part * LANES
                out_ref[slot, start : start + LANES, :] = word.T


def keep_words(pick, rest, which, rows, hint):
    part = rows // ROW_TILE * K * TOPK
    clust = rest.shape[2]
    return pl.pallas_call(
        words_kernel,
        out_shape=jax.ShapeDtypeStruct((K, rows, LANES), jnp.int32),
        grid_spec=pltpu.PrefetchScalarGridSpec(
            num_scalar_prefetch=1,
            grid=(1,),
            in_specs=[pl.BlockSpec((1, part, clust), lambda i, pick: (which(pick), rows // part, 0))],
            out_specs=pl.BlockSpec((K, rows, LANES), lambda i, pick: (0, 0, 0)),
        ),
        compiler_params=pltpu.CompilerParams(vmem_limit_bytes=VMEM_LIMIT),
        cost_estimate=pl.CostEstimate(flops=hint, bytes_accessed=rows * 512, transcendentals=0),
        name="keep_words",
    )(pick, rest)


def mix(acc, degree, anchor):
    return (ALPHA * acc / degree + (1.0 - ALPHA) * anchor.astype(jnp.float32)).astype(jnp.bfloat16)


def weights(cosine, word, total, put):
    for j in range(cosine.shape[1] // LANES):
        part = cosine[:, j * LANES : (j + 1) * LANES]
        raw = jnp.where((word & (1 << j)) != 0, jnp.exp2(part * SCALE - SCALE), 0.0)
        total = total + raw
        put(slice(j * LANES, (j + 1) * LANES), raw.astype(jnp.bfloat16))
    return total


def cosines(rows, others):
    return lax.dot_general(rows, others, (((1,), (1,)), ((), ())), preferred_element_type=jnp.float32)


def flat(ref):
    value = ref[...]
    return value.reshape(-1, value.shape[-1])


def tile_kernel(has_carry, last, pick_ref, x_ref, other_ref, w_ref, y_ref, *refs):
    refs = list(refs)
    deg_in, acc_in = (refs.pop(0), refs.pop(0)) if has_carry else (None, None)
    anchor_ref = refs.pop(0) if last else None
    deg_ref, acc_ref, tile_ref = refs
    word = w_ref[0]
    total = deg_in[...] if has_carry else jnp.zeros(word.shape, jnp.float32)

    def put(lanes, value):
        tile_ref[:, lanes] = value

    total = weights(cosines(x_ref[...], flat(other_ref)), word, total, put)
    deg_ref[...] = total
    gathered = jnp.dot(tile_ref[...], flat(y_ref), preferred_element_type=jnp.float32)
    if has_carry:
        gathered = acc_in[...] + gathered
    if last:
        gathered = mix(gathered, jnp.sum(total, axis=1, keepdims=True), anchor_ref[...])
    acc_ref[...] = gathered


def tile_of(pick, x, other, y, words, slot, carry=None, anchor=None, keep=True):
    rows, clust = words.shape[1], y[1][-1]
    by_row = lambda cols: pl.BlockSpec((ROW_TILE, cols), lambda r, pick: (r, 0))
    spec = lambda operand: pl.BlockSpec(operand[1], operand[2])
    last = anchor is not None
    args = [x[0], other[0], words, y[0], *(carry or ())] + ([anchor[0]] if last else [])
    specs = [spec(x), spec(other), pl.BlockSpec((1, ROW_TILE, LANES), lambda r, pick: (slot(pick), r, 0)), spec(y)]
    specs += ([by_row(LANES), by_row(clust)] if carry else []) + ([spec(anchor)] if last else [])
    outs = [(LANES, jnp.float32), (clust, jnp.bfloat16 if last else jnp.float32)] + [(rows, jnp.bfloat16)] * keep
    return pl.pallas_call(
        functools.partial(tile_kernel, carry is not None, last),
        out_shape=[jax.ShapeDtypeStruct((rows, cols), kind) for cols, kind in outs],
        grid_spec=pltpu.PrefetchScalarGridSpec(
            num_scalar_prefetch=1,
            grid=(rows // ROW_TILE,),
            in_specs=specs,
            out_specs=[by_row(cols) for cols, _ in outs],
            scratch_shapes=[] if keep else [pltpu.VMEM((ROW_TILE, rows), jnp.bfloat16)],
        ),
        compiler_params=pltpu.CompilerParams(vmem_limit_bytes=VMEM_LIMIT),
        cost_estimate=pl.CostEstimate(flops=rows * clust, bytes_accessed=rows * clust, transcendentals=0),
        name="tile",
    )(pick, *args)


def put_to(ref):
    def put(lanes, value):
        ref[:, lanes] = value

    return put


def run_tiles(rows, plan, total, acc):
    for word, (other, y), tile in plan:
        total = weights(cosines(rows, other), word, total, put_to(tile))
        acc = acc + jnp.dot(tile[...], y, preferred_element_type=jnp.float32)
    return total, acc


def hub_blocks(near_ref, far_ref, width):
    near, far = near_ref[:, 0].reshape(-1, near_ref.shape[3]), flat(far_ref)
    return (near[:, :width], near[:, width:]), (far[:, :width], far[:, width:])


def hub_specs(near, far):
    chips, _, piece, full = near.shape
    once = pl.Buffered(1)
    return [
        pl.BlockSpec((chips, 1, piece, full), lambda r, pick: (0, 0, 0, 0), pipeline_mode=once),
        pl.BlockSpec((chips, piece, full), lambda r, pick: (0, 0, 0), pipeline_mode=once),
    ]


def two_kernel(pick_ref, rows_ref, near_ref, far_ref, words_ref, deg_in, acc_in, near_tile, far_tile, deg_ref, acc_ref):
    near, far = hub_blocks(near_ref, far_ref, rows_ref.shape[1])
    plan = (
        (words_ref[pick_ref[0]], near, near_tile),
        (words_ref[5 - pick_ref[0]], far, far_tile),
    )
    deg_ref[...], acc_ref[...] = run_tiles(rows_ref[...], plan, deg_in[...], acc_in[...])


def two_of(pick, own_rows, near, far, words, carry):
    rows, width = own_rows.shape
    clust = carry[1].shape[1]
    by_row = lambda cols: pl.BlockSpec((ROW_TILE, cols), lambda r, pick: (r, 0))
    by_word = pl.BlockSpec((K, ROW_TILE, LANES), lambda r, pick: (0, r, 0))
    outs = [(rows, jnp.bfloat16)] * 2 + [(LANES, jnp.float32), (clust, jnp.float32)]
    return pl.pallas_call(
        two_kernel,
        out_shape=[jax.ShapeDtypeStruct((rows, cols), kind) for cols, kind in outs],
        grid_spec=pltpu.PrefetchScalarGridSpec(
            num_scalar_prefetch=1,
            grid=(rows // ROW_TILE,),
            in_specs=[by_row(width), *hub_specs(near, far), by_word, by_row(LANES), by_row(clust)],
            out_specs=[by_row(cols) for cols, _ in outs],
        ),
        compiler_params=pltpu.CompilerParams(vmem_limit_bytes=VMEM_LIMIT),
        cost_estimate=pl.CostEstimate(flops=rows * clust, bytes_accessed=rows * clust, transcendentals=0),
        name="two",
    )(pick, own_rows, near, far, words, *carry)


def five_kernel(pick_ref, *refs):
    blocks, refs = refs[:BLOCKS_NEAR], refs[BLOCKS_NEAR:]
    rows_ref, first_y, second_y, near_ref, far_ref, own_ref, member_ref, deg_in, acc_in, anchor_ref = refs[:10]
    member_tile, deg_ref, new_ref, other_ref, first_x, second_x, held, spare, sems = refs[10:]
    step = pl.program_id(0)

    @pl.when(step == 0)
    def _():
        for which, target in enumerate((first_x, second_x)):
            for i, block in enumerate(blocks):

                @pl.when(pick_ref[1 + which] == i)
                def _():
                    copy = pltpu.make_async_copy(block, target, sems.at[which])
                    copy.start()
                    copy.wait()

    first, second = (first_x[...], first_y[0]), (second_x[...], second_y[0])
    near, far = hub_blocks(near_ref, far_ref, rows_ref.shape[1])
    total, acc = run_tiles(rows_ref[...], ((own_ref[0], first, member_tile),), deg_in[...], acc_in[...])
    deg_ref[...] = total
    new_ref[...] = mix(acc, jnp.sum(total, axis=1, keepdims=True), anchor_ref[...])
    here = pl.ds(pl.multiple_of(step * ROW_TILE, ROW_TILE), ROW_TILE)
    plan = (
        (member_ref[pick_ref[3]], near, held),
        (member_ref[5 - pick_ref[3]], far, spare),
        (member_ref[0], first, held),
        (member_ref[1], second, spare),
    )
    zeros = lambda ref: jnp.zeros(ref.shape, jnp.float32)
    total, acc = run_tiles(first_x[here, :], plan, zeros(deg_in), zeros(acc_in))
    other_ref[...] = mix(acc, jnp.sum(total, axis=1, keepdims=True), first_y[0, here, :])


def five_of(pick, blocks, own_rows, rest, near, far, words, member_words, carry, anchor):
    rows, width = blocks[0].shape
    clust = rest.shape[2]
    by_row = lambda cols: pl.BlockSpec((ROW_TILE, cols), lambda r, pick: (r, 0))
    rest_at = lambda k: pl.BlockSpec(
        (1, rows, clust), lambda r, pick: (pick[k], 0, 0), pipeline_mode=pl.Buffered(1)
    )
    outs = [(rows, jnp.bfloat16), (LANES, jnp.float32)] + [(clust, jnp.bfloat16)] * 2
    return pl.pallas_call(
        five_kernel,
        out_shape=[jax.ShapeDtypeStruct((rows, cols), kind) for cols, kind in outs],
        grid_spec=pltpu.PrefetchScalarGridSpec(
            num_scalar_prefetch=1,
            grid=(rows // ROW_TILE,),
            in_specs=[pl.BlockSpec(memory_space=pl.ANY)] * len(blocks)
            + [by_row(width), rest_at(4), rest_at(5), *hub_specs(near, far)]
            + [
                pl.BlockSpec((1, ROW_TILE, LANES), lambda r, pick: (1, r, 0)),
                pl.BlockSpec((K, ROW_TILE, LANES), lambda r, pick: (0, r, 0)),
                by_row(LANES),
                by_row(clust),
                by_row(clust),
            ],
            out_specs=[by_row(cols) for cols, _ in outs],
            scratch_shapes=[pltpu.VMEM((rows, width), jnp.bfloat16)] * 2
            + [pltpu.VMEM((ROW_TILE, rows), jnp.bfloat16)] * 2
            + [pltpu.SemaphoreType.DMA((2,))],
        ),
        compiler_params=pltpu.CompilerParams(vmem_limit_bytes=VMEM_LIMIT),
        cost_estimate=pl.CostEstimate(
            flops=10 * rows * rows * 768, bytes_accessed=8 * rows * rows, transcendentals=5 * rows * rows
        ),
        name="five",
    )(pick, *blocks, own_rows, rest, rest, near, far, words, member_words, *carry, anchor)


def last_kernel(*refs):
    tiles, news, (deg_ref, anchor_ref, out_ref) = refs[:K], refs[K : 2 * K], refs[2 * K :]
    acc = sum(jnp.dot(t[...], y[...], preferred_element_type=jnp.float32) for t, y in zip(tiles, news))
    out_ref[...] = mix(acc, jnp.sum(deg_ref[...], axis=1, keepdims=True), anchor_ref[...])


def last_of(tiles, news, degree, anchor):
    rows, clust = anchor.shape
    by_row = lambda cols: pl.BlockSpec((ROW_TILE, cols), lambda r: (r, 0))
    return pl.pallas_call(
        last_kernel,
        out_shape=jax.ShapeDtypeStruct((rows, clust), jnp.bfloat16),
        grid=(rows // ROW_TILE,),
        in_specs=[by_row(rows)] * K
        + [pl.BlockSpec((rows, clust), lambda r: (0, 0))] * K
        + [by_row(LANES), by_row(clust)],
        out_specs=by_row(clust),
        compiler_params=pltpu.CompilerParams(vmem_limit_bytes=VMEM_LIMIT),
        cost_estimate=pl.CostEstimate(flops=8 * rows * rows * clust, bytes_accessed=8 * rows * rows, transcendentals=0),
        name="last",
    )(*tiles, *news, degree, anchor)


def hub_rows_kernel(width, pick_ref, rows_ref, near_ref, far_ref, out_ref, word_ref, tile_ref):
    clust = out_ref.shape[1]
    half = K * TOPK
    coded = rows_ref[:, width + clust :].astype(jnp.float32).astype(jnp.int32)
    high = coded[:, :half] & (HALF - 1)
    low = (high & 3) * HALF + coded[:, half:]
    bit = jnp.left_shift(jnp.ones_like(high), high >> 2)
    lane = lax.broadcasted_iota(jnp.int32, (rows_ref.shape[0], LANES), 1)
    for slot in range(K):
        word = jnp.zeros(lane.shape, jnp.int32)
        for t in range(slot * TOPK, (slot + 1) * TOPK):
            word = word | jnp.where(lane == low[:, t : t + 1], bit[:, t : t + 1], 0)
        word_ref[slot] = word
    total = jnp.zeros(lane.shape, jnp.float32)
    acc = jnp.zeros(out_ref.shape, jnp.float32)

    def put(lanes, value):
        tile_ref[:, lanes] = value

    self_block = near_ref[:, 0].reshape(-1, width + clust)
    member_block = near_ref[:, 1].reshape(-1, width + clust)
    far_block = flat(far_ref)
    slots = (0, 1, pick_ref[0], 5 - pick_ref[0])
    for slot, block in zip(slots, (self_block, member_block, self_block, far_block)):
        total = weights(cosines(rows_ref[:, :width], block[:, :width]), word_ref[slot], total, put)
        acc = acc + jnp.dot(tile_ref[...], block[:, width:], preferred_element_type=jnp.float32)
    out_ref[...] = mix(acc, jnp.sum(total, axis=1, keepdims=True), rows_ref[:, width : width + clust])


def hub_rows(self_slot, mine, near, far, width):
    share = mine.shape[0]
    clust = near.shape[3] - width
    rows = near.shape[0] * near.shape[2]
    return pl.pallas_call(
        functools.partial(hub_rows_kernel, width),
        out_shape=jax.ShapeDtypeStruct((share, clust), jnp.bfloat16),
        grid_spec=pltpu.PrefetchScalarGridSpec(
            num_scalar_prefetch=1,
            grid=(1,),
            in_specs=[
                pl.BlockSpec(mine.shape, lambda i, pick: (0, 0)),
                pl.BlockSpec(near.shape, lambda i, pick: (0, 0, 0, 0)),
                pl.BlockSpec(far.shape, lambda i, pick: (0, 0, 0)),
            ],
            out_specs=pl.BlockSpec((share, clust), lambda i, pick: (0, 0)),
            scratch_shapes=[pltpu.VMEM((K, share, LANES), jnp.int32), pltpu.VMEM((share, rows), jnp.bfloat16)],
        ),
        compiler_params=pltpu.CompilerParams(vmem_limit_bytes=VMEM_LIMIT),
        cost_estimate=pl.CostEstimate(flops=rows, bytes_accessed=rows, transcendentals=0),
        name="hub_rows",
    )(self_slot, mine, near, far)


def send(block, target):
    slabs, reps = lax.axis_size("slab"), lax.axis_size("rep")
    chips = slabs // 4
    pairs = []
    for device in range(slabs * reps):
        slab, rep = divmod(device, reps)
        to = target(slab // (2 * chips), slab // 2 % chips, slab % 2, rep)
        if to is not None:
            pairs.append((device, ((to[0] * chips + to[1]) * 2 + to[2]) * reps + to[3]))
    return lax.ppermute(block, AXES, pairs)


def along_line(block, table):
    return send(
        block, lambda half, chip, core, rep: (half, chip, core, table[rep]) if rep in table else None
    )


def swap_cores(block):
    return send(block, lambda half, chip, core, rep: (half, chip, 1 - core, rep))


def flags_of(code):
    flag = code.astype(jnp.float32).astype(jnp.int32) // HALF
    return flag & 3, (flag >> 2) & 1


def join_pieces(piece):
    slabs = lax.axis_size("slab")
    members, chips = slabs // 2, slabs // 4
    layers = [[h * members + c * 2 + core for c in range(chips)] for h in range(2) for core in range(2)]
    repeated = jnp.broadcast_to(piece[None], (chips,) + piece.shape)
    return lax.all_to_all(repeated, "slab", 0, 0, axis_index_groups=layers, tiled=True)


OUTWARD = {1: 0, 2: 3}
MIDDLE = {1: 2, 2: 1}


def spread_line(block):
    across = along_line(block, {0: 2, 2: 0, 1: 3, 3: 1})
    beside = along_line(block, {0: 1, 1: 0, 2: 3, 3: 2})
    return across, beside


def scatter(block):
    members = lax.axis_size("slab") // 2
    rows, width = block.shape
    planes = [[h * members + m for m in range(members)] for h in range(2)]
    return lax.all_to_all(
        block.reshape(members, rows // members, width), "slab", 0, 0, axis_index_groups=planes, tiled=True
    )


def hub_candidates(mine, hub_ids):
    members, reps = lax.axis_size("slab") // 2, lax.axis_size("rep")
    slab = lax.axis_index("slab")
    hub_slab, hub_rep = lax.div(hub_ids, reps), lax.rem(hub_ids, reps)
    member = lax.rem(hub_slab, members)
    held = jnp.stack(
        [lax.dynamic_index_in_dim(mine, member[h], 0, keepdims=False) for h in range(HUBS)], axis=0
    )
    got = send(held, lambda half, chip, core, rep: (1 - half, chip, core, rep))
    away = lax.div(hub_slab, members) != lax.div(slab, members)
    held = jnp.where(away[:, None, None], got, held)[None]
    rep = lax.axis_index("rep")
    for bit in range(2):
        got = along_line(held, {r: r ^ (1 << bit) for r in range(4)})
        upper = (rep >> bit) & 1 == 1
        held = jnp.concatenate([jnp.where(upper, got, held), jnp.where(upper, held, got)], axis=0)
    return held, hub_rep


def hub_share(held, hub_rep, code_at):
    slab = lax.axis_index("slab")
    pick = lambda pieces, at: jnp.where(
        at < 2, jnp.where(at == 0, pieces[0], pieces[1]), jnp.where(at == 2, pieces[2], pieces[3])
    )
    chosen = []
    for h in range(HUBS):
        hub = pick(held[:, h], hub_rep[h])
        want, _ = flags_of(hub[:1, code_at : code_at + 1])
        chosen.append(jnp.stack([hub, pick(held[:, h], want)], axis=0))
    held = jnp.stack(chosen, axis=0)
    first_core = lax.rem(slab, 2) == 0
    keep = jnp.where(first_core, held[0], held[1])
    got = swap_cores(jnp.where(first_core, held[1], held[0]))
    return jnp.concatenate([jnp.where(first_core, keep, got), jnp.where(first_core, got, keep)], axis=1)


def body(embeddings, indicators, neighbours, hub_ids, columns):
    rows, width = embeddings.shape
    clust = indicators.shape[1]
    full = width + clust
    reps = lax.axis_size("rep")
    total = lax.axis_size("slab") * reps
    rep = lax.axis_index("rep")
    steps = rows // ROW_TILE
    slots = neighbours[0].astype(jnp.int32)
    want = slots[1] & 3
    order = slots[2] - total
    core = lax.rem(lax.axis_index("slab"), 2)
    near_slot = jnp.where(order == core, 2, 3)
    barrier = lax.optimization_barrier

    joined, normed, rest = join(total, neighbours.reshape(-1), embeddings, indicators, columns)
    across, beside = spread_line(rest)

    pick = jnp.stack([near_slot]).astype(jnp.int32)
    own_rows = (joined, (ROW_TILE, width), lambda r, pick: (r, 0))
    own_x = (joined, (rows, width), lambda r, pick: (0, 0))
    own_y = (joined, (rows, clust), lambda r, pick: (0, width // clust))
    words = keep_words(pick, rest[None], lambda pick: 0, rows, 1)
    *carry, own_tile = tile_of(pick, own_rows, own_x, own_y, words, lambda pick: 0)
    mine, words, carry, own_tile, rest, across, beside = barrier(
        (scatter(joined), words, carry, own_tile, rest, across, beside)
    )

    held, hub_rep = hub_candidates(mine, hub_ids)
    held, normed, rest, across = barrier((held, normed, rest, across))

    outer, middle = along_line(across, OUTWARD), along_line(rest, MIDDLE)
    across_x, beside_x = spread_line(normed)
    both = hub_share(held, hub_rep, full)
    near = join_pieces(both[:, :, :full])
    at_end = (rep == 0) | (rep == 3)
    group_rest = jnp.stack([rest, beside, across, jnp.where(at_end, outer, middle)], axis=0)
    at = want ^ rep
    flag = lax.dynamic_index_in_dim(group_rest[:, -1, 0], at, 0, keepdims=False).astype(jnp.int32)
    member_want, member_order = flag & 3, (flag >> 2) & 1
    second = member_want ^ rep
    place = lambda k: jnp.where((k == 3) & at_end, 4, k)
    pick = jnp.stack(
        [near_slot, place(at), place(second), jnp.where(member_order == core, 2, 3), at, second]
    ).astype(jnp.int32)
    member_words = keep_words(pick, group_rest, lambda pick: pick[4], rows, WORDS_HINT)
    near, group_rest, member_words, pick, normed, across_x, beside_x = barrier(
        (near, group_rest, member_words, pick, normed, across_x, beside_x)
    )

    far = swap_cores(near[:, 0])
    outer_x, middle_x = along_line(across_x, OUTWARD), along_line(normed, MIDDLE)
    _, hub_order = flags_of(both[0, 0, full])
    share = hub_rows(jnp.where(hub_order == core, 2, 3)[None], both[0], near, far, width)
    share, near, far = barrier((share, near, far))
    near_new = join_pieces(share).reshape(rows, clust)
    near_tile, far_tile, *carry = two_of(pick, normed, near, far, words, carry)
    near_new, carry = barrier((near_new, carry))
    far_new = swap_cores(near_new)
    near_new, far_new, outer_x, middle_x = barrier((near_new, far_new, outer_x, middle_x))

    member_tile, degree, new, member_new = five_of(
        pick, (normed, beside_x, across_x, middle_x, outer_x), normed, group_rest, near, far, words, member_words,
        carry, indicators,
    )
    return last_of(
        (own_tile, member_tile, near_tile, far_tile), (new, member_new, near_new, far_new), degree, indicators
    )


def solution(mesh):
    return jax.shard_map(
        body,
        mesh=mesh,
        in_specs=(
            P(("slab", "rep"), None),
            P(("slab", "rep"), None),
            P(("slab", "rep"), None),
            P(),
            P(("slab", "rep"), None, None),
        ),
        out_specs=P(("slab", "rep"), None),
        check_vma=False,
    )
```

```python
import functools

import jax
import jax.numpy as jnp
from jax import lax
from jax.experimental import pallas as pl
from jax.experimental.pallas import tpu as pltpu
from jax.sharding import PartitionSpec as P

K = 4
HUBS = 2
TOPK = 16
LANES = 128
EPS = 1e-06
TAU = 0.04
ALPHA = 0.8
AXES = ("slab", "rep")
ROW_TILE = 256
VMEM_LIMIT = 58 << 20
SCALE = 1.4426950408889634 / TAU
HALF = 32
FLAG_ROWS = 16
BLOCKS_NEAR = 5
WORDS_HINT = 30_000_000_000


def join_kernel(blocks, near_ref, x_ref, y_ref, cols_ref, all_ref, normed_ref, rest_ref):
    width, clust = x_ref.shape[1], y_ref.shape[1]
    step = pl.program_id(0)
    rows = pl.num_programs(0) * ROW_TILE
    values = x_ref[...].astype(jnp.float32)
    scale = lax.rsqrt(jnp.sum(values * values, axis=1, keepdims=True) + EPS)
    normed = (values * scale).astype(jnp.bfloat16)
    cols = cols_ref[...].reshape(K * TOPK, cols_ref.shape[2])
    flag = (near_ref[1] & 3) + 4 * (near_ref[2] - blocks)
    coded = jnp.concatenate([(cols >> 5) + HALF * flag, cols & (HALF - 1)], axis=0)
    all_ref[:, :width] = normed
    all_ref[:, width : width + clust] = y_ref[...]
    all_ref[:, width + clust :] = coded.astype(jnp.float32).T.astype(jnp.bfloat16)
    normed_ref[...] = normed
    rest_ref[pl.ds(pl.multiple_of(step * ROW_TILE, ROW_TILE), ROW_TILE), :] = y_ref[...]
    single = jnp.left_shift((cols & (LANES - 1)) + LANES, cols >> 7)
    place = pl.multiple_of(rows + step * K * TOPK, K * TOPK)
    rest_ref[pl.ds(place, K * TOPK), :] = single.astype(jnp.float32).astype(jnp.bfloat16)
    flags = jnp.full((FLAG_ROWS, clust), flag, jnp.int32)
    rest_ref[rows + rows // ROW_TILE * K * TOPK :, :] = flags.astype(jnp.float32).astype(jnp.bfloat16)


def join(blocks, near, embeddings, indicators, columns):
    rows, width = embeddings.shape
    clust = indicators.shape[1]
    by_row = lambda cols: pl.BlockSpec((ROW_TILE, cols), lambda r, flag: (r, 0))
    steps = rows // ROW_TILE
    rest = (rows + steps * K * TOPK + FLAG_ROWS, clust)
    return pl.pallas_call(
        functools.partial(join_kernel, blocks),
        out_shape=[
            jax.ShapeDtypeStruct(shape, jnp.bfloat16)
            for shape in ((rows, width + clust + 2 * K * TOPK), (rows, width), rest)
        ],
        grid_spec=pltpu.PrefetchScalarGridSpec(
            num_scalar_prefetch=1,
            grid=(steps,),
            in_specs=[
                by_row(width),
                by_row(clust),
                pl.BlockSpec((K, TOPK, ROW_TILE), lambda r, flag: (0, 0, r)),
            ],
            out_specs=[by_row(width + clust + 2 * K * TOPK), by_row(width), pl.BlockSpec(rest, lambda r, flag: (0, 0))],
        ),
        compiler_params=pltpu.CompilerParams(vmem_limit_bytes=VMEM_LIMIT),
        name="join",
    )(near, embeddings, indicators, jnp.transpose(columns, (1, 2, 0)))


def words_kernel(pick_ref, coded_ref, out_ref):
    lane = lax.broadcasted_iota(jnp.int32, (LANES, LANES), 0)
    for step in range(coded_ref.shape[1] // (K * TOPK)):
        coded = coded_ref[0, step * K * TOPK : (step + 1) * K * TOPK].astype(jnp.float32).astype(jnp.int32)
        high = sum((coded >= LANES << m).astype(jnp.int32) for m in range(1, 8))
        low = jnp.right_shift(coded, high) & (LANES - 1)
        bit = jnp.left_shift(jnp.ones_like(high), high)
        for part in range(ROW_TILE // LANES):
            here = slice(part * LANES, (part + 1) * LANES)
            for slot in range(K):
                word = jnp.zeros((LANES, LANES), jnp.int32)
                for t in range(slot * TOPK, (slot + 1) * TOPK):
                    word = word | jnp.where(lane == low[t : t + 1, here], bit[t : t + 1, here], 0)
                start = step * ROW_TILE + part * LANES
                out_ref[slot, start : start + LANES, :] = word.T


def keep_words(pick, rest, which, rows, hint):
    part = rows // ROW_TILE * K * TOPK
    clust = rest.shape[2]
    return pl.pallas_call(
        words_kernel,
        out_shape=jax.ShapeDtypeStruct((K, rows, LANES), jnp.int32),
        grid_spec=pltpu.PrefetchScalarGridSpec(
            num_scalar_prefetch=1,
            grid=(1,),
            in_specs=[pl.BlockSpec((1, part, clust), lambda i, pick: (which(pick), rows // part, 0))],
            out_specs=pl.BlockSpec((K, rows, LANES), lambda i, pick: (0, 0, 0)),
        ),
        compiler_params=pltpu.CompilerParams(vmem_limit_bytes=VMEM_LIMIT),
        cost_estimate=pl.CostEstimate(flops=hint, bytes_accessed=rows * 512, transcendentals=0),
        name="keep_words",
    )(pick, rest)


def mix(acc, degree, anchor):
    return (ALPHA * acc / degree + (1.0 - ALPHA) * anchor.astype(jnp.float32)).astype(jnp.bfloat16)


def weights(cosine, word, total, put):
    for j in range(cosine.shape[1] // LANES):
        part = cosine[:, j * LANES : (j + 1) * LANES]
        raw = jnp.where((word & (1 << j)) != 0, jnp.exp2(part * SCALE - SCALE), 0.0)
        total = total + raw
        put(slice(j * LANES, (j + 1) * LANES), raw.astype(jnp.bfloat16))
    return total


def cosines(rows, others):
    return lax.dot_general(rows, others, (((1,), (1,)), ((), ())), preferred_element_type=jnp.float32)


def flat(ref):
    value = ref[...]
    return value.reshape(-1, value.shape[-1])


def tile_kernel(has_carry, last, pick_ref, x_ref, other_ref, w_ref, y_ref, *refs):
    refs = list(refs)
    deg_in, acc_in = (refs.pop(0), refs.pop(0)) if has_carry else (None, None)
    anchor_ref = refs.pop(0) if last else None
    deg_ref, acc_ref, tile_ref = refs
    word = w_ref[0]
    total = deg_in[...] if has_carry else jnp.zeros(word.shape, jnp.float32)

    def put(lanes, value):
        tile_ref[:, lanes] = value

    total = weights(cosines(x_ref[...], flat(other_ref)), word, total, put)
    deg_ref[...] = total
    gathered = jnp.dot(tile_ref[...], flat(y_ref), preferred_element_type=jnp.float32)
    if has_carry:
        gathered = acc_in[...] + gathered
    if last:
        gathered = mix(gathered, jnp.sum(total, axis=1, keepdims=True), anchor_ref[...])
    acc_ref[...] = gathered


def tile_of(pick, x, other, y, words, slot, carry=None, anchor=None, keep=True):
    rows, clust = words.shape[1], y[1][-1]
    by_row = lambda cols: pl.BlockSpec((ROW_TILE, cols), lambda r, pick: (r, 0))
    spec = lambda operand: pl.BlockSpec(operand[1], operand[2])
    last = anchor is not None
    args = [x[0], other[0], words, y[0], *(carry or ())] + ([anchor[0]] if last else [])
    specs = [spec(x), spec(other), pl.BlockSpec((1, ROW_TILE, LANES), lambda r, pick: (slot(pick), r, 0)), spec(y)]
    specs += ([by_row(LANES), by_row(clust)] if carry else []) + ([spec(anchor)] if last else [])
    outs = [(LANES, jnp.float32), (clust, jnp.bfloat16 if last else jnp.float32)] + [(rows, jnp.bfloat16)] * keep
    return pl.pallas_call(
        functools.partial(tile_kernel, carry is not None, last),
        out_shape=[jax.ShapeDtypeStruct((rows, cols), kind) for cols, kind in outs],
        grid_spec=pltpu.PrefetchScalarGridSpec(
            num_scalar_prefetch=1,
            grid=(rows // ROW_TILE,),
            in_specs=specs,
            out_specs=[by_row(cols) for cols, _ in outs],
            scratch_shapes=[] if keep else [pltpu.VMEM((ROW_TILE, rows), jnp.bfloat16)],
        ),
        compiler_params=pltpu.CompilerParams(vmem_limit_bytes=VMEM_LIMIT),
        cost_estimate=pl.CostEstimate(flops=rows * clust, bytes_accessed=rows * clust, transcendentals=0),
        name="tile",
    )(pick, *args)


def put_to(ref):
    def put(lanes, value):
        ref[:, lanes] = value

    return put


def run_tiles(rows, plan, total, acc):
    for word, (other, y), tile in plan:
        total = weights(cosines(rows, other), word, total, put_to(tile))
        acc = acc + jnp.dot(tile[...], y, preferred_element_type=jnp.float32)
    return total, acc


def hub_blocks(near_ref, far_ref, width):
    near, far = near_ref[:, 0].reshape(-1, near_ref.shape[3]), flat(far_ref)
    return (near[:, :width], near[:, width:]), (far[:, :width], far[:, width:])


def hub_specs(near, far):
    chips, _, piece, full = near.shape
    once = pl.Buffered(1)
    return [
        pl.BlockSpec((chips, 1, piece, full), lambda r, pick: (0, 0, 0, 0), pipeline_mode=once),
        pl.BlockSpec((chips, piece, full), lambda r, pick: (0, 0, 0), pipeline_mode=once),
    ]


def two_kernel(pick_ref, rows_ref, near_ref, far_ref, words_ref, deg_in, acc_in, near_tile, far_tile, deg_ref, acc_ref):
    near, far = hub_blocks(near_ref, far_ref, rows_ref.shape[1])
    plan = (
        (words_ref[pick_ref[0]], near, near_tile),
        (words_ref[5 - pick_ref[0]], far, far_tile),
    )
    deg_ref[...], acc_ref[...] = run_tiles(rows_ref[...], plan, deg_in[...], acc_in[...])


def two_of(pick, own_rows, near, far, words, carry):
    rows, width = own_rows.shape
    clust = carry[1].shape[1]
    by_row = lambda cols: pl.BlockSpec((ROW_TILE, cols), lambda r, pick: (r, 0))
    by_word = pl.BlockSpec((K, ROW_TILE, LANES), lambda r, pick: (0, r, 0))
    outs = [(rows, jnp.bfloat16)] * 2 + [(LANES, jnp.float32), (clust, jnp.float32)]
    return pl.pallas_call(
        two_kernel,
        out_shape=[jax.ShapeDtypeStruct((rows, cols), kind) for cols, kind in outs],
        grid_spec=pltpu.PrefetchScalarGridSpec(
            num_scalar_prefetch=1,
            grid=(rows // ROW_TILE,),
            in_specs=[by_row(width), *hub_specs(near, far), by_word, by_row(LANES), by_row(clust)],
            out_specs=[by_row(cols) for cols, _ in outs],
        ),
        compiler_params=pltpu.CompilerParams(vmem_limit_bytes=VMEM_LIMIT),
        cost_estimate=pl.CostEstimate(flops=rows * clust, bytes_accessed=rows * clust, transcendentals=0),
        name="two",
    )(pick, own_rows, near, far, words, *carry)


def finish_kernel(pick_ref, *refs):
    blocks, refs = refs[:BLOCKS_NEAR], refs[BLOCKS_NEAR:]
    rows_ref, first_y, second_y, near_ref, far_ref, own_ref, member_ref, deg_in, acc_in, anchor_ref = refs[:10]
    own_tile, near_tile, far_tile, near_new, far_new, out_ref = refs[10:16]
    member_tile, degree, new, other_new, first_x, second_x, held, spare, sems = refs[16:]
    phase, step = pl.program_id(0), pl.program_id(1)
    here = pl.ds(pl.multiple_of(step * ROW_TILE, ROW_TILE), ROW_TILE)

    @pl.when((phase == 0) & (step == 0))
    def _():
        for which, target in enumerate((first_x, second_x)):
            for i, block in enumerate(blocks):

                @pl.when(pick_ref[1 + which] == i)
                def _():
                    copy = pltpu.make_async_copy(block, target, sems.at[which])
                    copy.start()
                    copy.wait()

    @pl.when(phase == 0)
    def _():
        first, second = (first_x[...], first_y[0]), (second_x[...], second_y[0])
        near, far = hub_blocks(near_ref, far_ref, rows_ref.shape[1])
        plan = ((own_ref[0], first, member_tile.at[here, :]),)
        total, acc = run_tiles(rows_ref[...], plan, deg_in[...], acc_in[...])
        degree[here, :] = total
        new[here, :] = mix(acc, jnp.sum(total, axis=1, keepdims=True), anchor_ref[...])
        plan = (
            (member_ref[pick_ref[3]], near, held),
            (member_ref[5 - pick_ref[3]], far, spare),
            (member_ref[0], first, held),
            (member_ref[1], second, spare),
        )
        zeros = lambda ref: jnp.zeros(ref.shape, jnp.float32)
        total, acc = run_tiles(first_x[here, :], plan, zeros(deg_in), zeros(acc_in))
        other_new[here, :] = mix(acc, jnp.sum(total, axis=1, keepdims=True), first_y[0, here, :])

    @pl.when(phase == 1)
    def _():
        pairs = ((own_tile[...], new), (member_tile[here, :], other_new), (near_tile[...], near_new), (far_tile[...], far_new))
        acc = sum(jnp.dot(tile, y[...], preferred_element_type=jnp.float32) for tile, y in pairs)
        out_ref[...] = mix(acc, jnp.sum(degree[here, :], axis=1, keepdims=True), anchor_ref[...])


def finish_of(pick, blocks, own_rows, rest, near, far, words, member_words, carry, anchor, tiles, news):
    rows, width = blocks[0].shape
    clust = rest.shape[2]
    steps = rows // ROW_TILE
    once = pl.Buffered(1)
    before = lambda p, r: jnp.where(p == 0, r, steps - 1)
    after = lambda p, r: jnp.where(p == 0, 0, r)
    by_row = lambda cols, row: pl.BlockSpec((ROW_TILE, cols), lambda p, r, pick: (row(p, r), 0))
    rest_at = lambda k: pl.BlockSpec((1, rows, clust), lambda p, r, pick: (pick[k], 0, 0), pipeline_mode=once)
    whole = pl.BlockSpec((rows, clust), lambda p, r, pick: (0, 0), pipeline_mode=once)
    chips, _, piece, full = near.shape
    return pl.pallas_call(
        finish_kernel,
        out_shape=jax.ShapeDtypeStruct((rows, clust), jnp.bfloat16),
        grid_spec=pltpu.PrefetchScalarGridSpec(
            num_scalar_prefetch=1,
            grid=(2, steps),
            in_specs=[pl.BlockSpec(memory_space=pl.ANY)] * len(blocks)
            + [
                by_row(width, before),
                rest_at(4),
                rest_at(5),
                pl.BlockSpec((chips, 1, piece, full), lambda p, r, pick: (0, 0, 0, 0), pipeline_mode=once),
                pl.BlockSpec((chips, piece, full), lambda p, r, pick: (0, 0, 0), pipeline_mode=once),
                pl.BlockSpec((1, ROW_TILE, LANES), lambda p, r, pick: (1, before(p, r), 0)),
                pl.BlockSpec((K, ROW_TILE, LANES), lambda p, r, pick: (0, before(p, r), 0)),
                by_row(LANES, before),
                by_row(clust, before),
                by_row(clust, lambda p, r: r),
            ]
            + [by_row(rows, after)] * 3
            + [whole] * 2,
            out_specs=by_row(clust, after),
            scratch_shapes=[
                pltpu.VMEM((rows, rows), jnp.bfloat16),
                pltpu.VMEM((rows, LANES), jnp.float32),
                pltpu.VMEM((rows, clust), jnp.bfloat16),
                pltpu.VMEM((rows, clust), jnp.bfloat16),
            ]
            + [pltpu.VMEM((rows, width), jnp.bfloat16)] * 2
            + [pltpu.VMEM((ROW_TILE, rows), jnp.bfloat16)] * 2
            + [pltpu.SemaphoreType.DMA((2,))],
        ),
        compiler_params=pltpu.CompilerParams(vmem_limit_bytes=VMEM_LIMIT),
        cost_estimate=pl.CostEstimate(
            flops=12 * rows * rows * 768, bytes_accessed=12 * rows * rows, transcendentals=5 * rows * rows
        ),
        name="finish",
    )(pick, *blocks, own_rows, rest, rest, near, far, words, member_words, *carry, anchor, *tiles, *news)


def hub_rows_kernel(width, pick_ref, rows_ref, near_ref, far_ref, out_ref, word_ref, tile_ref):
    clust = out_ref.shape[1]
    half = K * TOPK
    coded = rows_ref[:, width + clust :].astype(jnp.float32).astype(jnp.int32)
    high = coded[:, :half] & (HALF - 1)
    low = (high & 3) * HALF + coded[:, half:]
    bit = jnp.left_shift(jnp.ones_like(high), high >> 2)
    lane = lax.broadcasted_iota(jnp.int32, (rows_ref.shape[0], LANES), 1)
    for slot in range(K):
        word = jnp.zeros(lane.shape, jnp.int32)
        for t in range(slot * TOPK, (slot + 1) * TOPK):
            word = word | jnp.where(lane == low[:, t : t + 1], bit[:, t : t + 1], 0)
        word_ref[slot] = word
    total = jnp.zeros(lane.shape, jnp.float32)
    acc = jnp.zeros(out_ref.shape, jnp.float32)

    def put(lanes, value):
        tile_ref[:, lanes] = value

    self_block = near_ref[:, 0].reshape(-1, width + clust)
    member_block = near_ref[:, 1].reshape(-1, width + clust)
    far_block = flat(far_ref)
    slots = (0, 1, pick_ref[0], 5 - pick_ref[0])
    for slot, block in zip(slots, (self_block, member_block, self_block, far_block)):
        total = weights(cosines(rows_ref[:, :width], block[:, :width]), word_ref[slot], total, put)
        acc = acc + jnp.dot(tile_ref[...], block[:, width:], preferred_element_type=jnp.float32)
    out_ref[...] = mix(acc, jnp.sum(total, axis=1, keepdims=True), rows_ref[:, width : width + clust])


def hub_rows(self_slot, mine, near, far, width):
    share = mine.shape[0]
    clust = near.shape[3] - width
    rows = near.shape[0] * near.shape[2]
    return pl.pallas_call(
        functools.partial(hub_rows_kernel, width),
        out_shape=jax.ShapeDtypeStruct((share, clust), jnp.bfloat16),
        grid_spec=pltpu.PrefetchScalarGridSpec(
            num_scalar_prefetch=1,
            grid=(1,),
            in_specs=[
                pl.BlockSpec(mine.shape, lambda i, pick: (0, 0)),
                pl.BlockSpec(near.shape, lambda i, pick: (0, 0, 0, 0)),
                pl.BlockSpec(far.shape, lambda i, pick: (0, 0, 0)),
            ],
            out_specs=pl.BlockSpec((share, clust), lambda i, pick: (0, 0)),
            scratch_shapes=[pltpu.VMEM((K, share, LANES), jnp.int32), pltpu.VMEM((share, rows), jnp.bfloat16)],
        ),
        compiler_params=pltpu.CompilerParams(vmem_limit_bytes=VMEM_LIMIT),
        cost_estimate=pl.CostEstimate(flops=rows, bytes_accessed=rows, transcendentals=0),
        name="hub_rows",
    )(self_slot, mine, near, far)


def send(block, target):
    slabs, reps = lax.axis_size("slab"), lax.axis_size("rep")
    chips = slabs // 4
    pairs = []
    for device in range(slabs * reps):
        slab, rep = divmod(device, reps)
        to = target(slab // (2 * chips), slab // 2 % chips, slab % 2, rep)
        if to is not None:
            pairs.append((device, ((to[0] * chips + to[1]) * 2 + to[2]) * reps + to[3]))
    return lax.ppermute(block, AXES, pairs)


def along_line(block, table):
    return send(
        block, lambda half, chip, core, rep: (half, chip, core, table[rep]) if rep in table else None
    )


def swap_cores(block):
    return send(block, lambda half, chip, core, rep: (half, chip, 1 - core, rep))


def flags_of(code):
    flag = code.astype(jnp.float32).astype(jnp.int32) // HALF
    return flag & 3, (flag >> 2) & 1


def join_pieces(piece):
    slabs = lax.axis_size("slab")
    members, chips = slabs // 2, slabs // 4
    layers = [[h * members + c * 2 + core for c in range(chips)] for h in range(2) for core in range(2)]
    repeated = jnp.broadcast_to(piece[None], (chips,) + piece.shape)
    return lax.all_to_all(repeated, "slab", 0, 0, axis_index_groups=layers, tiled=True)


OUTWARD = {1: 0, 2: 3}
MIDDLE = {1: 2, 2: 1}


def spread_line(block):
    across = along_line(block, {0: 2, 2: 0, 1: 3, 3: 1})
    beside = along_line(block, {0: 1, 1: 0, 2: 3, 3: 2})
    return across, beside


def scatter(block):
    members = lax.axis_size("slab") // 2
    rows, width = block.shape
    planes = [[h * members + m for m in range(members)] for h in range(2)]
    return lax.all_to_all(
        block.reshape(members, rows // members, width), "slab", 0, 0, axis_index_groups=planes, tiled=True
    )


def hub_candidates(mine, hub_ids):
    members, reps = lax.axis_size("slab") // 2, lax.axis_size("rep")
    slab = lax.axis_index("slab")
    hub_slab, hub_rep = lax.div(hub_ids, reps), lax.rem(hub_ids, reps)
    member = lax.rem(hub_slab, members)
    held = jnp.stack(
        [lax.dynamic_index_in_dim(mine, member[h], 0, keepdims=False) for h in range(HUBS)], axis=0
    )
    got = send(held, lambda half, chip, core, rep: (1 - half, chip, core, rep))
    away = lax.div(hub_slab, members) != lax.div(slab, members)
    held = jnp.where(away[:, None, None], got, held)[None]
    rep = lax.axis_index("rep")
    for bit in range(2):
        got = along_line(held, {r: r ^ (1 << bit) for r in range(4)})
        upper = (rep >> bit) & 1 == 1
        held = jnp.concatenate([jnp.where(upper, got, held), jnp.where(upper, held, got)], axis=0)
    return held, hub_rep


def hub_share(held, hub_rep, code_at):
    slab = lax.axis_index("slab")
    pick = lambda pieces, at: jnp.where(
        at < 2, jnp.where(at == 0, pieces[0], pieces[1]), jnp.where(at == 2, pieces[2], pieces[3])
    )
    chosen = []
    for h in range(HUBS):
        hub = pick(held[:, h], hub_rep[h])
        want, _ = flags_of(hub[:1, code_at : code_at + 1])
        chosen.append(jnp.stack([hub, pick(held[:, h], want)], axis=0))
    held = jnp.stack(chosen, axis=0)
    first_core = lax.rem(slab, 2) == 0
    keep = jnp.where(first_core, held[0], held[1])
    got = swap_cores(jnp.where(first_core, held[1], held[0]))
    return jnp.concatenate([jnp.where(first_core, keep, got), jnp.where(first_core, got, keep)], axis=1)


def body(embeddings, indicators, neighbours, hub_ids, columns):
    rows, width = embeddings.shape
    clust = indicators.shape[1]
    full = width + clust
    reps = lax.axis_size("rep")
    total = lax.axis_size("slab") * reps
    rep = lax.axis_index("rep")
    steps = rows // ROW_TILE
    slots = neighbours[0].astype(jnp.int32)
    want = slots[1] & 3
    order = slots[2] - total
    core = lax.rem(lax.axis_index("slab"), 2)
    near_slot = jnp.where(order == core, 2, 3)
    barrier = lax.optimization_barrier

    joined, normed, rest = join(total, neighbours.reshape(-1), embeddings, indicators, columns)
    across, beside = spread_line(rest)

    pick = jnp.stack([near_slot]).astype(jnp.int32)
    own_rows = (joined, (ROW_TILE, width), lambda r, pick: (r, 0))
    own_x = (joined, (rows, width), lambda r, pick: (0, 0))
    own_y = (joined, (rows, clust), lambda r, pick: (0, width // clust))
    words = keep_words(pick, rest[None], lambda pick: 0, rows, 1)
    *carry, own_tile = tile_of(pick, own_rows, own_x, own_y, words, lambda pick: 0)
    mine, words, carry, own_tile, rest, across, beside = barrier(
        (scatter(joined), words, carry, own_tile, rest, across, beside)
    )

    held, hub_rep = hub_candidates(mine, hub_ids)
    held, normed, rest, across = barrier((held, normed, rest, across))

    outer, middle = along_line(across, OUTWARD), along_line(rest, MIDDLE)
    across_x, beside_x = spread_line(normed)
    both = hub_share(held, hub_rep, full)
    near = join_pieces(both[:, :, :full])
    at_end = (rep == 0) | (rep == 3)
    group_rest = jnp.stack([rest, beside, across, jnp.where(at_end, outer, middle)], axis=0)
    at = want ^ rep
    flag = lax.dynamic_index_in_dim(group_rest[:, -1, 0], at, 0, keepdims=False).astype(jnp.int32)
    member_want, member_order = flag & 3, (flag >> 2) & 1
    second = member_want ^ rep
    place = lambda k: jnp.where((k == 3) & at_end, 4, k)
    pick = jnp.stack(
        [near_slot, place(at), place(second), jnp.where(member_order == core, 2, 3), at, second]
    ).astype(jnp.int32)
    member_words = keep_words(pick, group_rest, lambda pick: pick[4], rows, WORDS_HINT)
    near, group_rest, member_words, pick, normed, across_x, beside_x = barrier(
        (near, group_rest, member_words, pick, normed, across_x, beside_x)
    )

    far = swap_cores(near[:, 0])
    outer_x, middle_x = along_line(across_x, OUTWARD), along_line(normed, MIDDLE)
    _, hub_order = flags_of(both[0, 0, full])
    share = hub_rows(jnp.where(hub_order == core, 2, 3)[None], both[0], near, far, width)
    share, near, far = barrier((share, near, far))
    near_new = join_pieces(share).reshape(rows, clust)
    near_tile, far_tile, *carry = two_of(pick, normed, near, far, words, carry)
    near_new, carry = barrier((near_new, carry))
    far_new = swap_cores(near_new)
    near_new, far_new, outer_x, middle_x = barrier((near_new, far_new, outer_x, middle_x))

    return finish_of(
        pick, (normed, beside_x, across_x, middle_x, outer_x), normed, group_rest, near, far, words, member_words,
        carry, indicators, (own_tile, near_tile, far_tile), (near_new, far_new),
    )


def solution(mesh):
    return jax.shard_map(
        body,
        mesh=mesh,
        in_specs=(
            P(("slab", "rep"), None),
            P(("slab", "rep"), None),
            P(("slab", "rep"), None),
            P(),
            P(("slab", "rep"), None, None),
        ),
        out_specs=P(("slab", "rep"), None),
        check_vma=False,
    )
```

```python
import functools

import jax
import jax.numpy as jnp
from jax import lax
from jax.experimental import pallas as pl
from jax.experimental.pallas import tpu as pltpu
from jax.sharding import PartitionSpec as P

K = 4
HUBS = 2
TOPK = 16
LANES = 128
EPS = 1e-06
TAU = 0.04
ALPHA = 0.8
AXES = ("slab", "rep")
ROW_TILE = 256
VMEM_LIMIT = 58 << 20
SCALE = 1.4426950408889634 / TAU
HALF = 32
FLAG_ROWS = 16
BLOCKS_NEAR = 5
WORDS_HINT = 30_000_000_000


def join_kernel(blocks, near_ref, x_ref, y_ref, cols_ref, all_ref, normed_ref, rest_ref):
    width, clust = x_ref.shape[1], y_ref.shape[1]
    step = pl.program_id(0)
    rows = pl.num_programs(0) * ROW_TILE
    values = x_ref[...].astype(jnp.float32)
    scale = lax.rsqrt(jnp.sum(values * values, axis=1, keepdims=True) + EPS)
    normed = (values * scale).astype(jnp.bfloat16)
    cols = cols_ref[...].reshape(K * TOPK, cols_ref.shape[2])
    flag = (near_ref[1] & 3) + 4 * (near_ref[2] - blocks)
    coded = jnp.concatenate([(cols >> 5) + HALF * flag, cols & (HALF - 1)], axis=0)
    all_ref[:, :width] = normed
    all_ref[:, width : width + clust] = y_ref[...]
    all_ref[:, width + clust :] = coded.astype(jnp.float32).T.astype(jnp.bfloat16)
    normed_ref[...] = normed
    rest_ref[pl.ds(pl.multiple_of(step * ROW_TILE, ROW_TILE), ROW_TILE), :] = y_ref[...]
    single = jnp.left_shift((cols & (LANES - 1)) + LANES, cols >> 7)
    place = pl.multiple_of(rows + step * K * TOPK, K * TOPK)
    rest_ref[pl.ds(place, K * TOPK), :] = single.astype(jnp.float32).astype(jnp.bfloat16)
    flags = jnp.full((FLAG_ROWS, clust), flag, jnp.int32)
    rest_ref[rows + rows // ROW_TILE * K * TOPK :, :] = flags.astype(jnp.float32).astype(jnp.bfloat16)


def join(blocks, near, embeddings, indicators, columns):
    rows, width = embeddings.shape
    clust = indicators.shape[1]
    by_row = lambda cols: pl.BlockSpec((ROW_TILE, cols), lambda r, flag: (r, 0))
    steps = rows // ROW_TILE
    rest = (rows + steps * K * TOPK + FLAG_ROWS, clust)
    return pl.pallas_call(
        functools.partial(join_kernel, blocks),
        out_shape=[
            jax.ShapeDtypeStruct(shape, jnp.bfloat16)
            for shape in ((rows, width + clust + 2 * K * TOPK), (rows, width), rest)
        ],
        grid_spec=pltpu.PrefetchScalarGridSpec(
            num_scalar_prefetch=1,
            grid=(steps,),
            in_specs=[
                by_row(width),
                by_row(clust),
                pl.BlockSpec((K, TOPK, ROW_TILE), lambda r, flag: (0, 0, r)),
            ],
            out_specs=[by_row(width + clust + 2 * K * TOPK), by_row(width), pl.BlockSpec(rest, lambda r, flag: (0, 0))],
        ),
        compiler_params=pltpu.CompilerParams(vmem_limit_bytes=VMEM_LIMIT),
        name="join",
    )(near, embeddings, indicators, jnp.transpose(columns, (1, 2, 0)))


def words_kernel(pick_ref, coded_ref, out_ref):
    lane = lax.broadcasted_iota(jnp.int32, (LANES, LANES), 0)
    for step in range(coded_ref.shape[1] // (K * TOPK)):
        coded = coded_ref[0, step * K * TOPK : (step + 1) * K * TOPK].astype(jnp.float32).astype(jnp.int32)
        high = sum((coded >= LANES << m).astype(jnp.int32) for m in range(1, 8))
        low = jnp.right_shift(coded, high) & (LANES - 1)
        bit = jnp.left_shift(jnp.ones_like(high), high)
        for part in range(ROW_TILE // LANES):
            here = slice(part * LANES, (part + 1) * LANES)
            for slot in range(K):
                word = jnp.zeros((LANES, LANES), jnp.int32)
                for t in range(slot * TOPK, (slot + 1) * TOPK):
                    word = word | jnp.where(lane == low[t : t + 1, here], bit[t : t + 1, here], 0)
                start = step * ROW_TILE + part * LANES
                out_ref[slot, start : start + LANES, :] = word.T


def keep_words(pick, rest, which, rows, hint):
    part = rows // ROW_TILE * K * TOPK
    clust = rest.shape[2]
    return pl.pallas_call(
        words_kernel,
        out_shape=jax.ShapeDtypeStruct((K, rows, LANES), jnp.int32),
        grid_spec=pltpu.PrefetchScalarGridSpec(
            num_scalar_prefetch=1,
            grid=(1,),
            in_specs=[pl.BlockSpec((1, part, clust), lambda i, pick: (which(pick), rows // part, 0))],
            out_specs=pl.BlockSpec((K, rows, LANES), lambda i, pick: (0, 0, 0)),
        ),
        compiler_params=pltpu.CompilerParams(vmem_limit_bytes=VMEM_LIMIT),
        cost_estimate=pl.CostEstimate(flops=hint, bytes_accessed=rows * 512, transcendentals=0),
        name="keep_words",
    )(pick, rest)


def mix(acc, degree, anchor):
    return (ALPHA * acc / degree + (1.0 - ALPHA) * anchor.astype(jnp.float32)).astype(jnp.bfloat16)


def weights(cosine, word, total, put):
    for j in range(cosine.shape[1] // LANES):
        part = cosine[:, j * LANES : (j + 1) * LANES]
        raw = jnp.where((word & (1 << j)) != 0, jnp.exp2(part * SCALE - SCALE), 0.0)
        total = total + raw
        put(slice(j * LANES, (j + 1) * LANES), raw.astype(jnp.bfloat16))
    return total


def cosines(rows, others):
    return lax.dot_general(rows, others, (((1,), (1,)), ((), ())), preferred_element_type=jnp.float32)


def flat(ref):
    value = ref[...]
    return value.reshape(-1, value.shape[-1])


def tile_kernel(has_carry, last, pick_ref, x_ref, other_ref, w_ref, y_ref, *refs):
    refs = list(refs)
    deg_in, acc_in = (refs.pop(0), refs.pop(0)) if has_carry else (None, None)
    anchor_ref = refs.pop(0) if last else None
    deg_ref, acc_ref, tile_ref = refs
    word = w_ref[0]
    total = deg_in[...] if has_carry else jnp.zeros(word.shape, jnp.float32)

    def put(lanes, value):
        tile_ref[:, lanes] = value

    total = weights(cosines(x_ref[...], flat(other_ref)), word, total, put)
    deg_ref[...] = total
    gathered = jnp.dot(tile_ref[...], flat(y_ref), preferred_element_type=jnp.float32)
    if has_carry:
        gathered = acc_in[...] + gathered
    if last:
        gathered = mix(gathered, jnp.sum(total, axis=1, keepdims=True), anchor_ref[...])
    acc_ref[...] = gathered


def tile_of(pick, x, other, y, words, slot, carry=None, anchor=None, keep=True):
    rows, clust = words.shape[1], y[1][-1]
    by_row = lambda cols: pl.BlockSpec((ROW_TILE, cols), lambda r, pick: (r, 0))
    spec = lambda operand: pl.BlockSpec(operand[1], operand[2])
    last = anchor is not None
    args = [x[0], other[0], words, y[0], *(carry or ())] + ([anchor[0]] if last else [])
    specs = [spec(x), spec(other), pl.BlockSpec((1, ROW_TILE, LANES), lambda r, pick: (slot(pick), r, 0)), spec(y)]
    specs += ([by_row(LANES), by_row(clust)] if carry else []) + ([spec(anchor)] if last else [])
    outs = [(LANES, jnp.float32), (clust, jnp.bfloat16 if last else jnp.float32)] + [(rows, jnp.bfloat16)] * keep
    return pl.pallas_call(
        functools.partial(tile_kernel, carry is not None, last),
        out_shape=[jax.ShapeDtypeStruct((rows, cols), kind) for cols, kind in outs],
        grid_spec=pltpu.PrefetchScalarGridSpec(
            num_scalar_prefetch=1,
            grid=(rows // ROW_TILE,),
            in_specs=specs,
            out_specs=[by_row(cols) for cols, _ in outs],
            scratch_shapes=[] if keep else [pltpu.VMEM((ROW_TILE, rows), jnp.bfloat16)],
        ),
        compiler_params=pltpu.CompilerParams(vmem_limit_bytes=VMEM_LIMIT),
        cost_estimate=pl.CostEstimate(flops=rows * clust, bytes_accessed=rows * clust, transcendentals=0),
        name="tile",
    )(pick, *args)


def put_to(ref):
    def put(lanes, value):
        ref[:, lanes] = value

    return put


def run_tiles(rows, plan, total, acc):
    for word, (other, y), tile in plan:
        total = weights(cosines(rows, other), word, total, put_to(tile))
        acc = acc + jnp.dot(tile[...], y, preferred_element_type=jnp.float32)
    return total, acc


def hub_blocks(near_ref, far_ref, width):
    near, far = near_ref[:, 0].reshape(-1, near_ref.shape[3]), flat(far_ref)
    return (near[:, :width], near[:, width:]), (far[:, :width], far[:, width:])


def hub_specs(near, far):
    chips, _, piece, full = near.shape
    once = pl.Buffered(1)
    return [
        pl.BlockSpec((chips, 1, piece, full), lambda r, pick: (0, 0, 0, 0), pipeline_mode=once),
        pl.BlockSpec((chips, piece, full), lambda r, pick: (0, 0, 0), pipeline_mode=once),
    ]


def two_kernel(pick_ref, rows_ref, near_ref, far_ref, words_ref, deg_in, acc_in, near_tile, far_tile, deg_ref, acc_ref):
    near, far = hub_blocks(near_ref, far_ref, rows_ref.shape[1])
    plan = (
        (words_ref[pick_ref[0]], near, near_tile),
        (words_ref[5 - pick_ref[0]], far, far_tile),
    )
    deg_ref[...], acc_ref[...] = run_tiles(rows_ref[...], plan, deg_in[...], acc_in[...])


def two_of(pick, own_rows, near, far, words, carry):
    rows, width = own_rows.shape
    clust = carry[1].shape[1]
    by_row = lambda cols: pl.BlockSpec((ROW_TILE, cols), lambda r, pick: (r, 0))
    by_word = pl.BlockSpec((K, ROW_TILE, LANES), lambda r, pick: (0, r, 0))
    outs = [(rows, jnp.bfloat16)] * 2 + [(LANES, jnp.float32), (clust, jnp.float32)]
    return pl.pallas_call(
        two_kernel,
        out_shape=[jax.ShapeDtypeStruct((rows, cols), kind) for cols, kind in outs],
        grid_spec=pltpu.PrefetchScalarGridSpec(
            num_scalar_prefetch=1,
            grid=(rows // ROW_TILE,),
            in_specs=[by_row(width), *hub_specs(near, far), by_word, by_row(LANES), by_row(clust)],
            out_specs=[by_row(cols) for cols, _ in outs],
        ),
        compiler_params=pltpu.CompilerParams(vmem_limit_bytes=VMEM_LIMIT),
        cost_estimate=pl.CostEstimate(flops=rows * clust, bytes_accessed=rows * clust, transcendentals=0),
        name="two",
    )(pick, own_rows, near, far, words, *carry)


def finish_kernel(pick_ref, *refs):
    blocks, refs = refs[:BLOCKS_NEAR], refs[BLOCKS_NEAR:]
    rows_ref, first_y, second_y, near_ref, far_ref, own_ref, member_ref, deg_in, acc_in, anchor_ref = refs[:10]
    own_tile, near_tile, far_tile, near_new, far_new, out_ref = refs[10:16]
    member_tile, degree, new, other_new, first_x, second_x, held, spare, sems = refs[16:]
    phase, step = pl.program_id(0), pl.program_id(1)
    here = pl.ds(pl.multiple_of(step * ROW_TILE, ROW_TILE), ROW_TILE)

    @pl.when((phase == 0) & (step == 0))
    def _():
        for which, target in enumerate((first_x, second_x)):
            for i, block in enumerate(blocks):

                @pl.when(pick_ref[1 + which] == i)
                def _():
                    copy = pltpu.make_async_copy(block, target, sems.at[which])
                    copy.start()
                    copy.wait()

    @pl.when(phase == 0)
    def _():
        first, second = (first_x[...], first_y[0]), (second_x[...], second_y[0])
        near, far = hub_blocks(near_ref, far_ref, rows_ref.shape[1])
        plan = ((own_ref[0], first, member_tile.at[here, :]),)
        total, acc = run_tiles(rows_ref[...], plan, deg_in[...], acc_in[...])
        degree[here, :] = total
        new[here, :] = mix(acc, jnp.sum(total, axis=1, keepdims=True), anchor_ref[...])
        plan = (
            (member_ref[pick_ref[3]], near, held),
            (member_ref[5 - pick_ref[3]], far, spare),
            (member_ref[0], first, held),
            (member_ref[1], second, spare),
        )
        zeros = lambda ref: jnp.zeros(ref.shape, jnp.float32)
        total, acc = run_tiles(first_x[here, :], plan, zeros(deg_in), zeros(acc_in))
        other_new[here, :] = mix(acc, jnp.sum(total, axis=1, keepdims=True), first_y[0, here, :])

    @pl.when(phase == 1)
    def _():
        pairs = ((own_tile[...], new), (member_tile[here, :], other_new), (near_tile[...], near_new), (far_tile[...], far_new))
        acc = sum(jnp.dot(tile, y[...], preferred_element_type=jnp.float32) for tile, y in pairs)
        out_ref[...] = mix(acc, jnp.sum(degree[here, :], axis=1, keepdims=True), anchor_ref[...])


def finish_of(pick, blocks, own_rows, rest, near, far, words, member_words, carry, anchor, tiles, news):
    rows, width = blocks[0].shape
    clust = rest.shape[2]
    steps = rows // ROW_TILE
    once = pl.Buffered(1)
    before = lambda p, r: jnp.where(p == 0, r, steps - 1)
    after = lambda p, r: jnp.where(p == 0, 0, r)
    by_row = lambda cols, row: pl.BlockSpec((ROW_TILE, cols), lambda p, r, pick: (row(p, r), 0))
    rest_at = lambda k: pl.BlockSpec((1, rows, clust), lambda p, r, pick: (pick[k], 0, 0), pipeline_mode=once)
    whole = pl.BlockSpec((rows, clust), lambda p, r, pick: (0, 0), pipeline_mode=once)
    chips, _, piece, full = near.shape
    return pl.pallas_call(
        finish_kernel,
        out_shape=jax.ShapeDtypeStruct((rows, clust), jnp.bfloat16),
        grid_spec=pltpu.PrefetchScalarGridSpec(
            num_scalar_prefetch=1,
            grid=(2, steps),
            in_specs=[pl.BlockSpec(memory_space=pl.ANY)] * len(blocks)
            + [
                by_row(width, before),
                rest_at(4),
                rest_at(5),
                pl.BlockSpec((chips, 1, piece, full), lambda p, r, pick: (0, 0, 0, 0), pipeline_mode=once),
                pl.BlockSpec((chips, piece, full), lambda p, r, pick: (0, 0, 0), pipeline_mode=once),
                pl.BlockSpec((1, ROW_TILE, LANES), lambda p, r, pick: (1, before(p, r), 0)),
                pl.BlockSpec((K, ROW_TILE, LANES), lambda p, r, pick: (0, before(p, r), 0)),
                by_row(LANES, before),
                by_row(clust, before),
                by_row(clust, lambda p, r: r),
            ]
            + [by_row(rows, after)] * 3
            + [whole] * 2,
            out_specs=by_row(clust, after),
            scratch_shapes=[
                pltpu.VMEM((rows, rows), jnp.bfloat16),
                pltpu.VMEM((rows, LANES), jnp.float32),
                pltpu.VMEM((rows, clust), jnp.bfloat16),
                pltpu.VMEM((rows, clust), jnp.bfloat16),
            ]
            + [pltpu.VMEM((rows, width), jnp.bfloat16)] * 2
            + [pltpu.VMEM((ROW_TILE, rows), jnp.bfloat16)] * 2
            + [pltpu.SemaphoreType.DMA((2,))],
        ),
        compiler_params=pltpu.CompilerParams(vmem_limit_bytes=VMEM_LIMIT),
        cost_estimate=pl.CostEstimate(
            flops=12 * rows * rows * 768, bytes_accessed=12 * rows * rows, transcendentals=5 * rows * rows
        ),
        name="finish",
    )(pick, *blocks, own_rows, rest, rest, near, far, words, member_words, *carry, anchor, *tiles, *news)


def hub_rows_kernel(width, pick_ref, rows_ref, near_ref, far_ref, out_ref, word_ref, tile_ref):
    clust = out_ref.shape[1]
    half = K * TOPK
    coded = rows_ref[:, width + clust :].astype(jnp.float32).astype(jnp.int32)
    high = coded[:, :half] & (HALF - 1)
    low = (high & 3) * HALF + coded[:, half:]
    bit = jnp.left_shift(jnp.ones_like(high), high >> 2)
    lane = lax.broadcasted_iota(jnp.int32, (rows_ref.shape[0], LANES), 1)
    for slot in range(K):
        word = jnp.zeros(lane.shape, jnp.int32)
        for t in range(slot * TOPK, (slot + 1) * TOPK):
            word = word | jnp.where(lane == low[:, t : t + 1], bit[:, t : t + 1], 0)
        word_ref[slot] = word
    total = jnp.zeros(lane.shape, jnp.float32)
    acc = jnp.zeros(out_ref.shape, jnp.float32)

    def put(lanes, value):
        tile_ref[:, lanes] = value

    self_block = near_ref[:, 0].reshape(-1, width + clust)
    member_block = near_ref[:, 1].reshape(-1, width + clust)
    far_block = flat(far_ref)
    slots = (0, 1, pick_ref[0], 5 - pick_ref[0])
    for slot, block in zip(slots, (self_block, member_block, self_block, far_block)):
        total = weights(cosines(rows_ref[:, :width], block[:, :width]), word_ref[slot], total, put)
        acc = acc + jnp.dot(tile_ref[...], block[:, width:], preferred_element_type=jnp.float32)
    out_ref[...] = mix(acc, jnp.sum(total, axis=1, keepdims=True), rows_ref[:, width : width + clust])


def hub_rows(self_slot, mine, near, far, width):
    share = mine.shape[0]
    clust = near.shape[3] - width
    rows = near.shape[0] * near.shape[2]
    return pl.pallas_call(
        functools.partial(hub_rows_kernel, width),
        out_shape=jax.ShapeDtypeStruct((share, clust), jnp.bfloat16),
        grid_spec=pltpu.PrefetchScalarGridSpec(
            num_scalar_prefetch=1,
            grid=(1,),
            in_specs=[
                pl.BlockSpec(mine.shape, lambda i, pick: (0, 0)),
                pl.BlockSpec(near.shape, lambda i, pick: (0, 0, 0, 0)),
                pl.BlockSpec(far.shape, lambda i, pick: (0, 0, 0)),
            ],
            out_specs=pl.BlockSpec((share, clust), lambda i, pick: (0, 0)),
            scratch_shapes=[pltpu.VMEM((K, share, LANES), jnp.int32), pltpu.VMEM((share, rows), jnp.bfloat16)],
        ),
        compiler_params=pltpu.CompilerParams(vmem_limit_bytes=VMEM_LIMIT),
        cost_estimate=pl.CostEstimate(flops=rows, bytes_accessed=rows, transcendentals=0),
        name="hub_rows",
    )(self_slot, mine, near, far)


def send(block, target):
    slabs, reps = lax.axis_size("slab"), lax.axis_size("rep")
    chips = slabs // 4
    pairs = []
    for device in range(slabs * reps):
        slab, rep = divmod(device, reps)
        to = target(slab // (2 * chips), slab // 2 % chips, slab % 2, rep)
        if to is not None:
            pairs.append((device, ((to[0] * chips + to[1]) * 2 + to[2]) * reps + to[3]))
    return lax.ppermute(block, AXES, pairs)


def along_line(block, table):
    return send(
        block, lambda half, chip, core, rep: (half, chip, core, table[rep]) if rep in table else None
    )


def swap_cores(block):
    return send(block, lambda half, chip, core, rep: (half, chip, 1 - core, rep))


def flags_of(code):
    flag = code.astype(jnp.float32).astype(jnp.int32) // HALF
    return flag & 3, (flag >> 2) & 1


def join_pieces(piece):
    slabs = lax.axis_size("slab")
    members, chips = slabs // 2, slabs // 4
    layers = [[h * members + c * 2 + core for c in range(chips)] for h in range(2) for core in range(2)]
    repeated = jnp.broadcast_to(piece[None], (chips,) + piece.shape)
    return lax.all_to_all(repeated, "slab", 0, 0, axis_index_groups=layers, tiled=True)


OUTWARD = {1: 0, 2: 3}
MIDDLE = {1: 2, 2: 1}


def spread_line(block):
    across = along_line(block, {0: 2, 2: 0, 1: 3, 3: 1})
    beside = along_line(block, {0: 1, 1: 0, 2: 3, 3: 2})
    return across, beside


def scatter(block):
    members = lax.axis_size("slab") // 2
    rows, width = block.shape
    planes = [[h * members + m for m in range(members)] for h in range(2)]
    return lax.all_to_all(
        block.reshape(members, rows // members, width), "slab", 0, 0, axis_index_groups=planes, tiled=True
    )


def hub_candidates(mine, hub_ids):
    members, reps = lax.axis_size("slab") // 2, lax.axis_size("rep")
    slab = lax.axis_index("slab")
    hub_slab, hub_rep = lax.div(hub_ids, reps), lax.rem(hub_ids, reps)
    member = lax.rem(hub_slab, members)
    held = jnp.stack(
        [lax.dynamic_index_in_dim(mine, member[h], 0, keepdims=False) for h in range(HUBS)], axis=0
    )
    got = send(held, lambda half, chip, core, rep: (1 - half, chip, core, rep))
    away = lax.div(hub_slab, members) != lax.div(slab, members)
    held = jnp.where(away[:, None, None], got, held)[None]
    rep = lax.axis_index("rep")
    for bit in range(2):
        got = along_line(held, {r: r ^ (1 << bit) for r in range(4)})
        upper = (rep >> bit) & 1 == 1
        held = jnp.concatenate([jnp.where(upper, got, held), jnp.where(upper, held, got)], axis=0)
    return held, hub_rep


def hub_share(held, hub_rep, code_at):
    slab = lax.axis_index("slab")
    pick = lambda pieces, at: jnp.where(
        at < 2, jnp.where(at == 0, pieces[0], pieces[1]), jnp.where(at == 2, pieces[2], pieces[3])
    )
    chosen = []
    for h in range(HUBS):
        hub = pick(held[:, h], hub_rep[h])
        want, _ = flags_of(hub[:1, code_at : code_at + 1])
        chosen.append(jnp.stack([hub, pick(held[:, h], want)], axis=0))
    held = jnp.stack(chosen, axis=0)
    first_core = lax.rem(slab, 2) == 0
    keep = jnp.where(first_core, held[0], held[1])
    got = swap_cores(jnp.where(first_core, held[1], held[0]))
    return jnp.concatenate([jnp.where(first_core, keep, got), jnp.where(first_core, got, keep)], axis=1)


def body(embeddings, indicators, neighbours, hub_ids, columns):
    rows, width = embeddings.shape
    clust = indicators.shape[1]
    full = width + clust
    reps = lax.axis_size("rep")
    total = lax.axis_size("slab") * reps
    rep = lax.axis_index("rep")
    steps = rows // ROW_TILE
    slots = neighbours[0].astype(jnp.int32)
    want = slots[1] & 3
    order = slots[2] - total
    core = lax.rem(lax.axis_index("slab"), 2)
    near_slot = jnp.where(order == core, 2, 3)
    barrier = lax.optimization_barrier

    joined, normed, rest = join(total, neighbours.reshape(-1), embeddings, indicators, columns)
    across, beside = spread_line(rest)

    pick = jnp.stack([near_slot]).astype(jnp.int32)
    own_rows = (joined, (ROW_TILE, width), lambda r, pick: (r, 0))
    own_x = (joined, (rows, width), lambda r, pick: (0, 0))
    own_y = (joined, (rows, clust), lambda r, pick: (0, width // clust))
    words = keep_words(pick, rest[None], lambda pick: 0, rows, 1)
    *carry, own_tile = tile_of(pick, own_rows, own_x, own_y, words, lambda pick: 0)
    mine, words, carry, own_tile, rest, across, beside = barrier(
        (scatter(joined), words, carry, own_tile, rest, across, beside)
    )

    held, hub_rep = hub_candidates(mine, hub_ids)
    held, normed, rest, across = barrier((held, normed, rest, across))

    middle, outer = along_line(rest, MIDDLE), along_line(across, OUTWARD)
    beside_x = along_line(normed, {0: 1, 1: 0, 2: 3, 3: 2})
    across_x = along_line(normed, {0: 2, 2: 0, 1: 3, 3: 1})
    both = hub_share(held, hub_rep, full)
    near = join_pieces(both[:, :, :full])
    at_end = (rep == 0) | (rep == 3)
    group_rest = jnp.stack([rest, beside, across, jnp.where(at_end, outer, middle)], axis=0)
    at = want ^ rep
    flag = lax.dynamic_index_in_dim(group_rest[:, -1, 0], at, 0, keepdims=False).astype(jnp.int32)
    member_want, member_order = flag & 3, (flag >> 2) & 1
    second = member_want ^ rep
    place = lambda k: jnp.where((k == 3) & at_end, 4, k)
    pick = jnp.stack(
        [near_slot, place(at), place(second), jnp.where(member_order == core, 2, 3), at, second]
    ).astype(jnp.int32)
    member_words = keep_words(pick, group_rest, lambda pick: pick[4], rows, WORDS_HINT)
    near, group_rest, member_words, pick, normed, beside_x, across_x = barrier(
        (near, group_rest, member_words, pick, normed, beside_x, across_x)
    )

    far = swap_cores(near[:, 0])
    outer_x, middle_x = along_line(across_x, OUTWARD), along_line(normed, MIDDLE)
    _, hub_order = flags_of(both[0, 0, full])
    share = hub_rows(jnp.where(hub_order == core, 2, 3)[None], both[0], near, far, width)
    share, near, far = barrier((share, near, far))
    near_new = join_pieces(share).reshape(rows, clust)
    near_tile, far_tile, *carry = two_of(pick, normed, near, far, words, carry)
    near_new, carry = barrier((near_new, carry))
    far_new = swap_cores(near_new)
    near_new, far_new, outer_x, middle_x = barrier((near_new, far_new, outer_x, middle_x))

    return finish_of(
        pick, (normed, beside_x, across_x, middle_x, outer_x), normed, group_rest, near, far, words, member_words,
        carry, indicators, (own_tile, near_tile, far_tile), (near_new, far_new),
    )


def solution(mesh):
    return jax.shard_map(
        body,
        mesh=mesh,
        in_specs=(
            P(("slab", "rep"), None),
            P(("slab", "rep"), None),
            P(("slab", "rep"), None),
            P(),
            P(("slab", "rep"), None, None),
        ),
        out_specs=P(("slab", "rep"), None),
        check_vma=False,
    )
```

```python
import functools

import jax
import jax.numpy as jnp
from jax import lax
from jax.experimental import pallas as pl
from jax.experimental.pallas import tpu as pltpu
from jax.sharding import PartitionSpec as P

K = 4
HUBS = 2
TOPK = 16
LANES = 128
EPS = 1e-06
TAU = 0.04
ALPHA = 0.8
AXES = ("slab", "rep")
ROW_TILE = 256
VMEM_LIMIT = 58 << 20
SCALE = 1.4426950408889634 / TAU
HALF = 32
FLAG_ROWS = 16
BLOCKS_NEAR = 5
WORDS_HINT = 30_000_000_000


def join_kernel(blocks, near_ref, x_ref, y_ref, cols_ref, all_ref, normed_ref, rest_ref):
    width, clust = x_ref.shape[1], y_ref.shape[1]
    step = pl.program_id(0)
    rows = pl.num_programs(0) * ROW_TILE
    values = x_ref[...].astype(jnp.float32)
    scale = lax.rsqrt(jnp.sum(values * values, axis=1, keepdims=True) + EPS)
    normed = (values * scale).astype(jnp.bfloat16)
    cols = cols_ref[...].reshape(K * TOPK, cols_ref.shape[2])
    flag = (near_ref[1] & 3) + 4 * (near_ref[2] - blocks)
    coded = jnp.concatenate([(cols >> 5) + HALF * flag, cols & (HALF - 1)], axis=0)
    all_ref[:, :width] = normed
    all_ref[:, width : width + clust] = y_ref[...]
    all_ref[:, width + clust :] = coded.astype(jnp.float32).T.astype(jnp.bfloat16)
    normed_ref[...] = normed
    rest_ref[pl.ds(pl.multiple_of(step * ROW_TILE, ROW_TILE), ROW_TILE), :] = y_ref[...]
    single = jnp.left_shift((cols & (LANES - 1)) + LANES, cols >> 7)
    place = pl.multiple_of(rows + step * K * TOPK, K * TOPK)
    rest_ref[pl.ds(place, K * TOPK), :] = single.astype(jnp.float32).astype(jnp.bfloat16)
    flags = jnp.full((FLAG_ROWS, clust), flag, jnp.int32)
    rest_ref[rows + rows // ROW_TILE * K * TOPK :, :] = flags.astype(jnp.float32).astype(jnp.bfloat16)


def join(blocks, near, embeddings, indicators, columns):
    rows, width = embeddings.shape
    clust = indicators.shape[1]
    by_row = lambda cols: pl.BlockSpec((ROW_TILE, cols), lambda r, flag: (r, 0))
    steps = rows // ROW_TILE
    rest = (rows + steps * K * TOPK + FLAG_ROWS, clust)
    return pl.pallas_call(
        functools.partial(join_kernel, blocks),
        out_shape=[
            jax.ShapeDtypeStruct(shape, jnp.bfloat16)
            for shape in ((rows, width + clust + 2 * K * TOPK), (rows, width), rest)
        ],
        grid_spec=pltpu.PrefetchScalarGridSpec(
            num_scalar_prefetch=1,
            grid=(steps,),
            in_specs=[
                by_row(width),
                by_row(clust),
                pl.BlockSpec((K, TOPK, ROW_TILE), lambda r, flag: (0, 0, r)),
            ],
            out_specs=[by_row(width + clust + 2 * K * TOPK), by_row(width), pl.BlockSpec(rest, lambda r, flag: (0, 0))],
        ),
        compiler_params=pltpu.CompilerParams(vmem_limit_bytes=VMEM_LIMIT),
        name="join",
    )(near, embeddings, indicators, jnp.transpose(columns, (1, 2, 0)))


def words_kernel(pick_ref, coded_ref, out_ref):
    lane = lax.broadcasted_iota(jnp.int32, (LANES, LANES), 0)
    for step in range(coded_ref.shape[1] // (K * TOPK)):
        coded = coded_ref[0, step * K * TOPK : (step + 1) * K * TOPK].astype(jnp.float32).astype(jnp.int32)
        high = sum((coded >= LANES << m).astype(jnp.int32) for m in range(1, 8))
        low = jnp.right_shift(coded, high) & (LANES - 1)
        bit = jnp.left_shift(jnp.ones_like(high), high)
        for part in range(ROW_TILE // LANES):
            here = slice(part * LANES, (part + 1) * LANES)
            for slot in range(K):
                word = jnp.zeros((LANES, LANES), jnp.int32)
                for t in range(slot * TOPK, (slot + 1) * TOPK):
                    word = word | jnp.where(lane == low[t : t + 1, here], bit[t : t + 1, here], 0)
                start = step * ROW_TILE + part * LANES
                out_ref[slot, start : start + LANES, :] = word.T


def keep_words(pick, rest, which, rows, hint):
    part = rows // ROW_TILE * K * TOPK
    clust = rest.shape[2]
    return pl.pallas_call(
        words_kernel,
        out_shape=jax.ShapeDtypeStruct((K, rows, LANES), jnp.int32),
        grid_spec=pltpu.PrefetchScalarGridSpec(
            num_scalar_prefetch=1,
            grid=(1,),
            in_specs=[pl.BlockSpec((1, part, clust), lambda i, pick: (which(pick), rows // part, 0))],
            out_specs=pl.BlockSpec((K, rows, LANES), lambda i, pick: (0, 0, 0)),
        ),
        compiler_params=pltpu.CompilerParams(vmem_limit_bytes=VMEM_LIMIT),
        cost_estimate=pl.CostEstimate(flops=hint, bytes_accessed=rows * 512, transcendentals=0),
        name="keep_words",
    )(pick, rest)


def mix(acc, degree, anchor):
    return (ALPHA * acc / degree + (1.0 - ALPHA) * anchor.astype(jnp.float32)).astype(jnp.bfloat16)


def weights(cosine, word, total, put):
    for j in range(cosine.shape[1] // LANES):
        part = cosine[:, j * LANES : (j + 1) * LANES]
        raw = jnp.where((word & (1 << j)) != 0, jnp.exp2(part * SCALE - SCALE), 0.0)
        total = total + raw
        put(slice(j * LANES, (j + 1) * LANES), raw.astype(jnp.bfloat16))
    return total


def cosines(rows, others):
    return lax.dot_general(rows, others, (((1,), (1,)), ((), ())), preferred_element_type=jnp.float32)


def flat(ref):
    value = ref[...]
    return value.reshape(-1, value.shape[-1])


def tile_kernel(has_carry, last, pick_ref, x_ref, other_ref, w_ref, y_ref, *refs):
    refs = list(refs)
    deg_in, acc_in = (refs.pop(0), refs.pop(0)) if has_carry else (None, None)
    anchor_ref = refs.pop(0) if last else None
    deg_ref, acc_ref, tile_ref = refs
    word = w_ref[0]
    total = deg_in[...] if has_carry else jnp.zeros(word.shape, jnp.float32)

    def put(lanes, value):
        tile_ref[:, lanes] = value

    total = weights(cosines(x_ref[...], flat(other_ref)), word, total, put)
    deg_ref[...] = total
    gathered = jnp.dot(tile_ref[...], flat(y_ref), preferred_element_type=jnp.float32)
    if has_carry:
        gathered = acc_in[...] + gathered
    if last:
        gathered = mix(gathered, jnp.sum(total, axis=1, keepdims=True), anchor_ref[...])
    acc_ref[...] = gathered


def tile_of(pick, x, other, y, words, slot, carry=None, anchor=None, keep=True):
    rows, clust = words.shape[1], y[1][-1]
    by_row = lambda cols: pl.BlockSpec((ROW_TILE, cols), lambda r, pick: (r, 0))
    spec = lambda operand: pl.BlockSpec(operand[1], operand[2])
    last = anchor is not None
    args = [x[0], other[0], words, y[0], *(carry or ())] + ([anchor[0]] if last else [])
    specs = [spec(x), spec(other), pl.BlockSpec((1, ROW_TILE, LANES), lambda r, pick: (slot(pick), r, 0)), spec(y)]
    specs += ([by_row(LANES), by_row(clust)] if carry else []) + ([spec(anchor)] if last else [])
    outs = [(LANES, jnp.float32), (clust, jnp.bfloat16 if last else jnp.float32)] + [(rows, jnp.bfloat16)] * keep
    return pl.pallas_call(
        functools.partial(tile_kernel, carry is not None, last),
        out_shape=[jax.ShapeDtypeStruct((rows, cols), kind) for cols, kind in outs],
        grid_spec=pltpu.PrefetchScalarGridSpec(
            num_scalar_prefetch=1,
            grid=(rows // ROW_TILE,),
            in_specs=specs,
            out_specs=[by_row(cols) for cols, _ in outs],
            scratch_shapes=[] if keep else [pltpu.VMEM((ROW_TILE, rows), jnp.bfloat16)],
        ),
        compiler_params=pltpu.CompilerParams(vmem_limit_bytes=VMEM_LIMIT),
        cost_estimate=pl.CostEstimate(flops=rows * clust, bytes_accessed=rows * clust, transcendentals=0),
        name="tile",
    )(pick, *args)


def put_to(ref):
    def put(lanes, value):
        ref[:, lanes] = value

    return put


def run_tiles(rows, plan, total, acc):
    for word, (other, y), tile in plan:
        total = weights(cosines(rows, other), word, total, put_to(tile))
        acc = acc + jnp.dot(tile[...], y, preferred_element_type=jnp.float32)
    return total, acc


def hub_blocks(near_ref, far_ref, width):
    near, far = near_ref[:, 0].reshape(-1, near_ref.shape[3]), flat(far_ref)
    return (near[:, :width], near[:, width:]), (far[:, :width], far[:, width:])


def hub_specs(near, far):
    chips, _, piece, full = near.shape
    once = pl.Buffered(1)
    return [
        pl.BlockSpec((chips, 1, piece, full), lambda r, pick: (0, 0, 0, 0), pipeline_mode=once),
        pl.BlockSpec((chips, piece, full), lambda r, pick: (0, 0, 0), pipeline_mode=once),
    ]


def two_kernel(pick_ref, rows_ref, near_ref, far_ref, words_ref, deg_in, acc_in, near_tile, far_tile, deg_ref, acc_ref):
    near, far = hub_blocks(near_ref, far_ref, rows_ref.shape[1])
    plan = (
        (words_ref[pick_ref[0]], near, near_tile),
        (words_ref[5 - pick_ref[0]], far, far_tile),
    )
    deg_ref[...], acc_ref[...] = run_tiles(rows_ref[...], plan, deg_in[...], acc_in[...])


def two_of(pick, own_rows, near, far, words, carry):
    rows, width = own_rows.shape
    clust = carry[1].shape[1]
    by_row = lambda cols: pl.BlockSpec((ROW_TILE, cols), lambda r, pick: (r, 0))
    by_word = pl.BlockSpec((K, ROW_TILE, LANES), lambda r, pick: (0, r, 0))
    outs = [(rows, jnp.bfloat16)] * 2 + [(LANES, jnp.float32), (clust, jnp.float32)]
    return pl.pallas_call(
        two_kernel,
        out_shape=[jax.ShapeDtypeStruct((rows, cols), kind) for cols, kind in outs],
        grid_spec=pltpu.PrefetchScalarGridSpec(
            num_scalar_prefetch=1,
            grid=(rows // ROW_TILE,),
            in_specs=[by_row(width), *hub_specs(near, far), by_word, by_row(LANES), by_row(clust)],
            out_specs=[by_row(cols) for cols, _ in outs],
        ),
        compiler_params=pltpu.CompilerParams(vmem_limit_bytes=VMEM_LIMIT),
        cost_estimate=pl.CostEstimate(flops=rows * clust, bytes_accessed=rows * clust, transcendentals=0),
        name="two",
    )(pick, own_rows, near, far, words, *carry)


def finish_kernel(pick_ref, *refs):
    blocks, refs = refs[:BLOCKS_NEAR], refs[BLOCKS_NEAR:]
    rows_ref, first_y, second_y, near_ref, far_ref, own_ref, member_ref, deg_in, acc_in, anchor_ref = refs[:10]
    own_tile, near_tile, far_tile, near_new, far_new, out_ref = refs[10:16]
    member_tile, degree, new, other_new, first_x, second_x, held, spare, sems = refs[16:]
    phase, step = pl.program_id(0), pl.program_id(1)
    here = pl.ds(pl.multiple_of(step * ROW_TILE, ROW_TILE), ROW_TILE)

    @pl.when((phase == 0) & (step == 0))
    def _():
        for which, target in enumerate((first_x, second_x)):
            for i, block in enumerate(blocks):

                @pl.when(pick_ref[1 + which] == i)
                def _():
                    copy = pltpu.make_async_copy(block, target, sems.at[which])
                    copy.start()
                    copy.wait()

    @pl.when(phase == 0)
    def _():
        first, second = (first_x[...], first_y[0]), (second_x[...], second_y[0])
        near, far = hub_blocks(near_ref, far_ref, rows_ref.shape[1])
        plan = ((own_ref[0], first, member_tile.at[here, :]),)
        total, acc = run_tiles(rows_ref[...], plan, deg_in[...], acc_in[...])
        degree[here, :] = total
        new[here, :] = mix(acc, jnp.sum(total, axis=1, keepdims=True), anchor_ref[...])
        plan = (
            (member_ref[pick_ref[3]], near, held),
            (member_ref[5 - pick_ref[3]], far, spare),
            (member_ref[0], first, held),
            (member_ref[1], second, spare),
        )
        zeros = lambda ref: jnp.zeros(ref.shape, jnp.float32)
        total, acc = run_tiles(first_x[here, :], plan, zeros(deg_in), zeros(acc_in))
        other_new[here, :] = mix(acc, jnp.sum(total, axis=1, keepdims=True), first_y[0, here, :])

    @pl.when(phase == 1)
    def _():
        pairs = ((own_tile[...], new), (member_tile[here, :], other_new), (near_tile[...], near_new), (far_tile[...], far_new))
        acc = sum(jnp.dot(tile, y[...], preferred_element_type=jnp.float32) for tile, y in pairs)
        out_ref[...] = mix(acc, jnp.sum(degree[here, :], axis=1, keepdims=True), anchor_ref[...])


def finish_of(pick, blocks, own_rows, rest, near, far, words, member_words, carry, anchor, tiles, news):
    rows, width = blocks[0].shape
    clust = rest.shape[2]
    steps = rows // ROW_TILE
    once = pl.Buffered(1)
    before = lambda p, r: jnp.where(p == 0, r, steps - 1)
    after = lambda p, r: jnp.where(p == 0, 0, r)
    by_row = lambda cols, row: pl.BlockSpec((ROW_TILE, cols), lambda p, r, pick: (row(p, r), 0))
    rest_at = lambda k: pl.BlockSpec((1, rows, clust), lambda p, r, pick: (pick[k], 0, 0), pipeline_mode=once)
    whole = pl.BlockSpec((rows, clust), lambda p, r, pick: (0, 0), pipeline_mode=once)
    chips, _, piece, full = near.shape
    return pl.pallas_call(
        finish_kernel,
        out_shape=jax.ShapeDtypeStruct((rows, clust), jnp.bfloat16),
        grid_spec=pltpu.PrefetchScalarGridSpec(
            num_scalar_prefetch=1,
            grid=(2, steps),
            in_specs=[pl.BlockSpec(memory_space=pl.ANY)] * len(blocks)
            + [
                by_row(width, before),
                rest_at(4),
                rest_at(5),
                pl.BlockSpec((chips, 1, piece, full), lambda p, r, pick: (0, 0, 0, 0), pipeline_mode=once),
                pl.BlockSpec((chips, piece, full), lambda p, r, pick: (0, 0, 0), pipeline_mode=once),
                pl.BlockSpec((1, ROW_TILE, LANES), lambda p, r, pick: (1, before(p, r), 0)),
                pl.BlockSpec((K, ROW_TILE, LANES), lambda p, r, pick: (0, before(p, r), 0)),
                by_row(LANES, before),
                by_row(clust, before),
                by_row(clust, lambda p, r: r),
            ]
            + [by_row(rows, after)] * 3
            + [whole] * 2,
            out_specs=by_row(clust, after),
            scratch_shapes=[
                pltpu.VMEM((rows, rows), jnp.bfloat16),
                pltpu.VMEM((rows, LANES), jnp.float32),
                pltpu.VMEM((rows, clust), jnp.bfloat16),
                pltpu.VMEM((rows, clust), jnp.bfloat16),
            ]
            + [pltpu.VMEM((rows, width), jnp.bfloat16)] * 2
            + [pltpu.VMEM((ROW_TILE, rows), jnp.bfloat16)] * 2
            + [pltpu.SemaphoreType.DMA((2,))],
        ),
        compiler_params=pltpu.CompilerParams(vmem_limit_bytes=VMEM_LIMIT),
        cost_estimate=pl.CostEstimate(
            flops=12 * rows * rows * 768, bytes_accessed=12 * rows * rows, transcendentals=5 * rows * rows
        ),
        name="finish",
    )(pick, *blocks, own_rows, rest, rest, near, far, words, member_words, *carry, anchor, *tiles, *news)


def hub_rows_kernel(width, pick_ref, rows_ref, near_ref, far_ref, out_ref, word_ref, tile_ref):
    clust = out_ref.shape[1]
    half = K * TOPK
    coded = rows_ref[:, width + clust :].astype(jnp.float32).astype(jnp.int32)
    high = coded[:, :half] & (HALF - 1)
    low = (high & 3) * HALF + coded[:, half:]
    bit = jnp.left_shift(jnp.ones_like(high), high >> 2)
    lane = lax.broadcasted_iota(jnp.int32, (rows_ref.shape[0], LANES), 1)
    for slot in range(K):
        word = jnp.zeros(lane.shape, jnp.int32)
        for t in range(slot * TOPK, (slot + 1) * TOPK):
            word = word | jnp.where(lane == low[:, t : t + 1], bit[:, t : t + 1], 0)
        word_ref[slot] = word
    total = jnp.zeros(lane.shape, jnp.float32)
    acc = jnp.zeros(out_ref.shape, jnp.float32)

    def put(lanes, value):
        tile_ref[:, lanes] = value

    self_block = near_ref[:, 0].reshape(-1, width + clust)
    member_block = near_ref[:, 1].reshape(-1, width + clust)
    far_block = flat(far_ref)
    slots = (0, 1, pick_ref[0], 5 - pick_ref[0])
    for slot, block in zip(slots, (self_block, member_block, self_block, far_block)):
        total = weights(cosines(rows_ref[:, :width], block[:, :width]), word_ref[slot], total, put)
        acc = acc + jnp.dot(tile_ref[...], block[:, width:], preferred_element_type=jnp.float32)
    out_ref[...] = mix(acc, jnp.sum(total, axis=1, keepdims=True), rows_ref[:, width : width + clust])


def hub_rows(self_slot, mine, near, far, width):
    share = mine.shape[0]
    clust = near.shape[3] - width
    rows = near.shape[0] * near.shape[2]
    return pl.pallas_call(
        functools.partial(hub_rows_kernel, width),
        out_shape=jax.ShapeDtypeStruct((share, clust), jnp.bfloat16),
        grid_spec=pltpu.PrefetchScalarGridSpec(
            num_scalar_prefetch=1,
            grid=(1,),
            in_specs=[
                pl.BlockSpec(mine.shape, lambda i, pick: (0, 0)),
                pl.BlockSpec(near.shape, lambda i, pick: (0, 0, 0, 0)),
                pl.BlockSpec(far.shape, lambda i, pick: (0, 0, 0)),
            ],
            out_specs=pl.BlockSpec((share, clust), lambda i, pick: (0, 0)),
            scratch_shapes=[pltpu.VMEM((K, share, LANES), jnp.int32), pltpu.VMEM((share, rows), jnp.bfloat16)],
        ),
        compiler_params=pltpu.CompilerParams(vmem_limit_bytes=VMEM_LIMIT),
        cost_estimate=pl.CostEstimate(flops=rows, bytes_accessed=rows, transcendentals=0),
        name="hub_rows",
    )(self_slot, mine, near, far)


def send(block, target):
    slabs, reps = lax.axis_size("slab"), lax.axis_size("rep")
    chips = slabs // 4
    pairs = []
    for device in range(slabs * reps):
        slab, rep = divmod(device, reps)
        to = target(slab // (2 * chips), slab // 2 % chips, slab % 2, rep)
        if to is not None:
            pairs.append((device, ((to[0] * chips + to[1]) * 2 + to[2]) * reps + to[3]))
    return lax.ppermute(block, AXES, pairs)


def along_line(block, table):
    return send(
        block, lambda half, chip, core, rep: (half, chip, core, table[rep]) if rep in table else None
    )


def swap_cores(block):
    return send(block, lambda half, chip, core, rep: (half, chip, 1 - core, rep))


def flags_of(code):
    flag = code.astype(jnp.float32).astype(jnp.int32) // HALF
    return flag & 3, (flag >> 2) & 1


def join_pieces(piece):
    slabs = lax.axis_size("slab")
    members, chips = slabs // 2, slabs // 4
    layers = [[h * members + c * 2 + core for c in range(chips)] for h in range(2) for core in range(2)]
    repeated = jnp.broadcast_to(piece[None], (chips,) + piece.shape)
    return lax.all_to_all(repeated, "slab", 0, 0, axis_index_groups=layers, tiled=True)


OUTWARD = {1: 0, 2: 3}
MIDDLE = {1: 2, 2: 1}


def spread_line(block):
    across = along_line(block, {0: 2, 2: 0, 1: 3, 3: 1})
    beside = along_line(block, {0: 1, 1: 0, 2: 3, 3: 2})
    return across, beside


def scatter(block):
    members = lax.axis_size("slab") // 2
    rows, width = block.shape
    planes = [[h * members + m for m in range(members)] for h in range(2)]
    return lax.all_to_all(
        block.reshape(members, rows // members, width), "slab", 0, 0, axis_index_groups=planes, tiled=True
    )


def hub_candidates(mine, hub_ids):
    members, reps = lax.axis_size("slab") // 2, lax.axis_size("rep")
    slab = lax.axis_index("slab")
    hub_slab, hub_rep = lax.div(hub_ids, reps), lax.rem(hub_ids, reps)
    member = lax.rem(hub_slab, members)
    held = jnp.stack(
        [lax.dynamic_index_in_dim(mine, member[h], 0, keepdims=False) for h in range(HUBS)], axis=0
    )
    got = send(held, lambda half, chip, core, rep: (1 - half, chip, core, rep))
    away = lax.div(hub_slab, members) != lax.div(slab, members)
    held = jnp.where(away[:, None, None], got, held)[None]
    rep = lax.axis_index("rep")
    for bit in range(2):
        got = along_line(held, {r: r ^ (1 << bit) for r in range(4)})
        upper = (rep >> bit) & 1 == 1
        held = jnp.concatenate([jnp.where(upper, got, held), jnp.where(upper, held, got)], axis=0)
    return held, hub_rep


def hub_share(held, hub_rep, code_at):
    slab = lax.axis_index("slab")
    pick = lambda pieces, at: jnp.where(
        at < 2, jnp.where(at == 0, pieces[0], pieces[1]), jnp.where(at == 2, pieces[2], pieces[3])
    )
    chosen = []
    for h in range(HUBS):
        hub = pick(held[:, h], hub_rep[h])
        want, _ = flags_of(hub[:1, code_at : code_at + 1])
        chosen.append(jnp.stack([hub, pick(held[:, h], want)], axis=0))
    held = jnp.stack(chosen, axis=0)
    first_core = lax.rem(slab, 2) == 0
    keep = jnp.where(first_core, held[0], held[1])
    got = swap_cores(jnp.where(first_core, held[1], held[0]))
    return jnp.concatenate([jnp.where(first_core, keep, got), jnp.where(first_core, got, keep)], axis=1)


def body(embeddings, indicators, neighbours, hub_ids, columns):
    rows, width = embeddings.shape
    clust = indicators.shape[1]
    full = width + clust
    reps = lax.axis_size("rep")
    total = lax.axis_size("slab") * reps
    rep = lax.axis_index("rep")
    steps = rows // ROW_TILE
    slots = neighbours[0].astype(jnp.int32)
    want = slots[1] & 3
    order = slots[2] - total
    core = lax.rem(lax.axis_index("slab"), 2)
    near_slot = jnp.where(order == core, 2, 3)
    barrier = lax.optimization_barrier

    joined, normed, rest = join(total, neighbours.reshape(-1), embeddings, indicators, columns)
    across, beside = spread_line(rest)

    pick = jnp.stack([near_slot]).astype(jnp.int32)
    own_rows = (joined, (ROW_TILE, width), lambda r, pick: (r, 0))
    own_x = (joined, (rows, width), lambda r, pick: (0, 0))
    own_y = (joined, (rows, clust), lambda r, pick: (0, width // clust))
    words = keep_words(pick, rest[None], lambda pick: 0, rows, 1)
    *carry, own_tile = tile_of(pick, own_rows, own_x, own_y, words, lambda pick: 0)
    mine, words, carry, own_tile, rest, across, beside = barrier(
        (scatter(joined), words, carry, own_tile, rest, across, beside)
    )

    held, hub_rep = hub_candidates(mine, hub_ids)
    held, normed, rest, across = barrier((held, normed, rest, across))

    outer, middle = along_line(across, OUTWARD), along_line(rest, MIDDLE)
    beside_x = along_line(normed, {0: 1, 1: 0, 2: 3, 3: 2})
    across_x = along_line(normed, {0: 2, 2: 0, 1: 3, 3: 1})
    both = hub_share(held, hub_rep, full)
    near = join_pieces(both[:, :, :full])
    at_end = (rep == 0) | (rep == 3)
    group_rest = jnp.stack([rest, beside, across, jnp.where(~at_end, middle, outer)], axis=0)
    at = want ^ rep
    flag = lax.dynamic_index_in_dim(group_rest[:, -1, 0], at, 0, keepdims=False).astype(jnp.int32)
    member_want, member_order = flag & 3, (flag >> 2) & 1
    second = member_want ^ rep
    place = lambda k: jnp.where((k == 3) & at_end, 4, k)
    pick = jnp.stack(
        [near_slot, place(at), place(second), jnp.where(member_order == core, 2, 3), at, second]
    ).astype(jnp.int32)
    member_words = keep_words(pick, group_rest, lambda pick: pick[4], rows, WORDS_HINT)
    near, group_rest, member_words, pick, normed, beside_x, across_x = barrier(
        (near, group_rest, member_words, pick, normed, beside_x, across_x)
    )

    far = swap_cores(near[:, 0])
    outer_x, middle_x = along_line(across_x, OUTWARD), along_line(normed, MIDDLE)
    _, hub_order = flags_of(both[0, 0, full])
    share = hub_rows(jnp.where(hub_order == core, 2, 3)[None], both[0], near, far, width)
    share, near, far = barrier((share, near, far))
    near_new = join_pieces(share).reshape(rows, clust)
    near_tile, far_tile, *carry = two_of(pick, normed, near, far, words, carry)
    near_new, carry = barrier((near_new, carry))
    far_new = swap_cores(near_new)
    near_new, far_new, outer_x, middle_x = barrier((near_new, far_new, outer_x, middle_x))

    return finish_of(
        pick, (normed, beside_x, across_x, middle_x, outer_x), normed, group_rest, near, far, words, member_words,
        carry, indicators, (own_tile, near_tile, far_tile), (near_new, far_new),
    )


def solution(mesh):
    return jax.shard_map(
        body,
        mesh=mesh,
        in_specs=(
            P(("slab", "rep"), None),
            P(("slab", "rep"), None),
            P(("slab", "rep"), None),
            P(),
            P(("slab", "rep"), None, None),
        ),
        out_specs=P(("slab", "rep"), None),
        check_vma=False,
    )
```

```python
import functools

import jax
import jax.numpy as jnp
from jax import lax
from jax.experimental import pallas as pl
from jax.experimental.pallas import tpu as pltpu
from jax.sharding import PartitionSpec as P

K = 4
HUBS = 2
TOPK = 16
LANES = 128
EPS = 1e-06
TAU = 0.04
ALPHA = 0.8
AXES = ("slab", "rep")
ROW_TILE = 256
VMEM_LIMIT = 58 << 20
SCALE = 1.4426950408889634 / TAU
HALF = 32
FLAG_ROWS = 16
BLOCKS_NEAR = 5
WORDS_HINT = 30_000_000_000


def join_kernel(blocks, near_ref, x_ref, y_ref, cols_ref, all_ref, normed_ref, rest_ref):
    width, clust = x_ref.shape[1], y_ref.shape[1]
    step = pl.program_id(0)
    rows = pl.num_programs(0) * ROW_TILE
    values = x_ref[...].astype(jnp.float32)
    scale = lax.rsqrt(jnp.sum(values * values, axis=1, keepdims=True) + EPS)
    normed = (values * scale).astype(jnp.bfloat16)
    cols = cols_ref[...].reshape(K * TOPK, cols_ref.shape[2])
    flag = (near_ref[1] & 3) + 4 * (near_ref[2] - blocks)
    coded = jnp.concatenate([(cols >> 5) + HALF * flag, cols & (HALF - 1)], axis=0)
    all_ref[:, :width] = normed
    all_ref[:, width : width + clust] = y_ref[...]
    all_ref[:, width + clust :] = coded.astype(jnp.float32).T.astype(jnp.bfloat16)
    normed_ref[...] = normed
    rest_ref[pl.ds(pl.multiple_of(step * ROW_TILE, ROW_TILE), ROW_TILE), :] = y_ref[...]
    single = jnp.left_shift((cols & (LANES - 1)) + LANES, cols >> 7)
    place = pl.multiple_of(rows + step * K * TOPK, K * TOPK)
    rest_ref[pl.ds(place, K * TOPK), :] = single.astype(jnp.float32).astype(jnp.bfloat16)
    flags = jnp.full((FLAG_ROWS, clust), flag, jnp.int32)
    rest_ref[rows + rows // ROW_TILE * K * TOPK :, :] = flags.astype(jnp.float32).astype(jnp.bfloat16)


def join(blocks, near, embeddings, indicators, columns):
    rows, width = embeddings.shape
    clust = indicators.shape[1]
    by_row = lambda cols: pl.BlockSpec((ROW_TILE, cols), lambda r, flag: (r, 0))
    steps = rows // ROW_TILE
    rest = (rows + steps * K * TOPK + FLAG_ROWS, clust)
    return pl.pallas_call(
        functools.partial(join_kernel, blocks),
        out_shape=[
            jax.ShapeDtypeStruct(shape, jnp.bfloat16)
            for shape in ((rows, width + clust + 2 * K * TOPK), (rows, width), rest)
        ],
        grid_spec=pltpu.PrefetchScalarGridSpec(
            num_scalar_prefetch=1,
            grid=(steps,),
            in_specs=[
                by_row(width),
                by_row(clust),
                pl.BlockSpec((K, TOPK, ROW_TILE), lambda r, flag: (0, 0, r)),
            ],
            out_specs=[by_row(width + clust + 2 * K * TOPK), by_row(width), pl.BlockSpec(rest, lambda r, flag: (0, 0))],
        ),
        compiler_params=pltpu.CompilerParams(vmem_limit_bytes=VMEM_LIMIT),
        name="join",
    )(near, embeddings, indicators, jnp.transpose(columns, (1, 2, 0)))


def words_kernel(pick_ref, coded_ref, out_ref):
    lane = lax.broadcasted_iota(jnp.int32, (LANES, LANES), 0)
    for step in range(coded_ref.shape[1] // (K * TOPK)):
        coded = coded_ref[0, step * K * TOPK : (step + 1) * K * TOPK].astype(jnp.float32).astype(jnp.int32)
        high = sum((coded >= LANES << m).astype(jnp.int32) for m in range(1, 8))
        low = jnp.right_shift(coded, high) & (LANES - 1)
        bit = jnp.left_shift(jnp.ones_like(high), high)
        for part in range(ROW_TILE // LANES):
            here = slice(part * LANES, (part + 1) * LANES)
            for slot in range(K):
                word = jnp.zeros((LANES, LANES), jnp.int32)
                for t in range(slot * TOPK, (slot + 1) * TOPK):
                    word = word | jnp.where(lane == low[t : t + 1, here], bit[t : t + 1, here], 0)
                start = step * ROW_TILE + part * LANES
                out_ref[slot, start : start + LANES, :] = word.T


def keep_words(pick, rest, which, rows, hint):
    part = rows // ROW_TILE * K * TOPK
    clust = rest.shape[2]
    return pl.pallas_call(
        words_kernel,
        out_shape=jax.ShapeDtypeStruct((K, rows, LANES), jnp.int32),
        grid_spec=pltpu.PrefetchScalarGridSpec(
            num_scalar_prefetch=1,
            grid=(1,),
            in_specs=[pl.BlockSpec((1, part, clust), lambda i, pick: (which(pick), rows // part, 0))],
            out_specs=pl.BlockSpec((K, rows, LANES), lambda i, pick: (0, 0, 0)),
        ),
        compiler_params=pltpu.CompilerParams(vmem_limit_bytes=VMEM_LIMIT),
        cost_estimate=pl.CostEstimate(flops=hint, bytes_accessed=rows * 512, transcendentals=0),
        name="keep_words",
    )(pick, rest)


def mix(acc, degree, anchor):
    return (ALPHA * acc / degree + (1.0 - ALPHA) * anchor.astype(jnp.float32)).astype(jnp.bfloat16)


def weights(cosine, word, total, put):
    for j in range(cosine.shape[1] // LANES):
        part = cosine[:, j * LANES : (j + 1) * LANES]
        raw = jnp.where((word & (1 << j)) != 0, jnp.exp2(part * SCALE - SCALE), 0.0)
        total = total + raw
        put(slice(j * LANES, (j + 1) * LANES), raw.astype(jnp.bfloat16))
    return total


def cosines(rows, others):
    return lax.dot_general(rows, others, (((1,), (1,)), ((), ())), preferred_element_type=jnp.float32)


def flat(ref):
    value = ref[...]
    return value.reshape(-1, value.shape[-1])


def tile_kernel(has_carry, last, pick_ref, x_ref, other_ref, w_ref, y_ref, *refs):
    refs = list(refs)
    deg_in, acc_in = (refs.pop(0), refs.pop(0)) if has_carry else (None, None)
    anchor_ref = refs.pop(0) if last else None
    deg_ref, acc_ref, tile_ref = refs
    word = w_ref[0]
    total = deg_in[...] if has_carry else jnp.zeros(word.shape, jnp.float32)

    def put(lanes, value):
        tile_ref[:, lanes] = value

    total = weights(cosines(x_ref[...], flat(other_ref)), word, total, put)
    deg_ref[...] = total
    gathered = jnp.dot(tile_ref[...], flat(y_ref), preferred_element_type=jnp.float32)
    if has_carry:
        gathered = acc_in[...] + gathered
    if last:
        gathered = mix(gathered, jnp.sum(total, axis=1, keepdims=True), anchor_ref[...])
    acc_ref[...] = gathered


def tile_of(pick, x, other, y, words, slot, carry=None, anchor=None, keep=True):
    rows, clust = words.shape[1], y[1][-1]
    by_row = lambda cols: pl.BlockSpec((ROW_TILE, cols), lambda r, pick: (r, 0))
    spec = lambda operand: pl.BlockSpec(operand[1], operand[2])
    last = anchor is not None
    args = [x[0], other[0], words, y[0], *(carry or ())] + ([anchor[0]] if last else [])
    specs = [spec(x), spec(other), pl.BlockSpec((1, ROW_TILE, LANES), lambda r, pick: (slot(pick), r, 0)), spec(y)]
    specs += ([by_row(LANES), by_row(clust)] if carry else []) + ([spec(anchor)] if last else [])
    outs = [(LANES, jnp.float32), (clust, jnp.bfloat16 if last else jnp.float32)] + [(rows, jnp.bfloat16)] * keep
    return pl.pallas_call(
        functools.partial(tile_kernel, carry is not None, last),
        out_shape=[jax.ShapeDtypeStruct((rows, cols), kind) for cols, kind in outs],
        grid_spec=pltpu.PrefetchScalarGridSpec(
            num_scalar_prefetch=1,
            grid=(rows // ROW_TILE,),
            in_specs=specs,
            out_specs=[by_row(cols) for cols, _ in outs],
            scratch_shapes=[] if keep else [pltpu.VMEM((ROW_TILE, rows), jnp.bfloat16)],
        ),
        compiler_params=pltpu.CompilerParams(vmem_limit_bytes=VMEM_LIMIT),
        cost_estimate=pl.CostEstimate(flops=rows * clust, bytes_accessed=rows * clust, transcendentals=0),
        name="tile",
    )(pick, *args)


def put_to(ref):
    def put(lanes, value):
        ref[:, lanes] = value

    return put


def run_tiles(rows, plan, total, acc):
    for word, (other, y), tile in plan:
        total = weights(cosines(rows, other), word, total, put_to(tile))
        acc = acc + jnp.dot(tile[...], y, preferred_element_type=jnp.float32)
    return total, acc


def hub_blocks(near_ref, far_ref, width):
    near, far = near_ref[:, 0].reshape(-1, near_ref.shape[3]), flat(far_ref)
    return (near[:, :width], near[:, width:]), (far[:, :width], far[:, width:])


def hub_specs(near, far):
    chips, _, piece, full = near.shape
    once = pl.Buffered(1)
    return [
        pl.BlockSpec((chips, 1, piece, full), lambda r, pick: (0, 0, 0, 0), pipeline_mode=once),
        pl.BlockSpec((chips, piece, full), lambda r, pick: (0, 0, 0), pipeline_mode=once),
    ]


def two_kernel(pick_ref, rows_ref, near_ref, far_ref, words_ref, deg_in, acc_in, near_tile, far_tile, deg_ref, acc_ref):
    near, far = hub_blocks(near_ref, far_ref, rows_ref.shape[1])
    plan = (
        (words_ref[pick_ref[0]], near, near_tile),
        (words_ref[5 - pick_ref[0]], far, far_tile),
    )
    deg_ref[...], acc_ref[...] = run_tiles(rows_ref[...], plan, deg_in[...], acc_in[...])


def two_of(pick, own_rows, near, far, words, carry):
    rows, width = own_rows.shape
    clust = carry[1].shape[1]
    by_row = lambda cols: pl.BlockSpec((ROW_TILE, cols), lambda r, pick: (r, 0))
    by_word = pl.BlockSpec((K, ROW_TILE, LANES), lambda r, pick: (0, r, 0))
    outs = [(rows, jnp.bfloat16)] * 2 + [(LANES, jnp.float32), (clust, jnp.float32)]
    return pl.pallas_call(
        two_kernel,
        out_shape=[jax.ShapeDtypeStruct((rows, cols), kind) for cols, kind in outs],
        grid_spec=pltpu.PrefetchScalarGridSpec(
            num_scalar_prefetch=1,
            grid=(rows // ROW_TILE,),
            in_specs=[by_row(width), *hub_specs(near, far), by_word, by_row(LANES), by_row(clust)],
            out_specs=[by_row(cols) for cols, _ in outs],
        ),
        compiler_params=pltpu.CompilerParams(vmem_limit_bytes=VMEM_LIMIT),
        cost_estimate=pl.CostEstimate(flops=rows * clust, bytes_accessed=rows * clust, transcendentals=0),
        name="two",
    )(pick, own_rows, near, far, words, *carry)


def finish_kernel(pick_ref, *refs):
    blocks, refs = refs[:BLOCKS_NEAR], refs[BLOCKS_NEAR:]
    rows_ref, first_y, second_y, near_ref, far_ref, own_ref, member_ref, deg_in, acc_in, anchor_ref = refs[:10]
    own_tile, near_tile, far_tile, near_new, far_new, out_ref = refs[10:16]
    member_tile, degree, new, other_new, first_x, second_x, held, spare, sems = refs[16:]
    phase, step = pl.program_id(0), pl.program_id(1)
    here = pl.ds(pl.multiple_of(step * ROW_TILE, ROW_TILE), ROW_TILE)

    @pl.when((phase == 0) & (step == 0))
    def _():
        wanted = ((pick_ref[1], first_x, sems.at[0]), (pick_ref[2], second_x, sems.at[1]))
        for at, target, sem in wanted:
            for i, block in enumerate(blocks):

                @pl.when(at == i)
                def _():
                    pltpu.make_async_copy(block, target, sem).start()

        for _, target, sem in wanted:
            pltpu.make_async_copy(blocks[0], target, sem).wait()

    @pl.when(phase == 0)
    def _():
        first, second = (first_x[...], first_y[0]), (second_x[...], second_y[0])
        near, far = hub_blocks(near_ref, far_ref, rows_ref.shape[1])
        plan = ((own_ref[0], first, member_tile.at[here, :]),)
        total, acc = run_tiles(rows_ref[...], plan, deg_in[...], acc_in[...])
        degree[here, :] = total
        new[here, :] = mix(acc, jnp.sum(total, axis=1, keepdims=True), anchor_ref[...])
        plan = (
            (member_ref[pick_ref[3]], near, held),
            (member_ref[5 - pick_ref[3]], far, spare),
            (member_ref[0], first, held),
            (member_ref[1], second, spare),
        )
        zeros = lambda ref: jnp.zeros(ref.shape, jnp.float32)
        total, acc = run_tiles(first_x[here, :], plan, zeros(deg_in), zeros(acc_in))
        other_new[here, :] = mix(acc, jnp.sum(total, axis=1, keepdims=True), first_y[0, here, :])

    @pl.when(phase == 1)
    def _():
        pairs = ((own_tile[...], new), (member_tile[here, :], other_new), (near_tile[...], near_new), (far_tile[...], far_new))
        acc = sum(jnp.dot(tile, y[...], preferred_element_type=jnp.float32) for tile, y in pairs)
        out_ref[...] = mix(acc, jnp.sum(degree[here, :], axis=1, keepdims=True), anchor_ref[...])


def finish_of(pick, blocks, own_rows, rest, near, far, words, member_words, carry, anchor, tiles, news):
    rows, width = blocks[0].shape
    clust = rest.shape[2]
    steps = rows // ROW_TILE
    once = pl.Buffered(1)
    before = lambda p, r: jnp.where(p == 0, r, steps - 1)
    after = lambda p, r: jnp.where(p == 0, 0, r)
    by_row = lambda cols, row: pl.BlockSpec((ROW_TILE, cols), lambda p, r, pick: (row(p, r), 0))
    rest_at = lambda k: pl.BlockSpec((1, rows, clust), lambda p, r, pick: (pick[k], 0, 0), pipeline_mode=once)
    whole = pl.BlockSpec((rows, clust), lambda p, r, pick: (0, 0), pipeline_mode=once)
    chips, _, piece, full = near.shape
    return pl.pallas_call(
        finish_kernel,
        out_shape=jax.ShapeDtypeStruct((rows, clust), jnp.bfloat16),
        grid_spec=pltpu.PrefetchScalarGridSpec(
            num_scalar_prefetch=1,
            grid=(2, steps),
            in_specs=[pl.BlockSpec(memory_space=pl.ANY)] * len(blocks)
            + [
                by_row(width, before),
                rest_at(4),
                rest_at(5),
                pl.BlockSpec((chips, 1, piece, full), lambda p, r, pick: (0, 0, 0, 0), pipeline_mode=once),
                pl.BlockSpec((chips, piece, full), lambda p, r, pick: (0, 0, 0), pipeline_mode=once),
                pl.BlockSpec((1, ROW_TILE, LANES), lambda p, r, pick: (1, before(p, r), 0)),
                pl.BlockSpec((K, ROW_TILE, LANES), lambda p, r, pick: (0, before(p, r), 0)),
                by_row(LANES, before),
                by_row(clust, before),
                by_row(clust, lambda p, r: r),
            ]
            + [by_row(rows, after)] * 3
            + [whole] * 2,
            out_specs=by_row(clust, after),
            scratch_shapes=[
                pltpu.VMEM((rows, rows), jnp.bfloat16),
                pltpu.VMEM((rows, LANES), jnp.float32),
                pltpu.VMEM((rows, clust), jnp.bfloat16),
                pltpu.VMEM((rows, clust), jnp.bfloat16),
            ]
            + [pltpu.VMEM((rows, width), jnp.bfloat16)] * 2
            + [pltpu.VMEM((ROW_TILE, rows), jnp.bfloat16)] * 2
            + [pltpu.SemaphoreType.DMA((2,))],
        ),
        compiler_params=pltpu.CompilerParams(vmem_limit_bytes=VMEM_LIMIT),
        cost_estimate=pl.CostEstimate(
            flops=12 * rows * rows * 768, bytes_accessed=12 * rows * rows, transcendentals=5 * rows * rows
        ),
        name="finish",
    )(pick, *blocks, own_rows, rest, rest, near, far, words, member_words, *carry, anchor, *tiles, *news)


def hub_rows_kernel(width, pick_ref, rows_ref, near_ref, far_ref, out_ref, word_ref, tile_ref):
    clust = out_ref.shape[1]
    half = K * TOPK
    coded = rows_ref[:, width + clust :].astype(jnp.float32).astype(jnp.int32)
    high = coded[:, :half] & (HALF - 1)
    low = (high & 3) * HALF + coded[:, half:]
    bit = jnp.left_shift(jnp.ones_like(high), high >> 2)
    lane = lax.broadcasted_iota(jnp.int32, (rows_ref.shape[0], LANES), 1)
    for slot in range(K):
        word = jnp.zeros(lane.shape, jnp.int32)
        for t in range(slot * TOPK, (slot + 1) * TOPK):
            word = word | jnp.where(lane == low[:, t : t + 1], bit[:, t : t + 1], 0)
        word_ref[slot] = word
    total = jnp.zeros(lane.shape, jnp.float32)
    acc = jnp.zeros(out_ref.shape, jnp.float32)

    def put(lanes, value):
        tile_ref[:, lanes] = value

    self_block = near_ref[:, 0].reshape(-1, width + clust)
    member_block = near_ref[:, 1].reshape(-1, width + clust)
    far_block = flat(far_ref)
    slots = (0, 1, pick_ref[0], 5 - pick_ref[0])
    for slot, block in zip(slots, (self_block, member_block, self_block, far_block)):
        total = weights(cosines(rows_ref[:, :width], block[:, :width]), word_ref[slot], total, put)
        acc = acc + jnp.dot(tile_ref[...], block[:, width:], preferred_element_type=jnp.float32)
    out_ref[...] = mix(acc, jnp.sum(total, axis=1, keepdims=True), rows_ref[:, width : width + clust])


def hub_rows(self_slot, mine, near, far, width):
    share = mine.shape[0]
    clust = near.shape[3] - width
    rows = near.shape[0] * near.shape[2]
    return pl.pallas_call(
        functools.partial(hub_rows_kernel, width),
        out_shape=jax.ShapeDtypeStruct((share, clust), jnp.bfloat16),
        grid_spec=pltpu.PrefetchScalarGridSpec(
            num_scalar_prefetch=1,
            grid=(1,),
            in_specs=[
                pl.BlockSpec(mine.shape, lambda i, pick: (0, 0)),
                pl.BlockSpec(near.shape, lambda i, pick: (0, 0, 0, 0)),
                pl.BlockSpec(far.shape, lambda i, pick: (0, 0, 0)),
            ],
            out_specs=pl.BlockSpec((share, clust), lambda i, pick: (0, 0)),
            scratch_shapes=[pltpu.VMEM((K, share, LANES), jnp.int32), pltpu.VMEM((share, rows), jnp.bfloat16)],
        ),
        compiler_params=pltpu.CompilerParams(vmem_limit_bytes=VMEM_LIMIT),
        cost_estimate=pl.CostEstimate(flops=rows, bytes_accessed=rows, transcendentals=0),
        name="hub_rows",
    )(self_slot, mine, near, far)


def send(block, target):
    slabs, reps = lax.axis_size("slab"), lax.axis_size("rep")
    chips = slabs // 4
    pairs = []
    for device in range(slabs * reps):
        slab, rep = divmod(device, reps)
        to = target(slab // (2 * chips), slab // 2 % chips, slab % 2, rep)
        if to is not None:
            pairs.append((device, ((to[0] * chips + to[1]) * 2 + to[2]) * reps + to[3]))
    return lax.ppermute(block, AXES, pairs)


def along_line(block, table):
    return send(
        block, lambda half, chip, core, rep: (half, chip, core, table[rep]) if rep in table else None
    )


def swap_cores(block):
    return send(block, lambda half, chip, core, rep: (half, chip, 1 - core, rep))


def flags_of(code):
    flag = code.astype(jnp.float32).astype(jnp.int32) // HALF
    return flag & 3, (flag >> 2) & 1


def join_pieces(piece):
    slabs = lax.axis_size("slab")
    members, chips = slabs // 2, slabs // 4
    layers = [[h * members + c * 2 + core for c in range(chips)] for h in range(2) for core in range(2)]
    repeated = jnp.broadcast_to(piece[None], (chips,) + piece.shape)
    return lax.all_to_all(repeated, "slab", 0, 0, axis_index_groups=layers, tiled=True)


OUTWARD = {1: 0, 2: 3}
MIDDLE = {1: 2, 2: 1}


def spread_line(block):
    across = along_line(block, {0: 2, 2: 0, 1: 3, 3: 1})
    beside = along_line(block, {0: 1, 1: 0, 2: 3, 3: 2})
    return across, beside


def scatter(block):
    members = lax.axis_size("slab") // 2
    rows, width = block.shape
    planes = [[h * members + m for m in range(members)] for h in range(2)]
    return lax.all_to_all(
        block.reshape(members, rows // members, width), "slab", 0, 0, axis_index_groups=planes, tiled=True
    )


def hub_candidates(mine, hub_ids):
    members, reps = lax.axis_size("slab") // 2, lax.axis_size("rep")
    slab = lax.axis_index("slab")
    hub_slab, hub_rep = lax.div(hub_ids, reps), lax.rem(hub_ids, reps)
    member = lax.rem(hub_slab, members)
    held = jnp.stack(
        [lax.dynamic_index_in_dim(mine, member[h], 0, keepdims=False) for h in range(HUBS)], axis=0
    )
    got = send(held, lambda half, chip, core, rep: (1 - half, chip, core, rep))
    away = lax.div(hub_slab, members) != lax.div(slab, members)
    held = jnp.where(away[:, None, None], got, held)[None]
    rep = lax.axis_index("rep")
    for bit in range(2):
        got = along_line(held, {r: r ^ (1 << bit) for r in range(4)})
        upper = (rep >> bit) & 1 == 1
        held = jnp.concatenate([jnp.where(upper, got, held), jnp.where(upper, held, got)], axis=0)
    return held, hub_rep


def hub_share(held, hub_rep, code_at):
    slab = lax.axis_index("slab")
    pick = lambda pieces, at: jnp.where(
        at < 2, jnp.where(at == 0, pieces[0], pieces[1]), jnp.where(at == 2, pieces[2], pieces[3])
    )
    chosen = []
    for h in range(HUBS):
        hub = pick(held[:, h], hub_rep[h])
        want, _ = flags_of(hub[:1, code_at : code_at + 1])
        chosen.append(jnp.stack([hub, pick(held[:, h], want)], axis=0))
    held = jnp.stack(chosen, axis=0)
    first_core = lax.rem(slab, 2) == 0
    keep = jnp.where(first_core, held[0], held[1])
    got = swap_cores(jnp.where(first_core, held[1], held[0]))
    return jnp.concatenate([jnp.where(first_core, keep, got), jnp.where(first_core, got, keep)], axis=1)


def body(embeddings, indicators, neighbours, hub_ids, columns):
    rows, width = embeddings.shape
    clust = indicators.shape[1]
    full = width + clust
    reps = lax.axis_size("rep")
    total = lax.axis_size("slab") * reps
    rep = lax.axis_index("rep")
    steps = rows // ROW_TILE
    slots = neighbours[0].astype(jnp.int32)
    want = slots[1] & 3
    order = slots[2] - total
    core = lax.rem(lax.axis_index("slab"), 2)
    near_slot = jnp.where(order == core, 2, 3)
    barrier = lax.optimization_barrier

    joined, normed, rest = join(total, neighbours.reshape(-1), embeddings, indicators, columns)
    across, beside = spread_line(rest)

    pick = jnp.stack([near_slot]).astype(jnp.int32)
    own_rows = (joined, (ROW_TILE, width), lambda r, pick: (r, 0))
    own_x = (joined, (rows, width), lambda r, pick: (0, 0))
    own_y = (joined, (rows, clust), lambda r, pick: (0, width // clust))
    words = keep_words(pick, rest[None], lambda pick: 0, rows, 1)
    *carry, own_tile = tile_of(pick, own_rows, own_x, own_y, words, lambda pick: 0)
    mine, words, carry, own_tile, rest, across, beside = barrier(
        (scatter(joined), words, carry, own_tile, rest, across, beside)
    )

    held, hub_rep = hub_candidates(mine, hub_ids)
    held, normed, rest, across = barrier((held, normed, rest, across))

    outer, middle = along_line(across, OUTWARD), along_line(rest, MIDDLE)
    beside_x = along_line(normed, {0: 1, 1: 0, 2: 3, 3: 2})
    across_x = along_line(normed, {0: 2, 2: 0, 1: 3, 3: 1})
    both = hub_share(held, hub_rep, full)
    near = join_pieces(both[:, :, :full])
    at_end = (rep == 0) | (rep == 3)
    group_rest = jnp.stack([rest, beside, across, jnp.where(~at_end, middle, outer)], axis=0)
    at = want ^ rep
    flag = lax.dynamic_index_in_dim(group_rest[:, -1, 0], at, 0, keepdims=False).astype(jnp.int32)
    member_want, member_order = flag & 3, (flag >> 2) & 1
    second = member_want ^ rep
    place = lambda k: jnp.where((k == 3) & at_end, 4, k)
    pick = jnp.stack(
        [near_slot, place(at), place(second), jnp.where(member_order == core, 2, 3), at, second]
    ).astype(jnp.int32)
    member_words = keep_words(pick, group_rest, lambda pick: pick[4], rows, WORDS_HINT)
    near, group_rest, member_words, pick, normed, beside_x, across_x = barrier(
        (near, group_rest, member_words, pick, normed, beside_x, across_x)
    )

    far = swap_cores(near[:, 0])
    outer_x, middle_x = along_line(across_x, OUTWARD), along_line(normed, MIDDLE)
    _, hub_order = flags_of(both[0, 0, full])
    share = hub_rows(jnp.where(hub_order == core, 2, 3)[None], both[0], near, far, width)
    share, near, far = barrier((share, near, far))
    near_new = join_pieces(share).reshape(rows, clust)
    near_tile, far_tile, *carry = two_of(pick, normed, near, far, words, carry)
    near_new, carry = barrier((near_new, carry))
    far_new = swap_cores(near_new)
    near_new, far_new, outer_x, middle_x = barrier((near_new, far_new, outer_x, middle_x))

    return finish_of(
        pick, (normed, beside_x, across_x, middle_x, outer_x), normed, group_rest, near, far, words, member_words,
        carry, indicators, (own_tile, near_tile, far_tile), (near_new, far_new),
    )


def solution(mesh):
    return jax.shard_map(
        body,
        mesh=mesh,
        in_specs=(
            P(("slab", "rep"), None),
            P(("slab", "rep"), None),
            P(("slab", "rep"), None),
            P(),
            P(("slab", "rep"), None, None),
        ),
        out_specs=P(("slab", "rep"), None),
        check_vma=False,
    )
```
